32 devices in a mesh: dp: 8 (over z, y), seq: 4 (over x, core).
Axes of the slice: x: 2, y: 2, z: 4, core: 2. Of those that a mesh axis runs over, the one named last changes fastest.
Arguments:
- tokens: bfloat16 [8, 1024, 1024], P('dp', 'seq'), may hold values from -6 to 6
- segments: int32 [8, 1024], P('dp'), may hold values from 0 to 1023, as said below
- valid_mask: int32 [8, 1024], P('dp'), may hold values from 0 to 1, as said below
- attention_gain: float32 [1024], P('dp'), may hold values from 0.25 to 1.75
- query_weight: float32 [1024, 1024], P('dp'), may hold values from -0.1875 to 0.1875
- key_weight: float32 [1024, 512], P('dp'), may hold values from -0.1875 to 0.1875
- value_weight: float32 [1024, 512], P('dp'), may hold values from -0.1875 to 0.1875
- query_gain: float32 [64], replicated, may hold values from 0.25 to 1.75
- key_gain: float32 [64], replicated, may hold values from 0.25 to 1.75
- output_weight: float32 [1024, 1024], P('dp'), may hold values from -0.5 to 0.5
- feedforward_gain: float32 [1024], P('dp'), may hold values from 0.25 to 1.75
- gate_weight: float32 [1024, 4608], P('dp'), may hold values from -0.1875 to 0.1875
- up_weight: float32 [1024, 4608], P('dp'), may hold values from -0.1875 to 0.1875
- down_weight: float32 [4608, 1024], P('dp'), may hold values from -0.09375 to 0.09375
- cotangent: bfloat16 [8, 1024, 1024], P('dp', 'seq'), may hold values from -6 to 6
Outputs:
- layer_out: bfloat16 [8, 1024, 1024], P('dp', 'seq')
- token_grad: bfloat16 [8, 1024, 1024], P('dp', 'seq')
- attention_gain_grad: float32 [1024], P(('dp', 'seq'))
- query_weight_grad: float32 [1024, 1024], P(('dp', 'seq'))
- key_weight_grad: float32 [1024, 512], P(('dp', 'seq'))
- value_weight_grad: float32 [1024, 512], P(('dp', 'seq'))
- query_gain_grad: float32 [64], replicated
- key_gain_grad: float32 [64], replicated
- output_weight_grad: float32 [1024, 1024], P(('dp', 'seq'))
- feedforward_gain_grad: float32 [1024], P(('dp', 'seq'))
- gate_weight_grad: float32 [1024, 4608], P(('dp', 'seq'))
- up_weight_grad: float32 [1024, 4608], P(('dp', 'seq'))
- down_weight_grad: float32 [4608, 1024], P(('dp', 'seq'))
The draws below stay inside these ranges and needn't reach their ends.
Inputs may be any that keep to these rules, and one draw needn't show every extreme that they name: `segments`: document numbers start at 0 in each row and never fall; the row's last document is numbered 1024 - 1; every document but one has at most 128 tokens, and one document of exactly 512 tokens lies wholly among the row's valid tokens. `valid_mask`: each row is 1 on its first 1024 - k positions and 0 after them, for some k from 0 to 128.
All inputs are finite; a program needn't handle non-finite values.
Results may differ from the reference program's by a relative error of at most 0.017.
Values may be sent and summed in bfloat16 or wider, within the bound.
No kernel may reach another device: no remote copies, remote signals or barrier semaphores. Data moves between devices by JAX's collectives and lax.ppermute only.
A program may use at most 192 MiB of HBM per device.

```python
import math
import jax
import jax.numpy as jnp
from jax import lax

D = 1024
HQ = 16
HK = 8
HD = 64
FF = 4608
ROW = 1024
ROWS = 8
DOCMAX = 512


def layout_row(key):
    key_length, key_power, key_slot, key_pad = jax.random.split(key, 4)
    slot_count = 128
    power = jax.random.randint(key_power, (slot_count,), 0, 5)
    low_end = ROW // 256 + 1
    upper = jnp.right_shift(jnp.full((slot_count,), ROW // 8, dtype=jnp.int32), power) + 1
    upper = jnp.maximum(upper, low_end + 1)
    lengths = jax.random.randint(key_length, (slot_count,), low_end, upper)
    place = jax.random.randint(key_slot, (), 0, 4)
    lengths = jnp.where(jnp.arange(slot_count) == place, DOCMAX, lengths)
    ends = jnp.cumsum(lengths)
    spots = jnp.arange(ROW)
    numbers = jnp.sum((ends[None, :] <= spots[:, None]).astype(jnp.int32), axis=1)
    last_number = numbers[ROW - 1]
    numbers = jnp.where(numbers == last_number, ROW - 1, numbers)
    padding = jax.random.randint(key_pad, (), 0, ROW // 8 + 1)
    live = (spots < ROW - padding).astype(jnp.int32)
    return (numbers.astype(jnp.int32), live)


def layout(key):
    row_keys = jax.random.split(jax.random.fold_in(key, 7), ROWS)
    return jax.vmap(layout_row)(row_keys)


def draw_segments(key, part):
    return layout(key)[0]


def draw_valid_mask(key, part):
    return layout(key)[1]


def strengthened(entries, rng, source, target, shards_of, factor):
    owner, partner = [(jnp.arange(entries.shape[axis_at]) // (entries.shape[axis_at] // shards_of)).reshape([-1 if axis == axis_at else 1 for axis in range(entries.ndim)]) for axis_at in (source, target)]
    chosen = jax.random.permutation(rng, shards_of)[partner]
    strong = (owner == chosen) | (owner == (partner + shards_of // 2) % shards_of)
    return jnp.where(strong, factor * entries, entries)


def shard_levels(own_key, shape, pieces, smallest, top_value):
    def one(dim, shards_of):
        heights = jax.random.uniform(jax.random.fold_in(jax.random.fold_in(own_key, 6), dim), (shards_of,), jnp.float32, smallest / len(pieces), top_value / len(pieces))
        return jnp.repeat(jnp.exp(heights), shape[dim] // shards_of).reshape((-1,) + (1,) * (len(shape) - dim - 1))

    level = one(*pieces[0])
    for cut in pieces[1:]:
        level = level * one(*cut)
    return level


def bell_draw(rng, extent, spread, limit, pieces=(), kind=jnp.bfloat16):
    factor_of = shard_levels(rng, extent, pieces, -0.22, 0.18) if pieces else 1.0
    values = jax.random.normal(rng, extent, jnp.float32) * spread * factor_of
    return jnp.minimum(jnp.maximum(values, -limit), limit).astype(kind)


def gaussian_with(key, dims, spread, reach, cuts, heavy, kind=jnp.bfloat16):
    drawn = spread * jax.random.normal(key, dims, jnp.float32)
    if cuts:
        drawn = drawn * shard_levels(key, dims, cuts, -0.22, 0.18)
    return jnp.clip(strengthened(drawn, jax.random.fold_in(key, 3), *heavy), -reach, reach).astype(kind)


def setup_inputs(seed: int = 0) -> dict:
    splits = jax.random.split(jax.random.key(seed), 16)
    return {
        "tokens": gaussian_with(splits[0], (ROWS, ROW, D), 1.0, 6.0, ((0, 8), (1, 4)), (0, 2, 8, 2.0)),
        "segments": draw_segments(jax.random.fold_in(splits[15], 71), 0),
        "valid_mask": draw_valid_mask(jax.random.fold_in(splits[15], 71), 0),
        "attention_gain": jnp.clip(1.0 + 0.15 * jax.random.normal(splits[3], (D,), jnp.float32), 0.25, 1.75),
        "query_weight": bell_draw(splits[4], (D, HQ * HD), D ** -0.5, 0.1875, ((0, 8),), jnp.float32),
        "key_weight": bell_draw(splits[5], (D, HK * HD), D ** -0.5, 0.1875, ((0, 8),), jnp.float32),
        "value_weight": bell_draw(splits[6], (D, HK * HD), D ** -0.5, 0.1875, ((0, 8),), jnp.float32),
        "query_gain": jnp.clip(1.0 + 0.15 * jax.random.normal(splits[7], (HD,), jnp.float32), 0.25, 1.75),
        "key_gain": jnp.clip(1.0 + 0.15 * jax.random.normal(splits[8], (HD,), jnp.float32), 0.25, 1.75),
        "output_weight": bell_draw(splits[9], (HQ * HD, D), (HQ * HD // 8) ** -0.5, 0.5, ((0, 8),), jnp.float32),
        "feedforward_gain": jnp.clip(1.0 + 0.15 * jax.random.normal(splits[10], (D,), jnp.float32), 0.25, 1.75),
        "gate_weight": bell_draw(splits[11], (D, FF), D ** -0.5, 0.1875, ((0, 8),), jnp.float32),
        "up_weight": bell_draw(splits[12], (D, FF), D ** -0.5, 0.1875, ((0, 8),), jnp.float32),
        "down_weight": bell_draw(splits[13], (FF, D), FF ** -0.5, 0.09375, ((0, 8),), jnp.float32),
        "cotangent": bell_draw(splits[14], (ROWS, ROW, D), 1.0, 6.0, ((0, 8), (1, 4))),
    }


EPS = 1e-05
ROPE_BASE = 1000000.0
NEG_FILL = -1e+30
HIGHEST = lax.Precision.HIGHEST

@jax.custom_vjp
def low(v):
    return lax.optimization_barrier(v.astype(jnp.bfloat16)).astype(jnp.float32)

@jax.custom_vjp
def low_back(v):
    return v

def low_keep(v):
    return (low(v), None)

def low_pass(kept, grad):
    return (grad,)

def back_keep(v):
    return (v, None)

def back_low(kept, grad):
    return (low(grad),)
low.defvjp(low_keep, low_pass)
low_back.defvjp(back_keep, back_low)

def rms_unit(values):
    return values * lax.rsqrt(lax.optimization_barrier(jnp.mean(values * values, axis=-1, keepdims=True)) + EPS)

def doc_positions(segment_row):
    length = segment_row.shape[0]
    places = jnp.arange(length, dtype=jnp.int32)
    change = jnp.concatenate([jnp.ones((1,), dtype=jnp.bool_), segment_row[1:] != segment_row[:-1]])
    starts = lax.cummax(jnp.where(change, places, jnp.zeros_like(places)), axis=0)
    return places - starts

def rope_tables(positions, half_dim):
    frequency = ROPE_BASE ** (-jnp.arange(half_dim, dtype=jnp.float32) / half_dim)
    angles = positions.astype(jnp.float32)[:, None] * frequency[None, :]
    return (jnp.cos(angles), jnp.sin(angles))

def rotate(values, cos_table, sin_table):
    half_dim = values.shape[-1] // 2
    first_half = values[..., :half_dim]
    second_half = values[..., half_dim:]
    cos_wide = cos_table[:, None, :]
    sin_wide = sin_table[:, None, :]
    return jnp.concatenate([first_half * cos_wide - second_half * sin_wide, second_half * cos_wide + first_half * sin_wide], axis=-1)

def layer_row(inputs, segment_row, valid_row, params):
    attention_gain, query_weight, key_weight, value_weight, query_gain, key_gain, output_weight, feedforward_gain, gate_weight, up_weight, down_weight = params
    row_length = inputs.shape[0]
    head_dim = query_gain.shape[0]
    query_heads = query_weight.shape[1] // head_dim
    key_heads = key_weight.shape[1] // head_dim
    group_size = query_heads // key_heads
    block_rows = min(512, row_length)
    block_count = row_length // block_rows
    score_scale = 1.0 / math.sqrt(head_dim)
    normed = low(rms_unit(inputs) * low(attention_gain))
    query_raw = low_back(jnp.dot(normed, low(query_weight), precision=HIGHEST))
    key_raw = low_back(jnp.dot(normed, low(key_weight), precision=HIGHEST))
    value_raw = jnp.dot(normed, low(value_weight), precision=HIGHEST)
    positions = doc_positions(segment_row)
    cos_table, sin_table = rope_tables(positions, head_dim // 2)
    queries = rotate(rms_unit(query_raw.reshape(row_length, query_heads, head_dim)) * query_gain, cos_table, sin_table)
    queries = low_back(low(queries))
    keys_rot = rotate(rms_unit(key_raw.reshape(row_length, key_heads, head_dim)) * key_gain, cos_table, sin_table)
    keys_rot = low_back(low(keys_rot))
    values_all = low_back(low(value_raw)).reshape(row_length, key_heads, head_dim)
    keys_wide = jnp.repeat(keys_rot, group_size, axis=1)
    values_wide = jnp.repeat(values_all, group_size, axis=1)
    columns = jnp.arange(row_length, dtype=jnp.int32)

    def attend(block_index):
        first_row = (block_index * block_rows).astype(jnp.int32)
        rows_here = first_row + jnp.arange(block_rows, dtype=jnp.int32)
        query_block = lax.dynamic_slice_in_dim(queries, first_row, block_rows, 0)
        segment_here = lax.dynamic_slice_in_dim(segment_row, first_row, block_rows, 0)
        allowed = (columns[None, :] <= rows_here[:, None]) & (segment_here[:, None] == segment_row[None, :]) & (valid_row[None, :] > 0) | (columns[None, :] == rows_here[:, None])
        scores = low_back(jnp.einsum('qhd,khd->hqk', query_block, keys_wide, precision=HIGHEST) * score_scale)
        scores = jnp.where(allowed[None], scores, NEG_FILL)
        largest = lax.optimization_barrier(jnp.max(scores, axis=-1, keepdims=True))
        weights_exp = jnp.exp(scores - largest)
        shares = weights_exp / lax.optimization_barrier(jnp.sum(weights_exp, axis=-1, keepdims=True))
        return jnp.einsum('hqk,khd->qhd', low(shares), values_wide, precision=HIGHEST)
    mixed_heads = lax.map(jax.checkpoint(attend), jnp.arange(block_count, dtype=jnp.int32))
    mixed_heads = low_back(low(mixed_heads.reshape(row_length, query_heads * head_dim)))
    after_attention = inputs + low_back(jnp.dot(mixed_heads, low(output_weight), precision=HIGHEST))
    normed_two = low(rms_unit(after_attention) * low(feedforward_gain))
    gate_value = low_back(jnp.dot(normed_two, low(gate_weight), precision=HIGHEST))
    up_value = low_back(jnp.dot(normed_two, low(up_weight), precision=HIGHEST))
    hidden = low(jax.nn.silu(gate_value) * up_value)
    return after_attention + jnp.dot(hidden, low(down_weight), precision=HIGHEST)

def reference(tokens, segments, valid_mask, attention_gain, query_weight, key_weight, value_weight, query_gain, key_gain, output_weight, feedforward_gain, gate_weight, up_weight, down_weight, cotangent):
    params = (attention_gain, query_weight, key_weight, value_weight, query_gain, key_gain, output_weight, feedforward_gain, gate_weight, up_weight, down_weight)

    def one_row(totals, row_items):
        token_row, segment_row, valid_row, cotangent_row = row_items
        result, pullback = jax.vjp(lambda inputs, weights: layer_row(inputs, segment_row, valid_row, weights), token_row.astype(jnp.float32), params)
        input_grad, weight_grads = pullback(cotangent_row.astype(jnp.float32))
        totals = jax.tree.map(lambda held_sum, new_term: held_sum + new_term, totals, weight_grads)
        return (totals, (result.astype(jnp.bfloat16), input_grad.astype(jnp.bfloat16)))
    zero_grads = jax.tree.map(jnp.zeros_like, params)
    grad_sums, outputs = lax.scan(one_row, zero_grads, (tokens, segments, valid_mask, cotangent))
    return (outputs[0], outputs[1], grad_sums[0], grad_sums[1], grad_sums[2], grad_sums[3], grad_sums[4], grad_sums[5], grad_sums[6], grad_sums[7], grad_sums[8], grad_sums[9], grad_sums[10])
```

```python
import math

import jax
import jax.numpy as jnp
from jax import lax
from jax.sharding import PartitionSpec as P

EPS = 1e-05
ROPE_BASE = 1000000.0
NEG_FILL = -1e30
BF = jnp.bfloat16
F32 = jnp.float32


def dot(left, right, dims):
    return lax.dot_general(left, right, (dims, ((), ())), preferred_element_type=F32)


def mm(left, right):
    return dot(left, right, ((1,), (0,)))


def mm_nt(left, right):
    return dot(left, right, ((1,), (1,)))


def mm_tn(left, right):
    return dot(left, right, ((0,), (0,)))


def rms_stats(values):
    factor = lax.rsqrt(jnp.mean(values * values, axis=-1, keepdims=True) + EPS)
    return (values * factor, factor)


def rms_back(grad_unit, unit_values, factor):
    return factor * (
        grad_unit - unit_values * jnp.mean(grad_unit * unit_values, axis=-1, keepdims=True)
    )


def doc_positions(segment_row):
    length = segment_row.shape[0]
    places = jnp.arange(length, dtype=jnp.int32)
    change = jnp.concatenate([jnp.ones((1,), dtype=jnp.bool_), segment_row[1:] != segment_row[:-1]])
    starts = lax.cummax(jnp.where(change, places, jnp.zeros_like(places)), axis=0)
    return places - starts


def rope_tables(positions, half_dim):
    frequency = ROPE_BASE ** (-jnp.arange(half_dim, dtype=F32) / half_dim)
    angles = positions.astype(F32)[:, None] * frequency[None, :]
    return (jnp.cos(angles), jnp.sin(angles))


def rotate(values, cos_table, sin_table):
    half_dim = values.shape[-1] // 2
    first_half = values[..., :half_dim]
    second_half = values[..., half_dim:]
    cos_wide = cos_table[:, None, :]
    sin_wide = sin_table[:, None, :]
    return jnp.concatenate(
        [
            first_half * cos_wide - second_half * sin_wide,
            second_half * cos_wide + first_half * sin_wide,
        ],
        axis=-1,
    )


def block_mask(segment_row, valid_row, first_row, block_rows):
    length = segment_row.shape[0]
    columns = jnp.arange(length, dtype=jnp.int32)
    rows_here = first_row + jnp.arange(block_rows, dtype=jnp.int32)
    segment_here = lax.dynamic_slice_in_dim(segment_row, first_row, block_rows, 0)
    return (columns[None, :] <= rows_here[:, None]) & (
        segment_here[:, None] == segment_row[None, :]
    ) & (valid_row[None, :] > 0) | (columns[None, :] == rows_here[:, None])


def block_scores(query_block, keys_all, allowed, score_scale):
    scores = (
        jnp.einsum("qgrd,kgd->grqk", query_block, keys_all, preferred_element_type=F32)
        * score_scale
    )
    return jnp.where(allowed[None, None], scores, NEG_FILL)


def attention_forward(queries, keys_all, values_all, segment_row, valid_row, score_scale):
    block_count = queries.shape[0]
    block_rows = queries.shape[1]

    def one_block(block_items):
        query_block, block_index = block_items
        allowed = block_mask(segment_row, valid_row, block_index * block_rows, block_rows)
        scores = block_scores(query_block, keys_all, allowed, score_scale)
        largest = jnp.max(scores, axis=-1, keepdims=True)
        weights_exp = jnp.exp(scores - largest)
        totals = jnp.sum(weights_exp, axis=-1, keepdims=True)
        shares = (weights_exp / totals).astype(BF)
        mixed_block = jnp.einsum("grqk,kgd->qgrd", shares, values_all, preferred_element_type=F32)
        return (mixed_block.astype(BF), (largest + jnp.log(totals))[..., 0])

    return lax.map(one_block, (queries, jnp.arange(block_count, dtype=jnp.int32)))


def attention_backward(
    queries, keys_all, values_all, grad_out, log_totals, segment_row, valid_row, score_scale
):
    block_count = queries.shape[0]
    block_rows = queries.shape[1]

    def one_block(running, block_items):
        key_sum, value_sum = running
        query_block, grad_block, log_block, block_index = block_items
        allowed = block_mask(segment_row, valid_row, block_index * block_rows, block_rows)
        scores = block_scores(query_block, keys_all, allowed, score_scale)
        shares = jnp.exp(scores - log_block[..., None])
        grad_shares = jnp.einsum(
            "qgrd,kgd->grqk", grad_block, values_all, preferred_element_type=F32
        )
        centre = jnp.sum(shares * grad_shares, axis=-1, keepdims=True)
        grad_scores = (shares * (grad_shares - centre)).astype(BF)
        grad_query = (
            jnp.einsum("grqk,kgd->qgrd", grad_scores, keys_all, preferred_element_type=F32)
            * score_scale
        )
        key_sum = (
            key_sum
            + jnp.einsum("grqk,qgrd->kgd", grad_scores, query_block, preferred_element_type=F32)
            * score_scale
        )
        value_sum = value_sum + jnp.einsum(
            "grqk,qgrd->kgd", shares.astype(BF), grad_block, preferred_element_type=F32
        )
        return ((key_sum, value_sum), grad_query.astype(BF))

    zero_keys = jnp.zeros(keys_all.shape, F32)
    zero_values = jnp.zeros(values_all.shape, F32)
    sums_out, query_grad = lax.scan(
        one_block,
        (zero_keys, zero_values),
        (queries, grad_out, log_totals, jnp.arange(block_count, dtype=jnp.int32)),
    )
    return (sums_out[0], sums_out[1], query_grad)


def swap(values, bit):
    count = lax.axis_size("seq")
    return lax.ppermute(values, "seq", [(i, i ^ bit) for i in range(count)])


def seq_gather(values):
    count = lax.axis_size("seq")
    if count != 4:
        return lax.all_gather(values, "seq", axis=0)
    place = lax.axis_index("seq")
    far = swap(values, 2)
    near = swap(values, 1)
    far_near = swap(far, 1)
    odd = (place & 1) == 1
    high = place >= 2
    mine = (jnp.where(odd, near, values), jnp.where(odd, values, near))
    theirs = (jnp.where(odd, far_near, far), jnp.where(odd, far, far_near))
    return jnp.stack(
        [
            jnp.where(high, theirs[0], mine[0]),
            jnp.where(high, theirs[1], mine[1]),
            jnp.where(high, mine[0], theirs[0]),
            jnp.where(high, mine[1], theirs[1]),
        ]
    )


def seq_scatter(values):
    count = lax.axis_size("seq")
    if count != 4:
        return lax.psum_scatter(
            values.astype(BF), "seq", scatter_dimension=0, tiled=True
        ).astype(F32)
    place = lax.axis_index("seq")
    rows = values.shape[0] // 4
    split = values.reshape(2, 2, rows, -1)
    odd = (place & 1) == 1
    high = place >= 2
    keep = jnp.where(odd, split[:, 1], split[:, 0])
    send = jnp.where(odd, split[:, 0], split[:, 1]).astype(BF)
    pair = keep + swap(send, 1).astype(F32)
    keep = jnp.where(high, pair[1], pair[0])
    send = jnp.where(high, pair[0], pair[1]).astype(BF)
    return keep + swap(send, 2).astype(F32)


def dp_gather(values):
    return lax.all_gather(values, "dp", axis=0, tiled=True)


def dp_scatter(values):
    return lax.psum_scatter(values.astype(BF), "dp", scatter_dimension=0, tiled=True)


def sum_all(values):
    for axis in ("seq", "dp"):
        count = lax.axis_size(axis)
        bit = 1
        while bit < count:
            values = values + lax.ppermute(values, axis, [(i, i ^ bit) for i in range(count)])
            bit *= 2
    return values


def local(
    tokens,
    segments,
    valid_mask,
    attention_gain,
    query_weight,
    key_weight,
    value_weight,
    query_gain,
    key_gain,
    output_weight,
    feedforward_gain,
    gate_weight,
    up_weight,
    down_weight,
    cotangent,
):
    seq_count = lax.axis_size("seq")
    dp_count = lax.axis_size("dp")
    place = lax.axis_index("seq")
    local_rows = tokens.shape[1]
    row_length = segments.shape[1]
    head_dim = query_gain.shape[0]
    width = tokens.shape[2]
    hidden_width = gate_weight.shape[1]
    query_width = query_weight.shape[1]
    key_width = key_weight.shape[1]
    query_here = query_width // seq_count
    key_here = key_width // seq_count
    hidden_here = hidden_width // seq_count
    heads_here = query_here // head_dim
    groups_here = key_here // head_dim
    group_size = heads_here // groups_here
    weight_rows = query_weight.shape[0]
    own_rows = weight_rows // seq_count
    block_rows = min(512, row_length)
    block_count = row_length // block_rows
    score_scale = 1.0 / math.sqrt(head_dim)
    segment_row = segments[0]
    valid_row = valid_mask[0]

    def columns_of(weight, size):
        return lax.dynamic_slice_in_dim(weight, place * size, size, 1)

    def low(weight):
        return weight.astype(BF).astype(F32)

    gain_one = low(attention_gain)[:, None]
    gain_two = low(feedforward_gain)[:, None]
    attention_pack = jnp.concatenate(
        [
            (low(columns_of(query_weight, query_here)) * gain_one).astype(BF),
            (low(columns_of(key_weight, key_here)) * gain_one).astype(BF),
            (low(columns_of(value_weight, key_here)) * gain_one).astype(BF),
            columns_of(output_weight, width // seq_count).astype(BF),
        ],
        axis=1,
    )
    piece = hidden_width // (dp_count * seq_count)

    def hidden_columns(weight):
        split = weight.reshape(weight_rows, dp_count, seq_count, piece)
        mine = lax.dynamic_index_in_dim(split, place, 2, keepdims=False)
        return (low(mine.reshape(weight_rows, hidden_here)) * gain_two).astype(BF)

    gate_up_pack = jnp.concatenate([hidden_columns(gate_weight), hidden_columns(up_weight)], axis=1)
    down_pack = lax.dynamic_slice_in_dim(down_weight, place * piece, piece, 0).astype(BF)

    attention_all = dp_gather(attention_pack)
    gate_up_all = dp_gather(gate_up_pack)
    down_all = dp_gather(down_pack)

    inputs = seq_gather(tokens[0]).reshape(row_length, width).astype(F32)
    qkv_width = query_here + 2 * key_here
    qkv_weight = attention_all[:, :qkv_width]
    output_all = jnp.concatenate(list(seq_gather(attention_all[:, qkv_width:])), axis=1)
    grad_rows = seq_gather(cotangent[0]).reshape(row_length, width)

    positions = doc_positions(segment_row)
    cos_table, sin_table = rope_tables(positions, head_dim // 2)
    unit_one = rms_stats(inputs)[0].astype(BF)
    qkv_raw = mm(unit_one, qkv_weight)
    query_raw = qkv_raw[:, :query_here].reshape(row_length, heads_here, head_dim)
    key_raw = qkv_raw[:, query_here : query_here + key_here].reshape(
        row_length, groups_here, head_dim
    )
    values_all = (
        qkv_raw[:, query_here + key_here :].astype(BF).reshape(row_length, groups_here, head_dim)
    )
    query_unit, query_factor = rms_stats(query_raw)
    key_unit, key_factor = rms_stats(key_raw)
    queries = rotate(query_unit * query_gain, cos_table, sin_table).astype(BF)
    keys_all = rotate(key_unit * key_gain, cos_table, sin_table).astype(BF)
    query_blocks = queries.reshape(block_count, block_rows, groups_here, group_size, head_dim)
    mixed_blocks, log_totals = attention_forward(
        query_blocks, keys_all, values_all, segment_row, valid_row, score_scale
    )
    mixed_here = mixed_blocks.reshape(row_length, query_here)
    mixed_all = jnp.concatenate(list(seq_gather(mixed_here)), axis=1)
    after_attention = inputs + mm(mixed_all, output_all)
    unit_two = rms_stats(after_attention)[0].astype(BF)

    gate_up = mm(unit_two, gate_up_all)
    gate_value = gate_up[:, :hidden_here]
    up_value = gate_up[:, hidden_here:]
    sigmoid_gate = jax.nn.sigmoid(gate_value)
    silu_gate = gate_value * sigmoid_gate
    hidden = (silu_gate * up_value).astype(BF)
    grad_hidden = mm_nt(grad_rows, down_all)
    grad_gate = (
        grad_hidden * up_value * sigmoid_gate * (1.0 + gate_value * (1.0 - sigmoid_gate))
    ).astype(BF)
    grad_up = (grad_hidden * silu_gate).astype(BF)
    grad_gate_up = jnp.concatenate([grad_gate, grad_up], axis=1)
    grad_normed = seq_scatter(mm_nt(grad_gate_up, gate_up_all))

    down_sums = dp_scatter(mm_tn(hidden, grad_rows))
    gate_up_sums = dp_scatter(mm_tn(unit_two, grad_gate_up))

    after_here = lax.dynamic_slice_in_dim(after_attention, place * local_rows, local_rows, 0)
    layer_out = (after_here + seq_scatter(mm(hidden, down_all))).astype(BF)

    unit_here, factor_here = rms_stats(after_here)
    grad_after = cotangent[0].astype(F32) + rms_back(grad_normed, unit_here, factor_here)
    grad_branch = seq_gather(grad_after.astype(BF)).reshape(row_length, width)
    output_here = lax.dynamic_slice_in_dim(output_all, place * query_here, query_here, 0)
    grad_mixed = mm_nt(grad_branch, output_here).astype(BF)
    output_sums = dp_scatter(mm_tn(mixed_here, grad_branch))

    grad_blocks = grad_mixed.reshape(block_count, block_rows, groups_here, group_size, head_dim)
    key_sum, value_sum, query_grad = attention_backward(
        query_blocks,
        keys_all,
        values_all,
        grad_blocks,
        log_totals,
        segment_row,
        valid_row,
        score_scale,
    )
    query_turned = rotate(
        query_grad.reshape(row_length, heads_here, head_dim).astype(F32), cos_table, -sin_table
    )
    key_turned = rotate(key_sum.astype(BF).astype(F32), cos_table, -sin_table)
    gain_terms = jnp.stack(
        [
            jnp.sum(query_turned * query_unit, axis=(0, 1)),
            jnp.sum(key_turned * key_unit, axis=(0, 1)),
        ]
    )
    qkv_grad = jnp.concatenate(
        [
            rms_back(query_turned * query_gain, query_unit, query_factor)
            .astype(BF)
            .reshape(row_length, query_here),
            rms_back(key_turned * key_gain, key_unit, key_factor)
            .astype(BF)
            .reshape(row_length, key_here),
            value_sum.astype(BF).reshape(row_length, key_here),
        ],
        axis=1,
    )
    qkv_sums = dp_scatter(mm_tn(unit_one, qkv_grad))
    grad_one = seq_scatter(mm_nt(qkv_grad, qkv_weight))
    unit_tokens, factor_tokens = rms_stats(tokens[0].astype(F32))
    token_grad = (grad_after + rms_back(grad_one, unit_tokens, factor_tokens)).astype(BF)
    gain_sums = sum_all(gain_terms)

    def to_owners(sums):
        return lax.all_to_all(
            sums.reshape(seq_count, own_rows, -1), "seq", split_axis=0, concat_axis=0, tiled=True
        ).astype(F32)

    def own(weight):
        return lax.dynamic_slice_in_dim(weight, place * own_rows, own_rows, 0)

    def joined(pieces):
        return jnp.swapaxes(pieces, 0, 1).reshape(own_rows, -1)

    qkv_own = to_owners(qkv_sums)
    query_own = joined(qkv_own[:, :, :query_here])
    key_own = joined(qkv_own[:, :, query_here : query_here + key_here])
    value_own = joined(qkv_own[:, :, query_here + key_here :])
    gain_one_own = own(gain_one)
    attention_gain_grad = (
        jnp.sum(own(low(query_weight)) * query_own, axis=1)
        + jnp.sum(own(low(key_weight)) * key_own, axis=1)
        + jnp.sum(own(low(value_weight)) * value_own, axis=1)
    )

    hidden_own = to_owners(gate_up_sums).reshape(seq_count, own_rows, 2, dp_count, piece)
    hidden_own = jnp.transpose(hidden_own, (2, 1, 3, 0, 4)).reshape(2, own_rows, hidden_width)
    gain_two_own = own(gain_two)
    feed_gain_grad = jnp.sum(own(low(gate_weight)) * hidden_own[0], axis=1) + jnp.sum(
        own(low(up_weight)) * hidden_own[1], axis=1
    )

    moves = [
        (dp * seq_count + seq, seq * dp_count + dp)
        for dp in range(dp_count)
        for seq in range(seq_count)
    ]
    output_own = lax.ppermute(output_sums, ("dp", "seq"), moves).astype(F32)

    return (
        layer_out.reshape(1, local_rows, -1),
        token_grad.reshape(1, local_rows, -1),
        attention_gain_grad,
        query_own * gain_one_own,
        key_own * gain_one_own,
        value_own * gain_one_own,
        gain_sums[0],
        gain_sums[1],
        output_own,
        feed_gain_grad,
        hidden_own[0] * gain_two_own,
        hidden_own[1] * gain_two_own,
        down_sums.astype(F32),
    )


def solution(mesh):
    in_specs = (
        P("dp", "seq", None),
        P("dp", None),
        P("dp", None),
        P("dp"),
        P("dp", None),
        P("dp", None),
        P("dp", None),
        P(),
        P(),
        P("dp", None),
        P("dp"),
        P("dp", None),
        P("dp", None),
        P("dp", None),
        P("dp", "seq", None),
    )
    out_specs = (
        P("dp", "seq", None),
        P("dp", "seq", None),
        P(("dp", "seq")),
        P(("dp", "seq"), None),
        P(("dp", "seq"), None),
        P(("dp", "seq"), None),
        P(),
        P(),
        P(("dp", "seq"), None),
        P(("dp", "seq")),
        P(("dp", "seq"), None),
        P(("dp", "seq"), None),
        P(("dp", "seq"), None),
    )
    return jax.shard_map(local, mesh=mesh, in_specs=in_specs, out_specs=out_specs, check_vma=False)
```

```python
import math

import jax
import jax.numpy as jnp
from jax import lax
from jax.sharding import PartitionSpec as P

EPS = 1e-05
ROPE_BASE = 1000000.0
NEG_FILL = -1e30
BF = jnp.bfloat16
F32 = jnp.float32


def dot(left, right, dims):
    return lax.dot_general(left, right, (dims, ((), ())), preferred_element_type=F32)


def mm(left, right):
    return dot(left, right, ((1,), (0,)))


def mm_nt(left, right):
    return dot(left, right, ((1,), (1,)))


def mm_tn(left, right):
    return dot(left, right, ((0,), (0,)))


def rms_stats(values):
    factor = lax.rsqrt(jnp.mean(values * values, axis=-1, keepdims=True) + EPS)
    return (values * factor, factor)


def rms_back(grad_unit, unit_values, factor):
    return factor * (
        grad_unit - unit_values * jnp.mean(grad_unit * unit_values, axis=-1, keepdims=True)
    )


def doc_positions(segment_row):
    length = segment_row.shape[0]
    places = jnp.arange(length, dtype=jnp.int32)
    change = jnp.concatenate([jnp.ones((1,), dtype=jnp.bool_), segment_row[1:] != segment_row[:-1]])
    starts = lax.cummax(jnp.where(change, places, jnp.zeros_like(places)), axis=0)
    return places - starts


def rope_tables(positions, half_dim):
    frequency = ROPE_BASE ** (-jnp.arange(half_dim, dtype=F32) / half_dim)
    angles = positions.astype(F32)[:, None] * frequency[None, :]
    return (jnp.cos(angles), jnp.sin(angles))


def rotate(values, cos_table, sin_table):
    half_dim = values.shape[-1] // 2
    first_half = values[..., :half_dim]
    second_half = values[..., half_dim:]
    cos_wide = cos_table[:, None, :]
    sin_wide = sin_table[:, None, :]
    return jnp.concatenate(
        [
            first_half * cos_wide - second_half * sin_wide,
            second_half * cos_wide + first_half * sin_wide,
        ],
        axis=-1,
    )


def block_mask(segment_row, valid_row, first_row, block_rows):
    length = segment_row.shape[0]
    columns = jnp.arange(length, dtype=jnp.int32)
    rows_here = first_row + jnp.arange(block_rows, dtype=jnp.int32)
    segment_here = lax.dynamic_slice_in_dim(segment_row, first_row, block_rows, 0)
    return (columns[None, :] <= rows_here[:, None]) & (
        segment_here[:, None] == segment_row[None, :]
    ) & (valid_row[None, :] > 0) | (columns[None, :] == rows_here[:, None])


def block_scores(query_block, keys_all, allowed, score_scale):
    scores = (
        jnp.einsum("qgrd,kgd->grqk", query_block, keys_all, preferred_element_type=F32)
        * score_scale
    )
    return jnp.where(allowed[None, None], scores, NEG_FILL)


def attention_forward(queries, keys_all, values_all, segment_row, valid_row, score_scale):
    block_count = queries.shape[0]
    block_rows = queries.shape[1]

    def one_block(block_items):
        query_block, block_index = block_items
        allowed = block_mask(segment_row, valid_row, block_index * block_rows, block_rows)
        scores = block_scores(query_block, keys_all, allowed, score_scale)
        largest = jnp.max(scores, axis=-1, keepdims=True)
        weights_exp = jnp.exp(scores - largest)
        totals = jnp.sum(weights_exp, axis=-1, keepdims=True)
        shares = (weights_exp / totals).astype(BF)
        mixed_block = jnp.einsum("grqk,kgd->qgrd", shares, values_all, preferred_element_type=F32)
        return (mixed_block.astype(BF), (largest + jnp.log(totals))[..., 0])

    return lax.map(one_block, (queries, jnp.arange(block_count, dtype=jnp.int32)))


def attention_backward(
    queries, keys_all, values_all, grad_out, log_totals, segment_row, valid_row, score_scale
):
    block_count = queries.shape[0]
    block_rows = queries.shape[1]

    def one_block(running, block_items):
        key_sum, value_sum = running
        query_block, grad_block, log_block, block_index = block_items
        allowed = block_mask(segment_row, valid_row, block_index * block_rows, block_rows)
        scores = block_scores(query_block, keys_all, allowed, score_scale)
        shares = jnp.exp(scores - log_block[..., None])
        grad_shares = jnp.einsum(
            "qgrd,kgd->grqk", grad_block, values_all, preferred_element_type=F32
        )
        centre = jnp.sum(shares * grad_shares, axis=-1, keepdims=True)
        grad_scores = (shares * (grad_shares - centre)).astype(BF)
        grad_query = (
            jnp.einsum("grqk,kgd->qgrd", grad_scores, keys_all, preferred_element_type=F32)
            * score_scale
        )
        key_sum = (
            key_sum
            + jnp.einsum("grqk,qgrd->kgd", grad_scores, query_block, preferred_element_type=F32)
            * score_scale
        )
        value_sum = value_sum + jnp.einsum(
            "grqk,qgrd->kgd", shares.astype(BF), grad_block, preferred_element_type=F32
        )
        return ((key_sum, value_sum), grad_query.astype(BF))

    zero_keys = jnp.zeros(keys_all.shape, F32)
    zero_values = jnp.zeros(values_all.shape, F32)
    sums_out, query_grad = lax.scan(
        one_block,
        (zero_keys, zero_values),
        (queries, grad_out, log_totals, jnp.arange(block_count, dtype=jnp.int32)),
    )
    return (sums_out[0], sums_out[1], query_grad)


def swap(values, bit):
    count = lax.axis_size("seq")
    return lax.ppermute(values, "seq", [(i, i ^ bit) for i in range(count)])


def seq_gather(values):
    count = lax.axis_size("seq")
    if count != 4:
        return lax.all_gather(values, "seq", axis=0)
    place = lax.axis_index("seq")
    far = swap(values, 2)
    near = swap(values, 1)
    far_near = swap(far, 1)
    odd = (place & 1) == 1
    high = place >= 2
    mine = (jnp.where(odd, near, values), jnp.where(odd, values, near))
    theirs = (jnp.where(odd, far_near, far), jnp.where(odd, far, far_near))
    return jnp.stack(
        [
            jnp.where(high, theirs[0], mine[0]),
            jnp.where(high, theirs[1], mine[1]),
            jnp.where(high, mine[0], theirs[0]),
            jnp.where(high, mine[1], theirs[1]),
        ]
    )


def seq_scatter(values):
    count = lax.axis_size("seq")
    if count != 4:
        return lax.psum_scatter(
            values.astype(BF), "seq", scatter_dimension=0, tiled=True
        ).astype(F32)
    place = lax.axis_index("seq")
    rows = values.shape[0] // 4
    split = values.reshape(2, 2, rows, -1)
    odd = (place & 1) == 1
    high = place >= 2
    keep = jnp.where(odd, split[:, 1], split[:, 0])
    send = jnp.where(odd, split[:, 0], split[:, 1]).astype(BF)
    pair = keep + swap(send, 1).astype(F32)
    keep = jnp.where(high, pair[1], pair[0])
    send = jnp.where(high, pair[0], pair[1]).astype(BF)
    return keep + swap(send, 2).astype(F32)


def after(values, *others):
    return lax.optimization_barrier((values, others))[0]


def ring_length():
    count = lax.axis_size("dp")
    return count if count % 2 == 0 and 4 <= count <= 8 else 0


def ring_order(count):
    return list(range(0, count, 2)) + list(range(count - 1, 0, -2))


def ring_source(offset):
    count = lax.axis_size("dp")
    place = lax.axis_index("dp")
    spot = jnp.where(place % 2 == 0, place // 2, count - 1 - place // 2)
    spot = (spot + offset + count) % count
    return jnp.where(spot < count // 2, 2 * spot, 2 * (count - 1 - spot) + 1)


def ring_move(values, step):
    count = lax.axis_size("dp")
    order = ring_order(count)
    return lax.ppermute(
        values, "dp", [(order[i], order[(i + step) % count]) for i in range(count)]
    )


def dp_gather(shard):
    count = ring_length()
    if not count:
        return (lax.all_gather(shard, "dp", axis=0, tiled=True), shard)
    rows = shard.shape[0]
    half = rows // 2
    whole = jnp.zeros((count * rows, shard.shape[1]), shard.dtype)
    whole = lax.dynamic_update_slice_in_dim(whole, shard, ring_source(0) * rows, 0)
    up = down = shard
    for step in range(1, count // 2):
        up = ring_move(up, 1)
        down = ring_move(down, -1)
        whole = lax.dynamic_update_slice_in_dim(whole, up, ring_source(-step) * rows, 0)
        whole = lax.dynamic_update_slice_in_dim(whole, down, ring_source(step) * rows, 0)
    sign = (up, down)
    first = ring_move(up[:half], 1)
    second = ring_move(down[half:], -1)
    start = ring_source(count // 2) * rows
    whole = lax.dynamic_update_slice_in_dim(whole, first, start, 0)
    whole = lax.dynamic_update_slice_in_dim(whole, second, start + half, 0)
    return (whole, sign)


def dp_scatter(terms):
    count = ring_length()
    if not count:
        sums = lax.psum_scatter(terms.astype(BF), "dp", scatter_dimension=0, tiled=True)
        return (sums.astype(F32), sums)
    rows = terms.shape[0] // count
    half = rows // 2

    def term(offset):
        return lax.dynamic_slice_in_dim(terms, ring_source(offset) * rows, rows, 0)

    far = term(count // 2)
    up = ring_move(far[:half].astype(BF), 1).astype(F32)
    down = ring_move(far[half:].astype(BF), -1).astype(F32)
    blank = jnp.zeros((rows - half, terms.shape[1]), F32)
    up = jnp.concatenate([up, blank])
    down = jnp.concatenate([jnp.zeros((half, terms.shape[1]), F32), down])
    sign = (up, down)
    for step in range(count // 2 - 1, 0, -1):
        sign = (up, down)
        up = ring_move((term(step) + up).astype(BF), 1).astype(F32)
        down = ring_move((term(-step) + down).astype(BF), -1).astype(F32)
    return (term(0) + up + down, sign)


def sum_all(values):
    for axis in ("seq", "dp"):
        count = lax.axis_size(axis)
        bit = 1
        while bit < count:
            values = values + lax.ppermute(values, axis, [(i, i ^ bit) for i in range(count)])
            bit *= 2
    return values


def local(
    tokens,
    segments,
    valid_mask,
    attention_gain,
    query_weight,
    key_weight,
    value_weight,
    query_gain,
    key_gain,
    output_weight,
    feedforward_gain,
    gate_weight,
    up_weight,
    down_weight,
    cotangent,
):
    seq_count = lax.axis_size("seq")
    dp_count = lax.axis_size("dp")
    place = lax.axis_index("seq")
    local_rows = tokens.shape[1]
    row_length = segments.shape[1]
    head_dim = query_gain.shape[0]
    width = tokens.shape[2]
    hidden_width = gate_weight.shape[1]
    query_width = query_weight.shape[1]
    key_width = key_weight.shape[1]
    query_here = query_width // seq_count
    key_here = key_width // seq_count
    hidden_here = hidden_width // seq_count
    heads_here = query_here // head_dim
    groups_here = key_here // head_dim
    group_size = heads_here // groups_here
    weight_rows = query_weight.shape[0]
    own_rows = weight_rows // seq_count
    block_rows = min(512, row_length)
    block_count = row_length // block_rows
    score_scale = 1.0 / math.sqrt(head_dim)
    segment_row = segments[0]
    valid_row = valid_mask[0]

    def columns_of(weight, size):
        return lax.dynamic_slice_in_dim(weight, place * size, size, 1)

    def low(weight):
        return weight.astype(BF).astype(F32)

    gain_one = low(attention_gain)[:, None]
    gain_two = low(feedforward_gain)[:, None]
    attention_pack = jnp.concatenate(
        [
            (low(columns_of(query_weight, query_here)) * gain_one).astype(BF),
            (low(columns_of(key_weight, key_here)) * gain_one).astype(BF),
            (low(columns_of(value_weight, key_here)) * gain_one).astype(BF),
            columns_of(output_weight, width // seq_count).astype(BF),
        ],
        axis=1,
    )
    piece = hidden_width // (dp_count * seq_count)

    def hidden_columns(weight):
        split = weight.reshape(weight_rows, dp_count, seq_count, piece)
        mine = lax.dynamic_index_in_dim(split, place, 2, keepdims=False)
        return (low(mine.reshape(weight_rows, hidden_here)) * gain_two).astype(BF)

    gate_up_pack = jnp.concatenate([hidden_columns(gate_weight), hidden_columns(up_weight)], axis=1)
    down_pack = lax.dynamic_slice_in_dim(down_weight, place * piece, piece, 0).astype(BF)

    attention_all, sign = dp_gather(attention_pack)
    gate_up_all, sign = dp_gather(after(gate_up_pack, sign))
    down_all, sign = dp_gather(after(down_pack, sign))

    inputs = seq_gather(tokens[0]).reshape(row_length, width).astype(F32)
    qkv_width = query_here + 2 * key_here
    qkv_weight = attention_all[:, :qkv_width]
    output_all = jnp.concatenate(list(seq_gather(attention_all[:, qkv_width:])), axis=1)
    grad_rows = seq_gather(cotangent[0]).reshape(row_length, width)

    positions = doc_positions(segment_row)
    cos_table, sin_table = rope_tables(positions, head_dim // 2)
    unit_one = rms_stats(inputs)[0].astype(BF)
    qkv_raw = mm(unit_one, qkv_weight)
    query_raw = qkv_raw[:, :query_here].reshape(row_length, heads_here, head_dim)
    key_raw = qkv_raw[:, query_here : query_here + key_here].reshape(
        row_length, groups_here, head_dim
    )
    values_all = (
        qkv_raw[:, query_here + key_here :].astype(BF).reshape(row_length, groups_here, head_dim)
    )
    query_unit, query_factor = rms_stats(query_raw)
    key_unit, key_factor = rms_stats(key_raw)
    queries = rotate(query_unit * query_gain, cos_table, sin_table).astype(BF)
    keys_all = rotate(key_unit * key_gain, cos_table, sin_table).astype(BF)
    query_blocks = queries.reshape(block_count, block_rows, groups_here, group_size, head_dim)
    mixed_blocks, log_totals = attention_forward(
        query_blocks, keys_all, values_all, segment_row, valid_row, score_scale
    )
    mixed_here = mixed_blocks.reshape(row_length, query_here)
    mixed_all = jnp.concatenate(list(seq_gather(mixed_here)), axis=1)
    after_attention = inputs + mm(mixed_all, output_all)
    unit_two = rms_stats(after_attention)[0].astype(BF)

    gate_up = mm(unit_two, gate_up_all)
    gate_value = gate_up[:, :hidden_here]
    up_value = gate_up[:, hidden_here:]
    sigmoid_gate = jax.nn.sigmoid(gate_value)
    silu_gate = gate_value * sigmoid_gate
    hidden = (silu_gate * up_value).astype(BF)
    grad_hidden = mm_nt(grad_rows, down_all)
    grad_gate = (
        grad_hidden * up_value * sigmoid_gate * (1.0 + gate_value * (1.0 - sigmoid_gate))
    ).astype(BF)
    grad_up = (grad_hidden * silu_gate).astype(BF)
    grad_gate_up = jnp.concatenate([grad_gate, grad_up], axis=1)
    grad_normed = mm_nt(grad_gate_up, gate_up_all)

    down_terms = mm_tn(hidden, grad_rows)
    gate_up_terms = mm_tn(unit_two, grad_gate_up)
    grad_normed, down_terms, gate_up_terms = lax.optimization_barrier(
        (grad_normed, down_terms, gate_up_terms)
    )
    down_sums, sign = dp_scatter(down_terms)
    gate_up_sums, sign = dp_scatter(after(gate_up_terms, sign))

    grad_normed = seq_scatter(grad_normed)
    after_here = lax.dynamic_slice_in_dim(after_attention, place * local_rows, local_rows, 0)

    unit_here, factor_here = rms_stats(after_here)
    grad_after = cotangent[0].astype(F32) + rms_back(grad_normed, unit_here, factor_here)
    grad_branch = seq_gather(grad_after.astype(BF)).reshape(row_length, width)
    output_here = lax.dynamic_slice_in_dim(output_all, place * query_here, query_here, 0)
    grad_mixed = mm_nt(grad_branch, output_here).astype(BF)
    output_terms = mm_tn(mixed_here, grad_branch)

    grad_blocks = grad_mixed.reshape(block_count, block_rows, groups_here, group_size, head_dim)
    key_sum, value_sum, query_grad = attention_backward(
        query_blocks,
        keys_all,
        values_all,
        grad_blocks,
        log_totals,
        segment_row,
        valid_row,
        score_scale,
    )
    query_turned = rotate(
        query_grad.reshape(row_length, heads_here, head_dim).astype(F32), cos_table, -sin_table
    )
    key_turned = rotate(key_sum.astype(BF).astype(F32), cos_table, -sin_table)
    gain_terms = jnp.stack(
        [
            jnp.sum(query_turned * query_unit, axis=(0, 1)),
            jnp.sum(key_turned * key_unit, axis=(0, 1)),
        ]
    )
    qkv_grad = jnp.concatenate(
        [
            rms_back(query_turned * query_gain, query_unit, query_factor)
            .astype(BF)
            .reshape(row_length, query_here),
            rms_back(key_turned * key_gain, key_unit, key_factor)
            .astype(BF)
            .reshape(row_length, key_here),
            value_sum.astype(BF).reshape(row_length, key_here),
        ],
        axis=1,
    )
    qkv_terms = mm_tn(unit_one, qkv_grad)
    grad_one = mm_nt(qkv_grad, qkv_weight)
    qkv_terms, grad_one, output_terms = lax.optimization_barrier(
        (qkv_terms, grad_one, after(output_terms, sign))
    )
    output_sums, sign = dp_scatter(output_terms)
    qkv_sums, sign = dp_scatter(after(qkv_terms, sign))
    layer_out = (after_here + seq_scatter(mm(after(hidden, qkv_grad), down_all))).astype(BF)
    grad_one = seq_scatter(grad_one)
    unit_tokens, factor_tokens = rms_stats(tokens[0].astype(F32))
    token_grad = (grad_after + rms_back(grad_one, unit_tokens, factor_tokens)).astype(BF)
    gain_sums = sum_all(gain_terms)

    def to_owners(sums):
        return lax.all_to_all(
            sums.astype(BF).reshape(seq_count, own_rows, -1), "seq", split_axis=0, concat_axis=0, tiled=True
        ).astype(F32)

    def own(weight):
        return lax.dynamic_slice_in_dim(weight, place * own_rows, own_rows, 0)

    def joined(pieces):
        return jnp.swapaxes(pieces, 0, 1).reshape(own_rows, -1)

    qkv_own = to_owners(qkv_sums)
    query_own = joined(qkv_own[:, :, :query_here])
    key_own = joined(qkv_own[:, :, query_here : query_here + key_here])
    value_own = joined(qkv_own[:, :, query_here + key_here :])
    gain_one_own = own(gain_one)
    attention_gain_grad = (
        jnp.sum(own(low(query_weight)) * query_own, axis=1)
        + jnp.sum(own(low(key_weight)) * key_own, axis=1)
        + jnp.sum(own(low(value_weight)) * value_own, axis=1)
    )

    hidden_own = to_owners(gate_up_sums).reshape(seq_count, own_rows, 2, dp_count, piece)
    hidden_own = jnp.transpose(hidden_own, (2, 1, 3, 0, 4)).reshape(2, own_rows, hidden_width)
    gain_two_own = own(gain_two)
    feed_gain_grad = jnp.sum(own(low(gate_weight)) * hidden_own[0], axis=1) + jnp.sum(
        own(low(up_weight)) * hidden_own[1], axis=1
    )

    moves = [
        (dp * seq_count + seq, seq * dp_count + dp)
        for dp in range(dp_count)
        for seq in range(seq_count)
    ]
    output_own = lax.ppermute(output_sums.astype(BF), ("dp", "seq"), moves).astype(F32)

    return (
        layer_out.reshape(1, local_rows, -1),
        token_grad.reshape(1, local_rows, -1),
        attention_gain_grad,
        query_own * gain_one_own,
        key_own * gain_one_own,
        value_own * gain_one_own,
        gain_sums[0],
        gain_sums[1],
        output_own,
        feed_gain_grad,
        hidden_own[0] * gain_two_own,
        hidden_own[1] * gain_two_own,
        down_sums,
    )


def solution(mesh):
    in_specs = (
        P("dp", "seq", None),
        P("dp", None),
        P("dp", None),
        P("dp"),
        P("dp", None),
        P("dp", None),
        P("dp", None),
        P(),
        P(),
        P("dp", None),
        P("dp"),
        P("dp", None),
        P("dp", None),
        P("dp", None),
        P("dp", "seq", None),
    )
    out_specs = (
        P("dp", "seq", None),
        P("dp", "seq", None),
        P(("dp", "seq")),
        P(("dp", "seq"), None),
        P(("dp", "seq"), None),
        P(("dp", "seq"), None),
        P(),
        P(),
        P(("dp", "seq"), None),
        P(("dp", "seq")),
        P(("dp", "seq"), None),
        P(("dp", "seq"), None),
        P(("dp", "seq"), None),
    )
    return jax.shard_map(local, mesh=mesh, in_specs=in_specs, out_specs=out_specs, check_vma=False)
```

```python
import functools
import math

import jax
import jax.numpy as jnp
from jax import lax
from jax.experimental import pallas as pl
from jax.experimental.pallas import tpu as pltpu
from jax.sharding import PartitionSpec as P

EPS = 1e-05
ROPE_BASE = 1000000.0
NEG_FILL = -1e30
BF = jnp.bfloat16
F32 = jnp.float32
BLOCK = 128
PAIR = 128
VMEM_LIMIT = 48 * 1024 * 1024


def dot(left, right, dims):
    return lax.dot_general(left, right, (dims, ((), ())), preferred_element_type=F32)


def mm(left, right):
    return dot(left, right, ((1,), (0,)))


def mm_nt(left, right):
    return dot(left, right, ((1,), (1,)))


def mm_tn(left, right):
    return dot(left, right, ((0,), (0,)))


def rms_stats(values):
    factor = lax.rsqrt(jnp.mean(values * values, axis=-1, keepdims=True) + EPS)
    return (values * factor, factor)


def rms_back(grad_unit, unit_values, factor):
    return factor * (
        grad_unit - unit_values * jnp.mean(grad_unit * unit_values, axis=-1, keepdims=True)
    )


def doc_positions(segment_row):
    length = segment_row.shape[0]
    places = jnp.arange(length, dtype=jnp.int32)
    change = jnp.concatenate([jnp.ones((1,), dtype=jnp.bool_), segment_row[1:] != segment_row[:-1]])
    starts = lax.cummax(jnp.where(change, places, jnp.zeros_like(places)), axis=0)
    return places - starts


def rope_tables(positions, half_dim):
    frequency = ROPE_BASE ** (-jnp.arange(half_dim, dtype=F32) / half_dim)
    angles = positions.astype(F32)[:, None] * frequency[None, :]
    return (jnp.cos(angles), jnp.sin(angles))


def whole_vmem(count):
    return [pl.BlockSpec(memory_space=pltpu.VMEM)] * count


def scalars(count):
    return [pl.BlockSpec(memory_space=pltpu.SMEM)] * count


def lanes(shape):
    return lax.broadcasted_iota(jnp.int32, shape, 1)


def head_means(values, head_dim):
    width = values.shape[1]
    row = lax.broadcasted_iota(jnp.int32, (width, width), 0) // head_dim
    column = lax.broadcasted_iota(jnp.int32, (width, width), 1) // head_dim
    spread = jnp.where(row == column, 1.0 / head_dim, 0.0).astype(BF)
    high = values.astype(BF)
    rest = (values - high.astype(F32)).astype(BF)
    return mm(high, spread) + mm(rest, spread)


def half_partner(values, head_dim):
    half = head_dim // 2
    width = values.shape[1]
    upper = (lanes(values.shape) % head_dim) >= half
    return jnp.where(
        upper, pltpu.roll(values, half, 1), pltpu.roll(values, width - half, 1)
    )


def stacked_heads(pair, head_dim):
    first = lanes(pair.shape) < head_dim
    zero = jnp.zeros_like(pair)
    return jnp.concatenate([jnp.where(first, pair, zero), jnp.where(first, zero, pair)], axis=0)


def side_by_side(stacked, head_dim):
    rows = stacked.shape[0] // 2
    return jnp.where(
        lanes((rows, stacked.shape[1])) < head_dim, stacked[:rows], stacked[rows:]
    )


def mask_bias(start_ref, usable_ref, first_row, first_key, rows, window):
    row = first_row + lax.broadcasted_iota(jnp.int32, (rows, window), 0)
    key = first_key + lax.broadcasted_iota(jnp.int32, (rows, window), 1)
    start = start_ref[pl.ds(first_row, rows), :]
    usable = usable_ref[:, pl.ds(first_key, window)] > 0
    allowed = ((key >= start) & (key <= row) & usable) | (key == row)
    bias = jnp.where(allowed, 0.0, NEG_FILL)
    return jnp.concatenate([bias, bias], axis=0)


def each_block(low_ref, row_length, body):
    long_window = min(5 * BLOCK, row_length)

    def step(index, carry):
        first_row = pl.multiple_of(index * BLOCK, BLOCK)
        short_key = jnp.maximum(first_row - BLOCK, 0)
        is_short = low_ref[index] >= short_key

        @pl.when(is_short)
        def _():
            body(first_row, pl.multiple_of(short_key, BLOCK), 2 * BLOCK)

        @pl.when(jnp.logical_not(is_short))
        def _():
            long_key = jnp.maximum(first_row + BLOCK - long_window, 0)
            body(first_row, pl.multiple_of(long_key, BLOCK), long_window)

        return carry

    lax.fori_loop(0, row_length // BLOCK, step, 0)


def front_kernel(
    head_dim,
    place_ref,
    low_ref,
    x0_ref,
    x1_ref,
    x2_ref,
    x3_ref,
    weight_ref,
    cos_ref,
    sin_ref,
    gain_ref,
    start_ref,
    usable_ref,
    unit_ref,
    raw_ref,
    query_ref,
    key_ref,
    value_ref,
    mixed_ref,
):
    place = place_ref[0]
    pieces = (x0_ref, x1_ref, x2_ref, x3_ref)
    rows_each = x0_ref.shape[0]
    row_length = unit_ref.shape[0]
    query_groups = query_ref.shape[1] // PAIR
    chunk = 64
    for index, piece in enumerate(pieces):
        base = (place ^ index) * rows_each

        def normalize(step, carry, piece=piece, base=base):
            values = piece[pl.ds(pl.multiple_of(step * chunk, chunk), chunk), :].astype(F32)
            factor = lax.rsqrt(jnp.mean(values * values, axis=-1, keepdims=True) + EPS)
            unit_ref[pl.ds(pl.multiple_of(base + step * chunk, chunk), chunk), :] = (
                values * factor
            ).astype(BF)
            return carry

        lax.fori_loop(0, rows_each // chunk, normalize, 0)

    def project(step, carry):
        rows = pl.ds(pl.multiple_of(step * BLOCK, BLOCK), BLOCK)
        raw = mm(unit_ref[rows, :], weight_ref[...])
        raw_ref[rows, :] = raw[:, : raw_ref.shape[1]]
        cos = cos_ref[rows, :]
        sin = sin_ref[rows, :]
        for group in range(query_groups + 1):
            is_key = group == query_groups
            values = raw[:, group * PAIR : (group + 1) * PAIR]
            factor = lax.rsqrt(head_means(values * values, head_dim) + EPS)
            scaled = values * factor * gain_ref[int(is_key) : int(is_key) + 1, :]
            turned = scaled * cos + half_partner(scaled, head_dim) * sin
            if is_key:
                crossed = pltpu.roll(turned, head_dim, 1)
                first = lanes(turned.shape) < head_dim
                key_ref[rows, :PAIR] = jnp.where(first, turned, crossed).astype(BF)
                key_ref[rows, PAIR:] = jnp.where(first, crossed, turned).astype(BF)
                values = raw[:, (group + 1) * PAIR :]
                crossed = pltpu.roll(values, head_dim, 1)
                value_ref[rows, :PAIR] = jnp.where(first, values, crossed).astype(BF)
                value_ref[rows, PAIR:] = jnp.where(first, crossed, values).astype(BF)
            else:
                query_ref[rows, group * PAIR : (group + 1) * PAIR] = (
                    turned * (1.0 / math.sqrt(head_dim))
                ).astype(BF)
        return carry

    lax.fori_loop(0, row_length // BLOCK, project, 0)

    def attend(first_row, first_key, window):
        bias = mask_bias(start_ref, usable_ref, first_row, first_key, BLOCK, window)
        rows = pl.ds(first_row, BLOCK)
        keys = pl.ds(first_key, window)
        for group in range(query_groups):
            pair = slice(group * PAIR, (group + 1) * PAIR)
            stacked = stacked_heads(query_ref[rows, pair], head_dim)
            grown = jnp.exp(mm_nt(stacked, key_ref[keys, pair]) + bias)
            share = grown * (1.0 / jnp.sum(grown, axis=-1, keepdims=True))
            mixed = mm(share.astype(BF), value_ref[keys, pair])
            mixed_ref[rows, pair] = side_by_side(mixed, head_dim).astype(BF)

    each_block(low_ref, row_length, attend)


def middle_kernel(
    place_ref,
    x0_ref,
    x1_ref,
    x2_ref,
    x3_ref,
    o0_ref,
    o1_ref,
    o2_ref,
    o3_ref,
    w0_ref,
    w1_ref,
    w2_ref,
    w3_ref,
    unit_ref,
    here_ref,
    sum_ref,
):
    place = place_ref[0]
    rows_each, width = x0_ref.shape
    heads = o0_ref.shape[1]
    columns = w0_ref.shape[1]
    chunk = 64
    for index, piece in enumerate((x0_ref, x1_ref, x2_ref, x3_ref)):
        base = pl.multiple_of((place ^ index) * rows_each, rows_each)
        rows = pl.ds(base, rows_each)
        for part, weight in enumerate((w0_ref, w1_ref, w2_ref, w3_ref)):
            total = None
            for other, mixed in enumerate((o0_ref, o1_ref, o2_ref, o3_ref)):
                features = pl.ds(pl.multiple_of((place ^ other) * heads, heads), heads)
                term = mm(mixed[rows, :], weight[features, :])
                total = term if total is None else total + term
            spot = pl.multiple_of((place ^ part) * columns, columns)
            sum_ref[:, pl.ds(spot, columns)] = total

        def normalize(step, carry, piece=piece, base=base, index=index):
            part = pl.ds(pl.multiple_of(step * chunk, chunk), chunk)
            values = sum_ref[part, :] + piece[part, :].astype(F32)
            if index == 0:
                here_ref[part, :] = values
            factor = lax.rsqrt(jnp.mean(values * values, axis=-1, keepdims=True) + EPS)
            unit_ref[pl.ds(pl.multiple_of(base + step * chunk, chunk), chunk), :] = (
                values * factor
            ).astype(BF)
            return carry

        lax.fori_loop(0, rows_each // chunk, normalize, 0)


def back_kernel(
    head_dim,
    low_ref,
    grad_ref,
    query_ref,
    key_ref,
    value_ref,
    raw_ref,
    cos_ref,
    sin_ref,
    gain_ref,
    start_ref,
    usable_ref,
    out_ref,
    terms_ref,
    key_sum_ref,
    value_sum_ref,
):
    row_length = grad_ref.shape[0]
    query_groups = query_ref.shape[1] // PAIR
    scale = 1.0 / math.sqrt(head_dim)
    key_sum_ref[...] = jnp.zeros_like(key_sum_ref)
    value_sum_ref[...] = jnp.zeros_like(value_sum_ref)
    terms_ref[...] = jnp.zeros_like(terms_ref)

    def through_norm(rows, group, grad, kind):
        grad = grad.astype(BF).astype(F32)
        turned = grad * cos_ref[rows, :] - half_partner(grad, head_dim) * sin_ref[rows, :]
        values = raw_ref[rows, group * PAIR : (group + 1) * PAIR]
        factor = lax.rsqrt(head_means(values * values, head_dim) + EPS)
        unit = values * factor
        terms_ref[kind : kind + 1, :] += jnp.sum(turned * unit, axis=0, keepdims=True)
        scaled = turned * gain_ref[kind : kind + 1, :]
        back = factor * (scaled - unit * head_means(scaled * unit, head_dim))
        out_ref[rows, group * PAIR : (group + 1) * PAIR] = back.astype(BF)

    def attend(first_row, first_key, window):
        bias = mask_bias(start_ref, usable_ref, first_row, first_key, BLOCK, window)
        rows = pl.ds(first_row, BLOCK)
        keys = pl.ds(first_key, window)
        for group in range(query_groups):
            pair = slice(group * PAIR, (group + 1) * PAIR)
            stacked = stacked_heads(query_ref[rows, pair], head_dim)
            grads = stacked_heads(grad_ref[rows, pair], head_dim)
            grown = jnp.exp(mm_nt(stacked, key_ref[keys, pair]) + bias)
            share = grown * (1.0 / jnp.sum(grown, axis=-1, keepdims=True))
            grad_share = mm_nt(grads, value_ref[keys, pair])
            centre = jnp.sum(share * grad_share, axis=-1, keepdims=True)
            grad_score = (share * (grad_share - centre)).astype(BF)
            grad_query = side_by_side(mm(grad_score, key_ref[keys, pair]), head_dim) * scale
            key_sum_ref[keys, pair] += mm_tn(grad_score, stacked)
            value_sum_ref[keys, pair] += mm_tn(share.astype(BF), grads)
            through_norm(rows, group, grad_query, 0)

    each_block(low_ref, row_length, attend)

    def folded(sum_ref, rows):
        first = sum_ref[rows, :PAIR]
        second = sum_ref[rows, PAIR:]
        return jnp.where(
            lanes(first.shape) < head_dim,
            first + pltpu.roll(first, head_dim, 1),
            second + pltpu.roll(second, head_dim, 1),
        )

    def finish(step, carry):
        rows = pl.ds(pl.multiple_of(step * BLOCK, BLOCK), BLOCK)
        through_norm(rows, query_groups, folded(key_sum_ref, rows), 1)
        out_ref[rows, (query_groups + 1) * PAIR :] = folded(value_sum_ref, rows).astype(BF)
        return carry

    lax.fori_loop(0, row_length // BLOCK, finish, 0)


def call(kernel, results, scalar_count, operands, scratch=(), flops=0, moved=0):
    return pl.pallas_call(
        kernel,
        out_shape=[jax.ShapeDtypeStruct(shape, kind) for shape, kind in results],
        in_specs=scalars(scalar_count) + whole_vmem(len(operands) - scalar_count),
        out_specs=whole_vmem(len(results)),
        scratch_shapes=list(scratch),
        compiler_params=pltpu.CompilerParams(vmem_limit_bytes=VMEM_LIMIT),
        cost_estimate=pl.CostEstimate(flops=flops, bytes_accessed=moved, transcendentals=0),
    )(*operands)


def swap(values, bit):
    count = lax.axis_size("seq")
    return lax.ppermute(values, "seq", [(i, i ^ bit) for i in range(count)])


def seq_pieces(values):
    far = swap(values, 2)
    near = swap(values, 1)
    return (values, near, far, swap(far, 1))


def in_order(pieces):
    place = lax.axis_index("seq")
    odd = (place & 1) == 1
    high = place >= 2
    mine = (jnp.where(odd, pieces[1], pieces[0]), jnp.where(odd, pieces[0], pieces[1]))
    theirs = (jnp.where(odd, pieces[3], pieces[2]), jnp.where(odd, pieces[2], pieces[3]))
    return jnp.stack(
        [
            jnp.where(high, theirs[0], mine[0]),
            jnp.where(high, theirs[1], mine[1]),
            jnp.where(high, mine[0], theirs[0]),
            jnp.where(high, mine[1], theirs[1]),
        ]
    )


def seq_scatter(values):
    place = lax.axis_index("seq")
    rows = values.shape[0] // 4
    split = values.reshape(2, 2, rows, -1)
    odd = (place & 1) == 1
    high = place >= 2
    keep = jnp.where(odd, split[:, 1], split[:, 0])
    send = jnp.where(odd, split[:, 0], split[:, 1]).astype(BF)
    pair = keep + swap(send, 1).astype(F32)
    keep = jnp.where(high, pair[1], pair[0])
    send = jnp.where(high, pair[0], pair[1]).astype(BF)
    return keep + swap(send, 2).astype(F32)


def after(values, *others):
    return lax.optimization_barrier((values, others))[0]


def ring_length():
    count = lax.axis_size("dp")
    return count if count % 2 == 0 and 4 <= count <= 8 else 0


def ring_order(count):
    return list(range(0, count, 2)) + list(range(count - 1, 0, -2))


def ring_source(offset):
    count = lax.axis_size("dp")
    place = lax.axis_index("dp")
    spot = jnp.where(place % 2 == 0, place // 2, count - 1 - place // 2)
    spot = (spot + offset + count) % count
    return jnp.where(spot < count // 2, 2 * spot, 2 * (count - 1 - spot) + 1)


def ring_move(values, step):
    count = lax.axis_size("dp")
    order = ring_order(count)
    return lax.ppermute(
        values, "dp", [(order[i], order[(i + step) % count]) for i in range(count)]
    )


def dp_gather(shard):
    count = ring_length()
    if not count:
        return (lax.all_gather(shard, "dp", axis=0, tiled=True), shard)
    rows = shard.shape[0]
    half = rows // 32 * 16 or rows // 2
    whole = jnp.zeros((count * rows, shard.shape[1]), shard.dtype)
    whole = lax.dynamic_update_slice_in_dim(whole, shard, ring_source(0) * rows, 0)
    up = down = shard
    for step in range(1, count // 2):
        up = ring_move(up, 1)
        down = ring_move(down, -1)
        whole = lax.dynamic_update_slice_in_dim(whole, up, ring_source(-step) * rows, 0)
        whole = lax.dynamic_update_slice_in_dim(whole, down, ring_source(step) * rows, 0)
    sign = (up, down)
    first = ring_move(up[:half], 1)
    second = ring_move(down[half:], -1)
    start = ring_source(count // 2) * rows
    whole = lax.dynamic_update_slice_in_dim(whole, first, start, 0)
    whole = lax.dynamic_update_slice_in_dim(whole, second, start + half, 0)
    return (whole, sign)


def dp_scatter(terms):
    count = ring_length()
    if not count:
        sums = lax.psum_scatter(terms.astype(BF), "dp", scatter_dimension=0, tiled=True)
        return (sums.astype(F32), sums)
    rows = terms.shape[0] // count
    half = rows // 32 * 16 or rows // 2

    def term(offset):
        return lax.dynamic_slice_in_dim(terms, ring_source(offset) * rows, rows, 0)

    far = term(count // 2)
    up = ring_move(far[:half].astype(BF), 1).astype(F32)
    down = ring_move(far[half:].astype(BF), -1).astype(F32)
    blank = jnp.zeros((rows - half, terms.shape[1]), F32)
    up = jnp.concatenate([up, blank])
    down = jnp.concatenate([jnp.zeros((half, terms.shape[1]), F32), down])
    sign = (up, down)
    for step in range(count // 2 - 1, 0, -1):
        sign = (up, down)
        up = ring_move((term(step) + up).astype(BF), 1).astype(F32)
        down = ring_move((term(-step) + down).astype(BF), -1).astype(F32)
    return (term(0) + up + down, sign)


def sum_all(values):
    for axis in ("seq", "dp"):
        count = lax.axis_size(axis)
        bit = 1
        while bit < count:
            values = values + lax.ppermute(values, axis, [(i, i ^ bit) for i in range(count)])
            bit *= 2
    return values


def local(
    tokens,
    segments,
    valid_mask,
    attention_gain,
    query_weight,
    key_weight,
    value_weight,
    query_gain,
    key_gain,
    output_weight,
    feedforward_gain,
    gate_weight,
    up_weight,
    down_weight,
    cotangent,
):
    seq_count = lax.axis_size("seq")
    dp_count = lax.axis_size("dp")
    place = lax.axis_index("seq")
    local_rows = tokens.shape[1]
    row_length = segments.shape[1]
    head_dim = query_gain.shape[0]
    width = tokens.shape[2]
    hidden_width = gate_weight.shape[1]
    query_width = query_weight.shape[1]
    key_width = key_weight.shape[1]
    query_here = query_width // seq_count
    key_here = key_width // seq_count
    hidden_here = hidden_width // seq_count
    weight_rows = query_weight.shape[0]
    own_rows = weight_rows // seq_count
    segment_row = segments[0]
    valid_row = valid_mask[0]

    def columns_of(weight, size):
        return lax.dynamic_slice_in_dim(weight, place * size, size, 1)

    def low(weight):
        return weight.astype(BF).astype(F32)

    gain_one = low(attention_gain)[:, None]
    gain_two = low(feedforward_gain)[:, None]
    attention_pack = jnp.concatenate(
        [
            (low(columns_of(query_weight, query_here)) * gain_one).astype(BF),
            (low(columns_of(key_weight, key_here)) * gain_one).astype(BF),
            (low(columns_of(value_weight, key_here)) * gain_one).astype(BF),
            columns_of(output_weight, width // seq_count).astype(BF),
        ],
        axis=1,
    )
    piece = hidden_width // (dp_count * seq_count)

    def hidden_columns(weight):
        split = weight.reshape(weight_rows, dp_count, seq_count, piece)
        mine = lax.dynamic_index_in_dim(split, place, 2, keepdims=False)
        return (low(mine.reshape(weight_rows, hidden_here)) * gain_two).astype(BF)

    gate_up_pack = jnp.concatenate([hidden_columns(gate_weight), hidden_columns(up_weight)], axis=1)
    down_pack = lax.dynamic_slice_in_dim(down_weight, place * piece, piece, 0).astype(BF)

    token_pieces = seq_pieces(tokens[0])
    grad_row_pieces = seq_pieces(after(cotangent[0], token_pieces[2]))

    attention_all, sign = dp_gather(attention_pack)
    gate_up_all, sign = dp_gather(after(gate_up_pack, sign))
    down_all, sign = dp_gather(after(down_pack, sign))

    qkv_width = query_here + 2 * key_here
    qkv_weight = attention_all[:, :qkv_width]
    output_pieces = seq_pieces(attention_all[:, qkv_width:])
    grad_rows = in_order(grad_row_pieces).reshape(row_length, width)

    positions = doc_positions(segment_row)
    starts = jnp.arange(row_length, dtype=jnp.int32) - positions
    block_lows = starts[::BLOCK]
    cos_table, sin_table = rope_tables(positions, head_dim // 2)
    repeats = PAIR // head_dim
    cos_wide = jnp.tile(cos_table, (1, 2 * repeats))
    sin_wide = jnp.tile(jnp.concatenate([-sin_table, sin_table], axis=1), (1, repeats))
    head_gains = jnp.tile(jnp.stack([query_gain, key_gain]), (1, repeats))
    place_array = place.astype(jnp.int32).reshape(1)
    row_starts = starts[:, None]
    usable = valid_row[None, :]
    unit_one, raw, queries, keys_two, values_two, mixed_here = call(
        functools.partial(front_kernel, head_dim),
        [
            ((row_length, width), BF),
            ((row_length, query_here + key_here), F32),
            ((row_length, query_here), BF),
            ((row_length, 2 * key_here), BF),
            ((row_length, 2 * key_here), BF),
            ((row_length, query_here), BF),
        ],
        2,
        (place_array, block_lows, *token_pieces, qkv_weight, cos_wide, sin_wide)
        + (head_gains, row_starts, usable),
        flops=4 * row_length * width * qkv_width,
        moved=12 * row_length * width,
    )
    mixed_pieces = seq_pieces(mixed_here)
    unit_two, after_here = call(
        middle_kernel,
        [((row_length, width), BF), ((local_rows, width), F32)],
        1,
        (place_array, *token_pieces, *mixed_pieces, *output_pieces),
        scratch=[pltpu.VMEM((local_rows, width), F32)],
        flops=2 * row_length * width * width,
        moved=10 * row_length * width,
    )

    gate_up = mm(unit_two, gate_up_all)
    gate_value = gate_up[:, :hidden_here]
    up_value = gate_up[:, hidden_here:]
    sigmoid_gate = jax.nn.sigmoid(gate_value)
    silu_gate = gate_value * sigmoid_gate
    hidden = (silu_gate * up_value).astype(BF)
    grad_hidden = mm_nt(grad_rows, down_all)
    grad_gate = (
        grad_hidden * up_value * sigmoid_gate * (1.0 + gate_value * (1.0 - sigmoid_gate))
    ).astype(BF)
    grad_up = (grad_hidden * silu_gate).astype(BF)
    grad_gate_up = jnp.concatenate([grad_gate, grad_up], axis=1)
    grad_normed = mm_nt(grad_gate_up, gate_up_all)

    down_terms = mm_tn(hidden, grad_rows)
    gate_up_terms = mm_tn(unit_two, grad_gate_up)
    grad_normed, down_terms, gate_up_terms = lax.optimization_barrier(
        (grad_normed, down_terms, gate_up_terms)
    )
    down_sums, sign = dp_scatter(down_terms)
    gate_up_sums, sign = dp_scatter(after(gate_up_terms, sign))

    grad_normed = seq_scatter(grad_normed)

    unit_here, factor_here = rms_stats(after_here)
    grad_after = cotangent[0].astype(F32) + rms_back(grad_normed, unit_here, factor_here)
    grad_branch = in_order(seq_pieces(grad_after.astype(BF))).reshape(row_length, width)
    output_here = jnp.concatenate(
        list(
            in_order(
                [
                    lax.dynamic_slice_in_dim(piece, place * query_here, query_here, 0)
                    for piece in output_pieces
                ]
            )
        ),
        axis=1,
    )
    grad_mixed = mm_nt(grad_branch, output_here).astype(BF)
    output_terms = mm_tn(mixed_here, grad_branch)
    qkv_grad, gain_terms = call(
        functools.partial(back_kernel, head_dim),
        [((row_length, qkv_width), BF), ((8, PAIR), F32)],
        1,
        (block_lows, grad_mixed, queries, keys_two, values_two, raw, cos_wide, sin_wide)
        + (head_gains, row_starts, usable),
        scratch=[pltpu.VMEM((row_length, 2 * key_here), F32)] * 2,
        flops=8 * row_length * width * qkv_width,
        moved=12 * row_length * width,
    )
    qkv_terms = mm_tn(unit_one, qkv_grad)
    grad_one = mm_nt(qkv_grad, qkv_weight)
    side = width // qkv_width
    chunk_rows = query_width // (dp_count * seq_count)
    attention_terms = [qkv_terms.reshape(dp_count, weight_rows, qkv_width)]
    for part in range(side):
        attention_terms.append(
            output_terms[:, part * qkv_width : (part + 1) * qkv_width].reshape(
                dp_count, chunk_rows, qkv_width
            )
        )
    attention_terms = jnp.concatenate(attention_terms, axis=1).reshape(-1, qkv_width)
    attention_terms, grad_one = lax.optimization_barrier((after(attention_terms, sign), grad_one))
    attention_sums, sign = dp_scatter(attention_terms)
    qkv_sums = attention_sums[:weight_rows]
    output_sums = jnp.concatenate(
        [
            attention_sums[weight_rows + part * chunk_rows : weight_rows + (part + 1) * chunk_rows]
            for part in range(side)
        ],
        axis=1,
    )
    layer_out = (after_here + seq_scatter(mm(after(hidden, qkv_grad), down_all))).astype(BF)
    grad_one = seq_scatter(grad_one)
    unit_tokens, factor_tokens = rms_stats(tokens[0].astype(F32))
    token_grad = (grad_after + rms_back(grad_one, unit_tokens, factor_tokens)).astype(BF)
    gain_sums = jnp.sum(sum_all(gain_terms)[:2].reshape(2, repeats, head_dim), axis=1)

    def to_owners(sums):
        return lax.all_to_all(
            sums.astype(BF).reshape(seq_count, own_rows, -1), "seq", split_axis=0, concat_axis=0, tiled=True
        ).astype(F32)

    def own(weight):
        return lax.dynamic_slice_in_dim(weight, place * own_rows, own_rows, 0)

    def joined(pieces):
        return jnp.swapaxes(pieces, 0, 1).reshape(own_rows, -1)

    qkv_own = to_owners(qkv_sums)
    query_own = joined(qkv_own[:, :, :query_here])
    key_own = joined(qkv_own[:, :, query_here : query_here + key_here])
    value_own = joined(qkv_own[:, :, query_here + key_here :])
    gain_one_own = own(gain_one)
    attention_gain_grad = (
        jnp.sum(own(low(query_weight)) * query_own, axis=1)
        + jnp.sum(own(low(key_weight)) * key_own, axis=1)
        + jnp.sum(own(low(value_weight)) * value_own, axis=1)
    )

    hidden_own = to_owners(gate_up_sums).reshape(seq_count, own_rows, 2, dp_count, piece)
    hidden_own = jnp.transpose(hidden_own, (2, 1, 3, 0, 4)).reshape(2, own_rows, hidden_width)
    gain_two_own = own(gain_two)
    feed_gain_grad = jnp.sum(own(low(gate_weight)) * hidden_own[0], axis=1) + jnp.sum(
        own(low(up_weight)) * hidden_own[1], axis=1
    )

    moves = [
        (dp * seq_count + seq, seq * dp_count + dp)
        for dp in range(dp_count)
        for seq in range(seq_count)
    ]
    output_own = lax.ppermute(output_sums.astype(BF), ("dp", "seq"), moves).astype(F32)

    return (
        layer_out.reshape(1, local_rows, -1),
        token_grad.reshape(1, local_rows, -1),
        attention_gain_grad,
        query_own * gain_one_own,
        key_own * gain_one_own,
        value_own * gain_one_own,
        gain_sums[0],
        gain_sums[1],
        output_own,
        feed_gain_grad,
        hidden_own[0] * gain_two_own,
        hidden_own[1] * gain_two_own,
        down_sums,
    )


def solution(mesh):
    in_specs = (
        P("dp", "seq", None),
        P("dp", None),
        P("dp", None),
        P("dp"),
        P("dp", None),
        P("dp", None),
        P("dp", None),
        P(),
        P(),
        P("dp", None),
        P("dp"),
        P("dp", None),
        P("dp", None),
        P("dp", None),
        P("dp", "seq", None),
    )
    out_specs = (
        P("dp", "seq", None),
        P("dp", "seq", None),
        P(("dp", "seq")),
        P(("dp", "seq"), None),
        P(("dp", "seq"), None),
        P(("dp", "seq"), None),
        P(),
        P(),
        P(("dp", "seq"), None),
        P(("dp", "seq")),
        P(("dp", "seq"), None),
        P(("dp", "seq"), None),
        P(("dp", "seq"), None),
    )
    return jax.shard_map(local, mesh=mesh, in_specs=in_specs, out_specs=out_specs, check_vma=False)
```

```python
import functools
import math

import jax
import jax.numpy as jnp
from jax import lax
from jax.experimental import pallas as pl
from jax.experimental.pallas import tpu as pltpu
from jax.sharding import PartitionSpec as P

EPS = 1e-05
ROPE_BASE = 1000000.0
NEG_FILL = -1e30
BF = jnp.bfloat16
F32 = jnp.float32
BLOCK = 128
PAIR = 128
VMEM_LIMIT = 48 * 1024 * 1024


def dot(left, right, dims):
    return lax.dot_general(left, right, (dims, ((), ())), preferred_element_type=F32)


def mm(left, right):
    return dot(left, right, ((1,), (0,)))


def mm_nt(left, right):
    return dot(left, right, ((1,), (1,)))


def mm_tn(left, right):
    return dot(left, right, ((0,), (0,)))


def rms_stats(values):
    factor = lax.rsqrt(jnp.mean(values * values, axis=-1, keepdims=True) + EPS)
    return (values * factor, factor)


def rms_back(grad_unit, unit_values, factor):
    return factor * (
        grad_unit - unit_values * jnp.mean(grad_unit * unit_values, axis=-1, keepdims=True)
    )


def doc_positions(segment_row):
    length = segment_row.shape[0]
    places = jnp.arange(length, dtype=jnp.int32)
    change = jnp.concatenate([jnp.ones((1,), dtype=jnp.bool_), segment_row[1:] != segment_row[:-1]])
    starts = lax.cummax(jnp.where(change, places, jnp.zeros_like(places)), axis=0)
    return places - starts


def rope_tables(positions, half_dim):
    frequency = ROPE_BASE ** (-jnp.arange(half_dim, dtype=F32) / half_dim)
    angles = positions.astype(F32)[:, None] * frequency[None, :]
    return (jnp.cos(angles), jnp.sin(angles))


def whole_vmem(count):
    return [pl.BlockSpec(memory_space=pltpu.VMEM)] * count


def scalars(count):
    return [pl.BlockSpec(memory_space=pltpu.SMEM)] * count


def lanes(shape):
    return lax.broadcasted_iota(jnp.int32, shape, 1)


def head_means(values, head_dim):
    width = values.shape[1]
    row = lax.broadcasted_iota(jnp.int32, (width, width), 0) // head_dim
    column = lax.broadcasted_iota(jnp.int32, (width, width), 1) // head_dim
    spread = jnp.where(row == column, 1.0 / head_dim, 0.0).astype(BF)
    high = values.astype(BF)
    rest = (values - high.astype(F32)).astype(BF)
    return mm(high, spread) + mm(rest, spread)


def half_partner(values, head_dim):
    half = head_dim // 2
    width = values.shape[1]
    upper = (lanes(values.shape) % head_dim) >= half
    return jnp.where(
        upper, pltpu.roll(values, half, 1), pltpu.roll(values, width - half, 1)
    )


def stacked_heads(pair, head_dim):
    first = lanes(pair.shape) < head_dim
    zero = jnp.zeros_like(pair)
    return jnp.concatenate([jnp.where(first, pair, zero), jnp.where(first, zero, pair)], axis=0)


def side_by_side(stacked, head_dim):
    rows = stacked.shape[0] // 2
    return jnp.where(
        lanes((rows, stacked.shape[1])) < head_dim, stacked[:rows], stacked[rows:]
    )


def mask_bias(start_ref, usable_ref, first_row, first_key, rows, window):
    row = first_row + lax.broadcasted_iota(jnp.int32, (rows, window), 0)
    key = first_key + lax.broadcasted_iota(jnp.int32, (rows, window), 1)
    start = start_ref[pl.ds(first_row, rows), :]
    usable = usable_ref[:, pl.ds(first_key, window)] > 0
    allowed = ((key >= start) & (key <= row) & usable) | (key == row)
    bias = jnp.where(allowed, 0.0, NEG_FILL)
    return jnp.concatenate([bias, bias], axis=0)


def each_block(low_ref, row_length, body):
    long_window = min(5 * BLOCK, row_length)

    def step(index, carry):
        first_row = pl.multiple_of(index * BLOCK, BLOCK)
        short_key = jnp.maximum(first_row - BLOCK, 0)
        is_short = low_ref[index] >= short_key

        @pl.when(is_short)
        def _():
            body(first_row, pl.multiple_of(short_key, BLOCK), 2 * BLOCK)

        @pl.when(jnp.logical_not(is_short))
        def _():
            long_key = jnp.maximum(first_row + BLOCK - long_window, 0)
            body(first_row, pl.multiple_of(long_key, BLOCK), long_window)

        return carry

    lax.fori_loop(0, row_length // BLOCK, step, 0)


def front_kernel(
    head_dim,
    place_ref,
    low_ref,
    x0_ref,
    x1_ref,
    x2_ref,
    x3_ref,
    weight_ref,
    cos_ref,
    sin_ref,
    gain_ref,
    start_ref,
    usable_ref,
    unit_ref,
    raw_ref,
    query_ref,
    key_ref,
    value_ref,
    mixed_ref,
):
    place = place_ref[0]
    pieces = (x0_ref, x1_ref, x2_ref, x3_ref)
    rows_each = x0_ref.shape[0]
    row_length = unit_ref.shape[0]
    query_groups = query_ref.shape[1] // PAIR
    chunk = 64
    for index, piece in enumerate(pieces):
        base = (place ^ index) * rows_each

        def normalize(step, carry, piece=piece, base=base):
            values = piece[pl.ds(pl.multiple_of(step * chunk, chunk), chunk), :].astype(F32)
            factor = lax.rsqrt(jnp.mean(values * values, axis=-1, keepdims=True) + EPS)
            unit_ref[pl.ds(pl.multiple_of(base + step * chunk, chunk), chunk), :] = (
                values * factor
            ).astype(BF)
            return carry

        lax.fori_loop(0, rows_each // chunk, normalize, 0)

    def project(step, carry):
        rows = pl.ds(pl.multiple_of(step * BLOCK, BLOCK), BLOCK)
        raw = mm(unit_ref[rows, :], weight_ref[...])
        raw_ref[rows, :] = raw[:, : raw_ref.shape[1]]
        cos = cos_ref[rows, :]
        sin = sin_ref[rows, :]
        for group in range(query_groups + 1):
            is_key = group == query_groups
            values = raw[:, group * PAIR : (group + 1) * PAIR]
            factor = lax.rsqrt(head_means(values * values, head_dim) + EPS)
            scaled = values * factor * gain_ref[int(is_key) : int(is_key) + 1, :]
            turned = scaled * cos + half_partner(scaled, head_dim) * sin
            if is_key:
                crossed = pltpu.roll(turned, head_dim, 1)
                first = lanes(turned.shape) < head_dim
                key_ref[rows, :PAIR] = jnp.where(first, turned, crossed).astype(BF)
                key_ref[rows, PAIR:] = jnp.where(first, crossed, turned).astype(BF)
                values = raw[:, (group + 1) * PAIR :]
                crossed = pltpu.roll(values, head_dim, 1)
                value_ref[rows, :PAIR] = jnp.where(first, values, crossed).astype(BF)
                value_ref[rows, PAIR:] = jnp.where(first, crossed, values).astype(BF)
            else:
                query_ref[rows, group * PAIR : (group + 1) * PAIR] = (
                    turned * (1.0 / math.sqrt(head_dim))
                ).astype(BF)
        return carry

    lax.fori_loop(0, row_length // BLOCK, project, 0)

    def attend(first_row, first_key, window):
        bias = mask_bias(start_ref, usable_ref, first_row, first_key, BLOCK, window)
        rows = pl.ds(first_row, BLOCK)
        keys = pl.ds(first_key, window)
        for group in range(query_groups):
            pair = slice(group * PAIR, (group + 1) * PAIR)
            stacked = stacked_heads(query_ref[rows, pair], head_dim)
            grown = jnp.exp(mm_nt(stacked, key_ref[keys, pair]) + bias)
            share = grown * (1.0 / jnp.sum(grown, axis=-1, keepdims=True))
            mixed = mm(share.astype(BF), value_ref[keys, pair])
            mixed_ref[rows, pair] = side_by_side(mixed, head_dim).astype(BF)

    each_block(low_ref, row_length, attend)


def middle_kernel(
    place_ref,
    x0_ref,
    x1_ref,
    x2_ref,
    x3_ref,
    o0_ref,
    o1_ref,
    o2_ref,
    o3_ref,
    w0_ref,
    w1_ref,
    w2_ref,
    w3_ref,
    unit_ref,
    here_ref,
    sum_ref,
):
    place = place_ref[0]
    rows_each, width = x0_ref.shape
    heads = o0_ref.shape[1]
    columns = w0_ref.shape[1]
    chunk = 64
    for index, piece in enumerate((x0_ref, x1_ref, x2_ref, x3_ref)):
        base = pl.multiple_of((place ^ index) * rows_each, rows_each)
        rows = pl.ds(base, rows_each)
        for part, weight in enumerate((w0_ref, w1_ref, w2_ref, w3_ref)):
            total = None
            for other, mixed in enumerate((o0_ref, o1_ref, o2_ref, o3_ref)):
                features = pl.ds(pl.multiple_of((place ^ other) * heads, heads), heads)
                term = mm(mixed[rows, :], weight[features, :])
                total = term if total is None else total + term
            spot = pl.multiple_of((place ^ part) * columns, columns)
            sum_ref[:, pl.ds(spot, columns)] = total

        def normalize(step, carry, piece=piece, base=base, index=index):
            part = pl.ds(pl.multiple_of(step * chunk, chunk), chunk)
            values = sum_ref[part, :] + piece[part, :].astype(F32)
            if index == 0:
                here_ref[part, :] = values
            factor = lax.rsqrt(jnp.mean(values * values, axis=-1, keepdims=True) + EPS)
            unit_ref[pl.ds(pl.multiple_of(base + step * chunk, chunk), chunk), :] = (
                values * factor
            ).astype(BF)
            return carry

        lax.fori_loop(0, rows_each // chunk, normalize, 0)


def back_kernel(
    head_dim,
    low_ref,
    grad_ref,
    query_ref,
    key_ref,
    value_ref,
    raw_ref,
    cos_ref,
    sin_ref,
    gain_ref,
    start_ref,
    usable_ref,
    out_ref,
    terms_ref,
    key_sum_ref,
    value_sum_ref,
):
    row_length = grad_ref.shape[0]
    query_groups = query_ref.shape[1] // PAIR
    scale = 1.0 / math.sqrt(head_dim)
    key_sum_ref[...] = jnp.zeros_like(key_sum_ref)
    value_sum_ref[...] = jnp.zeros_like(value_sum_ref)
    terms_ref[...] = jnp.zeros_like(terms_ref)

    def through_norm(rows, group, grad, kind):
        grad = grad.astype(BF).astype(F32)
        turned = grad * cos_ref[rows, :] - half_partner(grad, head_dim) * sin_ref[rows, :]
        values = raw_ref[rows, group * PAIR : (group + 1) * PAIR]
        factor = lax.rsqrt(head_means(values * values, head_dim) + EPS)
        unit = values * factor
        terms_ref[kind : kind + 1, :] += jnp.sum(turned * unit, axis=0, keepdims=True)
        scaled = turned * gain_ref[kind : kind + 1, :]
        back = factor * (scaled - unit * head_means(scaled * unit, head_dim))
        out_ref[rows, group * PAIR : (group + 1) * PAIR] = back.astype(BF)

    def attend(first_row, first_key, window):
        bias = mask_bias(start_ref, usable_ref, first_row, first_key, BLOCK, window)
        rows = pl.ds(first_row, BLOCK)
        keys = pl.ds(first_key, window)
        for group in range(query_groups):
            pair = slice(group * PAIR, (group + 1) * PAIR)
            stacked = stacked_heads(query_ref[rows, pair], head_dim)
            grads = stacked_heads(grad_ref[rows, pair], head_dim)
            grown = jnp.exp(mm_nt(stacked, key_ref[keys, pair]) + bias)
            share = grown * (1.0 / jnp.sum(grown, axis=-1, keepdims=True))
            grad_share = mm_nt(grads, value_ref[keys, pair])
            centre = jnp.sum(share * grad_share, axis=-1, keepdims=True)
            grad_score = (share * (grad_share - centre)).astype(BF)
            grad_query = side_by_side(mm(grad_score, key_ref[keys, pair]), head_dim) * scale
            key_sum_ref[keys, pair] += mm_tn(grad_score, stacked)
            value_sum_ref[keys, pair] += mm_tn(share.astype(BF), grads)
            through_norm(rows, group, grad_query, 0)

    each_block(low_ref, row_length, attend)

    def folded(sum_ref, rows):
        first = sum_ref[rows, :PAIR]
        second = sum_ref[rows, PAIR:]
        return jnp.where(
            lanes(first.shape) < head_dim,
            first + pltpu.roll(first, head_dim, 1),
            second + pltpu.roll(second, head_dim, 1),
        )

    def finish(step, carry):
        rows = pl.ds(pl.multiple_of(step * BLOCK, BLOCK), BLOCK)
        through_norm(rows, query_groups, folded(key_sum_ref, rows), 1)
        out_ref[rows, (query_groups + 1) * PAIR :] = folded(value_sum_ref, rows).astype(BF)
        return carry

    lax.fori_loop(0, row_length // BLOCK, finish, 0)


def attention_pack_kernel(
    place_ref, query_ref, key_ref, value_ref, output_ref, gain_ref, pack_ref
):
    gain = gain_ref[...].astype(BF).astype(F32)
    start = 0
    for weight_ref in (query_ref, key_ref, value_ref):
        size = weight_ref.shape[1]
        pack_ref[:, start : start + size] = (
            weight_ref[...].astype(BF).astype(F32) * gain
        ).astype(BF)
        start += size
    pack_ref[:, start:] = output_ref[...].astype(BF)


def hidden_pack_kernel(pieces, seq_count, place_ref, gate_ref, up_ref, gain_ref, pack_ref):
    piece = gate_ref.shape[1] // (pieces * seq_count)
    here = pieces * piece
    chunk = 16
    for place in range(seq_count):

        @pl.when(place_ref[0] == place)
        def _(place=place):
            def step(index, carry):
                rows = pl.ds(pl.multiple_of(index * chunk, chunk), chunk)
                gain = gain_ref[rows, :].astype(BF).astype(F32)
                for part, weight_ref in enumerate((gate_ref, up_ref)):
                    joined = jnp.concatenate(
                        [
                            weight_ref[rows, start : start + piece]
                            for start in range(
                                place * piece, weight_ref.shape[1], seq_count * piece
                            )
                        ],
                        axis=1,
                    )
                    pack_ref[rows, part * here : (part + 1) * here] = (
                        joined.astype(BF).astype(F32) * gain
                    ).astype(BF)
                return carry

            lax.fori_loop(0, gate_ref.shape[0] // chunk, step, 0)


def hidden_owner_kernel(
    pieces, place_ref, sums_ref, gate_ref, up_ref, gain_ref, gate_grad_ref, up_grad_ref, terms_ref
):
    seq_count = sums_ref.shape[0]
    here = sums_ref.shape[2] // 2
    piece = here // pieces
    gain = gain_ref[...].astype(BF).astype(F32)
    total = None
    for part, (weight_ref, grad_ref) in enumerate(
        ((gate_ref, gate_grad_ref), (up_ref, up_grad_ref))
    ):
        sums = [sums_ref[seq].astype(F32) for seq in range(seq_count)]
        joined = jnp.concatenate(
            [
                sums[seq][:, part * here + step * piece : part * here + (step + 1) * piece]
                for step in range(pieces)
                for seq in range(seq_count)
            ],
            axis=1,
        )
        term = jnp.sum(weight_ref[...].astype(BF).astype(F32) * joined, axis=1, keepdims=True)
        total = term if total is None else total + term
        grad_ref[...] = joined * gain
    terms_ref[...] = total


def attention_owner_kernel(
    place_ref,
    sums_ref,
    query_ref,
    key_ref,
    value_ref,
    gain_ref,
    query_grad_ref,
    key_grad_ref,
    value_grad_ref,
    terms_ref,
):
    seq_count = sums_ref.shape[0]
    gain = gain_ref[...].astype(BF).astype(F32)
    start = 0
    total = None
    for weight_ref, grad_ref in (
        (query_ref, query_grad_ref),
        (key_ref, key_grad_ref),
        (value_ref, value_grad_ref),
    ):
        size = weight_ref.shape[1] // seq_count
        joined = jnp.concatenate(
            [sums_ref[seq, :, start : start + size].astype(F32) for seq in range(seq_count)],
            axis=1,
        )
        start += size
        term = jnp.sum(weight_ref[...].astype(BF).astype(F32) * joined, axis=1, keepdims=True)
        total = term if total is None else total + term
        grad_ref[...] = joined * gain
    terms_ref[...] = total


def placed_call(kernel, results, place_array, operands, blocks, flops=0, moved=0):
    return pl.pallas_call(
        kernel,
        out_shape=[jax.ShapeDtypeStruct(shape, kind) for shape, kind in results],
        grid_spec=pltpu.PrefetchScalarGridSpec(
            num_scalar_prefetch=1,
            grid=(1,),
            in_specs=[pl.BlockSpec(shape, index) for shape, index in blocks],
            out_specs=[
                pl.BlockSpec(shape, lambda i, place, rank=len(shape): (0,) * rank)
                for shape, _ in results
            ],
        ),
        compiler_params=pltpu.CompilerParams(vmem_limit_bytes=VMEM_LIMIT),
        cost_estimate=pl.CostEstimate(flops=flops, bytes_accessed=moved, transcendentals=0),
    )(place_array, *operands)


def own_columns(i, place):
    return (0, place[0])


def own_rows_block(i, place):
    return (place[0], 0)


def everything(i, place):
    return (0, 0)


def call(kernel, results, scalar_count, operands, scratch=(), flops=0, moved=0):
    return pl.pallas_call(
        kernel,
        out_shape=[jax.ShapeDtypeStruct(shape, kind) for shape, kind in results],
        in_specs=scalars(scalar_count) + whole_vmem(len(operands) - scalar_count),
        out_specs=whole_vmem(len(results)),
        scratch_shapes=list(scratch),
        compiler_params=pltpu.CompilerParams(vmem_limit_bytes=VMEM_LIMIT),
        cost_estimate=pl.CostEstimate(flops=flops, bytes_accessed=moved, transcendentals=0),
    )(*operands)


def swap(values, bit):
    count = lax.axis_size("seq")
    return lax.ppermute(values, "seq", [(i, i ^ bit) for i in range(count)])


def seq_pieces(values):
    far = swap(values, 2)
    near = swap(values, 1)
    return (values, near, far, swap(far, 1))


def in_order(pieces):
    place = lax.axis_index("seq")
    odd = (place & 1) == 1
    high = place >= 2
    mine = (jnp.where(odd, pieces[1], pieces[0]), jnp.where(odd, pieces[0], pieces[1]))
    theirs = (jnp.where(odd, pieces[3], pieces[2]), jnp.where(odd, pieces[2], pieces[3]))
    return jnp.stack(
        [
            jnp.where(high, theirs[0], mine[0]),
            jnp.where(high, theirs[1], mine[1]),
            jnp.where(high, mine[0], theirs[0]),
            jnp.where(high, mine[1], theirs[1]),
        ]
    )


def seq_scatter(values):
    place = lax.axis_index("seq")
    rows = values.shape[0] // 4
    split = values.reshape(2, 2, rows, -1)
    odd = (place & 1) == 1
    high = place >= 2
    keep = jnp.where(odd, split[:, 1], split[:, 0])
    send = jnp.where(odd, split[:, 0], split[:, 1]).astype(BF)
    pair = keep + swap(send, 1).astype(F32)
    keep = jnp.where(high, pair[1], pair[0])
    send = jnp.where(high, pair[0], pair[1]).astype(BF)
    return keep + swap(send, 2).astype(F32)


def after(values, *others):
    return lax.optimization_barrier((values, others))[0]


def ring_length():
    count = lax.axis_size("dp")
    return count if count % 2 == 0 and 4 <= count <= 8 else 0


def ring_order(count):
    return list(range(0, count, 2)) + list(range(count - 1, 0, -2))


def ring_source(offset):
    count = lax.axis_size("dp")
    place = lax.axis_index("dp")
    spot = jnp.where(place % 2 == 0, place // 2, count - 1 - place // 2)
    spot = (spot + offset + count) % count
    return jnp.where(spot < count // 2, 2 * spot, 2 * (count - 1 - spot) + 1)


def ring_move(values, step):
    count = lax.axis_size("dp")
    order = ring_order(count)
    return lax.ppermute(
        values, "dp", [(order[i], order[(i + step) % count]) for i in range(count)]
    )


def dp_gather(shard):
    count = ring_length()
    if not count:
        return (lax.all_gather(shard, "dp", axis=0, tiled=True), shard)
    rows = shard.shape[0]
    half = rows // 32 * 16 or rows // 2
    whole = jnp.zeros((count * rows, shard.shape[1]), shard.dtype)
    whole = lax.dynamic_update_slice_in_dim(whole, shard, ring_source(0) * rows, 0)
    up = down = shard
    for step in range(1, count // 2):
        up = ring_move(up, 1)
        down = ring_move(down, -1)
        whole = lax.dynamic_update_slice_in_dim(whole, up, ring_source(-step) * rows, 0)
        whole = lax.dynamic_update_slice_in_dim(whole, down, ring_source(step) * rows, 0)
    sign = (up, down)
    first = ring_move(up[:half], 1)
    second = ring_move(down[half:], -1)
    far = jnp.concatenate([first, second])
    whole = lax.dynamic_update_slice_in_dim(whole, far, ring_source(count // 2) * rows, 0)
    return (whole, sign)


def dp_scatter(terms):
    count = ring_length()
    if not count:
        sums = lax.psum_scatter(terms.astype(BF), "dp", scatter_dimension=0, tiled=True)
        return (sums.astype(F32), sums)
    rows = terms.shape[0] // count
    half = rows // 32 * 16 or rows // 2

    def term(offset):
        return lax.dynamic_slice_in_dim(terms, ring_source(offset) * rows, rows, 0)

    far = term(count // 2)
    up = ring_move(far[:half].astype(BF), 1).astype(F32)
    down = ring_move(far[half:].astype(BF), -1).astype(F32)
    blank = jnp.zeros((rows - half, terms.shape[1]), F32)
    up = jnp.concatenate([up, blank])
    down = jnp.concatenate([jnp.zeros((half, terms.shape[1]), F32), down])
    sign = (up, down)
    for step in range(count // 2 - 1, 0, -1):
        sign = (up, down)
        up = ring_move((term(step) + up).astype(BF), 1).astype(F32)
        down = ring_move((term(-step) + down).astype(BF), -1).astype(F32)
    return (term(0) + up + down, sign)


def sum_all(values):
    for axis in ("seq", "dp"):
        count = lax.axis_size(axis)
        bit = 1
        while bit < count:
            values = values + lax.ppermute(values, axis, [(i, i ^ bit) for i in range(count)])
            bit *= 2
    return values


def local(
    tokens,
    segments,
    valid_mask,
    attention_gain,
    query_weight,
    key_weight,
    value_weight,
    query_gain,
    key_gain,
    output_weight,
    feedforward_gain,
    gate_weight,
    up_weight,
    down_weight,
    cotangent,
):
    seq_count = lax.axis_size("seq")
    dp_count = lax.axis_size("dp")
    place = lax.axis_index("seq")
    local_rows = tokens.shape[1]
    row_length = segments.shape[1]
    head_dim = query_gain.shape[0]
    width = tokens.shape[2]
    hidden_width = gate_weight.shape[1]
    query_width = query_weight.shape[1]
    key_width = key_weight.shape[1]
    query_here = query_width // seq_count
    key_here = key_width // seq_count
    hidden_here = hidden_width // seq_count
    weight_rows = query_weight.shape[0]
    own_rows = weight_rows // seq_count
    segment_row = segments[0]
    valid_row = valid_mask[0]

    def low(weight):
        return weight.astype(BF).astype(F32)

    place_array = place.astype(jnp.int32).reshape(1)
    gain_one = attention_gain[:, None]
    gain_two = feedforward_gain[:, None]
    qkv_width = query_here + 2 * key_here
    piece = hidden_width // (dp_count * seq_count)
    kernels_fit = weight_rows % 16 == 0 and own_rows % 8 == 0 and dp_count <= 8

    (attention_pack,) = placed_call(
        attention_pack_kernel,
        [((weight_rows, qkv_width + width // seq_count), BF)],
        place_array,
        (query_weight, key_weight, value_weight, output_weight, gain_one),
        [
            ((weight_rows, query_here), own_columns),
            ((weight_rows, key_here), own_columns),
            ((weight_rows, key_here), own_columns),
            ((weight_rows, width // seq_count), own_columns),
            ((weight_rows, 1), everything),
        ],
        moved=8 * weight_rows * width,
    )
    if kernels_fit:
        (gate_up_pack,) = placed_call(
            functools.partial(hidden_pack_kernel, dp_count, seq_count),
            [((weight_rows, 2 * hidden_here), BF)],
            place_array,
            (gate_weight, up_weight, gain_two),
            [
                ((weight_rows, hidden_width), everything),
                ((weight_rows, hidden_width), everything),
                ((weight_rows, 1), everything),
            ],
            moved=8 * weight_rows * hidden_width,
        )
    else:

        def hidden_columns(weight):
            split = weight.reshape(weight_rows, dp_count, seq_count, piece)
            mine = lax.dynamic_index_in_dim(split, place, 2, keepdims=False)
            return (low(mine.reshape(weight_rows, hidden_here)) * low(gain_two)).astype(BF)

        gate_up_pack = jnp.concatenate(
            [hidden_columns(gate_weight), hidden_columns(up_weight)], axis=1
        )
    down_pack = lax.dynamic_slice_in_dim(down_weight, place * piece, piece, 0).astype(BF)

    token_pieces = seq_pieces(tokens[0])
    grad_row_pieces = seq_pieces(after(cotangent[0], token_pieces[2]))

    attention_all, sign = dp_gather(attention_pack)
    gate_up_all = lax.all_gather(gate_up_pack, "dp", axis=0, tiled=True)
    down_all, sign = dp_gather(after(down_pack, sign))

    qkv_weight = attention_all[:, :qkv_width]
    output_pieces = seq_pieces(attention_all[:, qkv_width:])
    grad_rows = in_order(grad_row_pieces).reshape(row_length, width)

    positions = doc_positions(segment_row)
    starts = jnp.arange(row_length, dtype=jnp.int32) - positions
    block_lows = starts[::BLOCK]
    cos_table, sin_table = rope_tables(positions, head_dim // 2)
    repeats = PAIR // head_dim
    cos_wide = jnp.tile(cos_table, (1, 2 * repeats))
    sin_wide = jnp.tile(jnp.concatenate([-sin_table, sin_table], axis=1), (1, repeats))
    head_gains = jnp.tile(jnp.stack([query_gain, key_gain]), (1, repeats))
    row_starts = starts[:, None]
    usable = valid_row[None, :]
    unit_one, raw, queries, keys_two, values_two, mixed_here = call(
        functools.partial(front_kernel, head_dim),
        [
            ((row_length, width), BF),
            ((row_length, query_here + key_here), F32),
            ((row_length, query_here), BF),
            ((row_length, 2 * key_here), BF),
            ((row_length, 2 * key_here), BF),
            ((row_length, query_here), BF),
        ],
        2,
        (place_array, block_lows, *token_pieces, qkv_weight, cos_wide, sin_wide)
        + (head_gains, row_starts, usable),
        flops=4 * row_length * width * qkv_width,
        moved=12 * row_length * width,
    )
    mixed_pieces = seq_pieces(mixed_here)
    unit_two, after_here = call(
        middle_kernel,
        [((row_length, width), BF), ((local_rows, width), F32)],
        1,
        (place_array, *token_pieces, *mixed_pieces, *output_pieces),
        scratch=[pltpu.VMEM((local_rows, width), F32)],
        flops=2 * row_length * width * width,
        moved=10 * row_length * width,
    )

    gate_up = mm(unit_two, gate_up_all)
    gate_value = gate_up[:, :hidden_here]
    up_value = gate_up[:, hidden_here:]
    sigmoid_gate = jax.nn.sigmoid(gate_value)
    silu_gate = gate_value * sigmoid_gate
    hidden = (silu_gate * up_value).astype(BF)
    grad_hidden = mm_nt(grad_rows, down_all)
    grad_gate = (
        grad_hidden * up_value * sigmoid_gate * (1.0 + gate_value * (1.0 - sigmoid_gate))
    ).astype(BF)
    grad_up = (grad_hidden * silu_gate).astype(BF)
    grad_gate_up = jnp.concatenate([grad_gate, grad_up], axis=1)
    grad_normed = mm_nt(grad_gate_up, gate_up_all)

    down_terms = mm_tn(hidden, grad_rows)
    gate_up_terms = mm_tn(unit_two, grad_gate_up)
    down_sums, sign = dp_scatter(down_terms)
    gate_up_sums = lax.psum_scatter(
        gate_up_terms.astype(BF), "dp", scatter_dimension=0, tiled=True
    )

    grad_normed = seq_scatter(grad_normed)

    unit_here, factor_here = rms_stats(after_here)
    grad_after = cotangent[0].astype(F32) + rms_back(grad_normed, unit_here, factor_here)
    grad_branch = in_order(seq_pieces(grad_after.astype(BF))).reshape(row_length, width)
    output_here = jnp.concatenate(
        list(
            in_order(
                [
                    lax.dynamic_slice_in_dim(piece, place * query_here, query_here, 0)
                    for piece in output_pieces
                ]
            )
        ),
        axis=1,
    )
    grad_mixed = mm_nt(grad_branch, output_here).astype(BF)
    output_terms = mm_tn(mixed_here, grad_branch)
    layer_out = (after_here + seq_scatter(mm(after(hidden, grad_branch), down_all))).astype(BF)
    qkv_grad, gain_terms = call(
        functools.partial(back_kernel, head_dim),
        [((row_length, qkv_width), BF), ((8, PAIR), F32)],
        1,
        (block_lows, grad_mixed, queries, keys_two, values_two, raw, cos_wide, sin_wide)
        + (head_gains, row_starts, usable),
        scratch=[pltpu.VMEM((row_length, 2 * key_here), F32)] * 2,
        flops=8 * row_length * width * qkv_width,
        moved=12 * row_length * width,
    )
    qkv_terms = mm_tn(unit_one, qkv_grad)
    grad_one = mm_nt(qkv_grad, qkv_weight)
    side = width // qkv_width
    chunk_rows = query_width // (dp_count * seq_count)
    attention_terms = [qkv_terms.reshape(dp_count, weight_rows, qkv_width)]
    for part in range(side):
        attention_terms.append(
            output_terms[:, part * qkv_width : (part + 1) * qkv_width].reshape(
                dp_count, chunk_rows, qkv_width
            )
        )
    attention_terms = jnp.concatenate(attention_terms, axis=1).reshape(-1, qkv_width)
    attention_terms, grad_one = lax.optimization_barrier((after(attention_terms, sign), grad_one))
    attention_sums, sign = dp_scatter(attention_terms)
    qkv_sums = attention_sums[:weight_rows]
    output_sums = jnp.concatenate(
        [
            attention_sums[weight_rows + part * chunk_rows : weight_rows + (part + 1) * chunk_rows]
            for part in range(side)
        ],
        axis=1,
    )
    grad_one = seq_scatter(grad_one)
    unit_tokens, factor_tokens = rms_stats(tokens[0].astype(F32))
    token_grad = (grad_after + rms_back(grad_one, unit_tokens, factor_tokens)).astype(BF)
    gain_sums = jnp.sum(sum_all(gain_terms)[:2].reshape(2, repeats, head_dim), axis=1)

    def to_owners(sums):
        return lax.all_to_all(
            sums.astype(BF).reshape(seq_count, own_rows, -1), "seq", split_axis=0, concat_axis=0, tiled=True
        )

    def own(weight):
        return lax.dynamic_slice_in_dim(weight, place * own_rows, own_rows, 0)

    def joined(pieces):
        return jnp.swapaxes(pieces, 0, 1).reshape(own_rows, -1).astype(F32)

    hidden_own = to_owners(gate_up_sums)
    qkv_own = to_owners(qkv_sums)
    if kernels_fit:
        gate_grad, up_grad, feed_gain_grad = placed_call(
            functools.partial(hidden_owner_kernel, dp_count),
            [((own_rows, hidden_width), F32)] * 2 + [((own_rows, 1), F32)],
            place_array,
            (hidden_own, gate_weight, up_weight, gain_two),
            [
                (hidden_own.shape, lambda i, place: (0, 0, 0)),
                ((own_rows, hidden_width), own_rows_block),
                ((own_rows, hidden_width), own_rows_block),
                ((own_rows, 1), own_rows_block),
            ],
            moved=20 * own_rows * hidden_width,
        )
        query_grad, key_grad, value_grad, attention_gain_grad = placed_call(
            attention_owner_kernel,
            [((own_rows, query_width), F32)]
            + [((own_rows, key_width), F32)] * 2
            + [((own_rows, 1), F32)],
            place_array,
            (qkv_own, query_weight, key_weight, value_weight, gain_one),
            [
                (qkv_own.shape, lambda i, place: (0, 0, 0)),
                ((own_rows, query_width), own_rows_block),
                ((own_rows, key_width), own_rows_block),
                ((own_rows, key_width), own_rows_block),
                ((own_rows, 1), own_rows_block),
            ],
            moved=20 * own_rows * query_width,
        )
    else:
        query_own = joined(qkv_own[:, :, :query_here])
        key_own = joined(qkv_own[:, :, query_here : query_here + key_here])
        value_own = joined(qkv_own[:, :, query_here + key_here :])
        attention_gain_grad = (
            jnp.sum(own(low(query_weight)) * query_own, axis=1)
            + jnp.sum(own(low(key_weight)) * key_own, axis=1)
            + jnp.sum(own(low(value_weight)) * value_own, axis=1)
        )
        gain_own = own(low(gain_one))
        query_grad, key_grad, value_grad = (
            query_own * gain_own,
            key_own * gain_own,
            value_own * gain_own,
        )
        hidden_own = hidden_own.reshape(seq_count, own_rows, 2, dp_count, piece)
        hidden_own = jnp.transpose(hidden_own, (2, 1, 3, 0, 4))
        hidden_own = hidden_own.reshape(2, own_rows, hidden_width).astype(F32)
        feed_gain_grad = jnp.sum(own(low(gate_weight)) * hidden_own[0], axis=1) + jnp.sum(
            own(low(up_weight)) * hidden_own[1], axis=1
        )
        gain_own = own(low(gain_two))
        gate_grad, up_grad = (hidden_own[0] * gain_own, hidden_own[1] * gain_own)

    moves = [
        (dp * seq_count + seq, seq * dp_count + dp)
        for dp in range(dp_count)
        for seq in range(seq_count)
    ]
    output_own = lax.ppermute(output_sums.astype(BF), ("dp", "seq"), moves).astype(F32)

    return (
        layer_out.reshape(1, local_rows, -1),
        token_grad.reshape(1, local_rows, -1),
        attention_gain_grad.reshape(own_rows),
        query_grad,
        key_grad,
        value_grad,
        gain_sums[0],
        gain_sums[1],
        output_own,
        feed_gain_grad.reshape(own_rows),
        gate_grad,
        up_grad,
        down_sums,
    )


def solution(mesh):
    in_specs = (
        P("dp", "seq", None),
        P("dp", None),
        P("dp", None),
        P("dp"),
        P("dp", None),
        P("dp", None),
        P("dp", None),
        P(),
        P(),
        P("dp", None),
        P("dp"),
        P("dp", None),
        P("dp", None),
        P("dp", None),
        P("dp", "seq", None),
    )
    out_specs = (
        P("dp", "seq", None),
        P("dp", "seq", None),
        P(("dp", "seq")),
        P(("dp", "seq"), None),
        P(("dp", "seq"), None),
        P(("dp", "seq"), None),
        P(),
        P(),
        P(("dp", "seq"), None),
        P(("dp", "seq")),
        P(("dp", "seq"), None),
        P(("dp", "seq"), None),
        P(("dp", "seq"), None),
    )
    return jax.shard_map(local, mesh=mesh, in_specs=in_specs, out_specs=out_specs, check_vma=False)
```

```python
import functools
import math

import jax
import jax.numpy as jnp
from jax import lax
from jax.experimental import pallas as pl
from jax.experimental.pallas import tpu as pltpu
from jax.sharding import PartitionSpec as P

EPS = 1e-05
ROPE_BASE = 1000000.0
NEG_FILL = -1e30
BF = jnp.bfloat16
F32 = jnp.float32
BLOCK = 128
PAIR = 128
SEQ = 4
MEGA = 1024 * 1024


def dot(left, right, dims):
    return lax.dot_general(left, right, (dims, ((), ())), preferred_element_type=F32)


def mm(left, right):
    return dot(left, right, ((1,), (0,)))


def mm_nt(left, right):
    return dot(left, right, ((1,), (1,)))


def mm_tn(left, right):
    return dot(left, right, ((0,), (0,)))


def rms_stats(values):
    factor = lax.rsqrt(jnp.mean(values * values, axis=-1, keepdims=True) + EPS)
    return (values * factor, factor)


def rms_back(grad_unit, unit_values, factor):
    return factor * (
        grad_unit - unit_values * jnp.mean(grad_unit * unit_values, axis=-1, keepdims=True)
    )


def doc_positions(segment_row):
    length = segment_row.shape[0]
    places = jnp.arange(length, dtype=jnp.int32)
    change = jnp.concatenate([jnp.ones((1,), dtype=jnp.bool_), segment_row[1:] != segment_row[:-1]])
    starts = lax.cummax(jnp.where(change, places, jnp.zeros_like(places)), axis=0)
    return places - starts


def rope_tables(positions, head_dim):
    half = head_dim // 2
    lane = jnp.arange(PAIR, dtype=jnp.int32)
    frequency = ROPE_BASE ** (-(lane % half).astype(F32) / half)
    angles = positions.astype(F32)[:, None] * frequency[None, :]
    sign = jnp.where(lane % head_dim < half, -1.0, 1.0)
    return (jnp.cos(angles), jnp.sin(angles) * sign[None, :])


def whole_vmem(count):
    return [pl.BlockSpec(memory_space=pltpu.VMEM)] * count


def scalars(count):
    return [pl.BlockSpec(memory_space=pltpu.SMEM)] * count


def lanes(shape):
    return lax.broadcasted_iota(jnp.int32, shape, 1)


def head_means(values, head_dim):
    width = values.shape[1]
    row = lax.broadcasted_iota(jnp.int32, (width, width), 0) // head_dim
    column = lax.broadcasted_iota(jnp.int32, (width, width), 1) // head_dim
    spread = jnp.where(row == column, 1.0 / head_dim, 0.0).astype(BF)
    high = values.astype(BF)
    rest = (values - high.astype(F32)).astype(BF)
    return mm(high, spread) + mm(rest, spread)


def half_partner(values, head_dim):
    half = head_dim // 2
    width = values.shape[1]
    upper = (lanes(values.shape) % head_dim) >= half
    return jnp.where(
        upper, pltpu.roll(values, half, 1), pltpu.roll(values, width - half, 1)
    )


def stacked_heads(pair, head_dim):
    first = lanes(pair.shape) < head_dim
    zero = jnp.zeros_like(pair)
    return jnp.concatenate([jnp.where(first, pair, zero), jnp.where(first, zero, pair)], axis=0)


def side_by_side(stacked, head_dim):
    rows = stacked.shape[0] // 2
    return jnp.where(
        lanes((rows, stacked.shape[1])) < head_dim, stacked[:rows], stacked[rows:]
    )


def mask_bias(start_ref, usable_ref, first_row, first_key, rows, window):
    row = first_row + lax.broadcasted_iota(jnp.int32, (rows, window), 0)
    key = first_key + lax.broadcasted_iota(jnp.int32, (rows, window), 1)
    start = start_ref[pl.ds(first_row, rows), :]
    usable = usable_ref[:, pl.ds(first_key, window)] > 0
    allowed = ((key >= start) & (key <= row) & usable) | (key == row)
    bias = jnp.where(allowed, 0.0, NEG_FILL)
    return jnp.concatenate([bias, bias], axis=0)


def each_block(low_ref, row_length, body):
    long_window = min(5 * BLOCK, row_length)

    def step(index, carry):
        first_row = pl.multiple_of(index * BLOCK, BLOCK)
        short_key = jnp.maximum(first_row - BLOCK, 0)
        is_short = low_ref[index] >= short_key

        @pl.when(is_short)
        def _():
            body(first_row, pl.multiple_of(short_key, BLOCK), 2 * BLOCK)

        @pl.when(jnp.logical_not(is_short))
        def _():
            long_key = jnp.maximum(first_row + BLOCK - long_window, 0)
            body(first_row, pl.multiple_of(long_key, BLOCK), long_window)

        return carry

    lax.fori_loop(0, row_length // BLOCK, step, 0)


def load_pieces(offset_ref, piece_refs, semaphore, *targets):
    copies = []
    for index, piece in enumerate(piece_refs):
        start = pl.multiple_of(offset_ref[index], 16)
        for part, (target, column) in enumerate(targets):
            rows = pl.ds(start, piece.shape[0])
            copies.append(
                pltpu.make_async_copy(
                    piece.at[:, column : column + target.shape[1]],
                    target.at[rows, :],
                    semaphore.at[part, index],
                )
            )
    for copy in copies:
        copy.start()

    def wait():
        for copy in copies:
            copy.wait()

    return wait


def project_kernel(
    head_dim,
    place_ref,
    offset_ref,
    x0_ref,
    x1_ref,
    x2_ref,
    x3_ref,
    cos_ref,
    sin_ref,
    gain_ref,
    *rest,
):
    (*piece_refs, unit_ref, raw_ref, query_ref, key_ref, value_ref, weight_ref, output_ref) = rest[:-1]
    semaphore = rest[-1]
    wait = load_pieces(
        offset_ref, piece_refs, semaphore, (weight_ref, 0), (output_ref, weight_ref.shape[1])
    )
    place = place_ref[0]
    pieces = (x0_ref, x1_ref, x2_ref, x3_ref)
    rows_each = x0_ref.shape[0]
    row_length = unit_ref.shape[0]
    query_groups = query_ref.shape[1] // PAIR
    chunk = 64
    for index, piece in enumerate(pieces):
        base = (place ^ index) * rows_each

        def normalize(step, carry, piece=piece, base=base):
            values = piece[pl.ds(pl.multiple_of(step * chunk, chunk), chunk), :].astype(F32)
            factor = lax.rsqrt(jnp.mean(values * values, axis=-1, keepdims=True) + EPS)
            unit_ref[pl.ds(pl.multiple_of(base + step * chunk, chunk), chunk), :] = (
                values * factor
            ).astype(BF)
            return carry

        lax.fori_loop(0, rows_each // chunk, normalize, 0)

    wait()

    def project(step, carry):
        rows = pl.ds(pl.multiple_of(step * BLOCK, BLOCK), BLOCK)
        raw = mm(unit_ref[rows, :], weight_ref[...])
        raw_ref[rows, :] = raw[:, : raw_ref.shape[1]]
        cos = cos_ref[rows, :]
        sin = sin_ref[rows, :]
        for group in range(query_groups + 1):
            is_key = group == query_groups
            values = raw[:, group * PAIR : (group + 1) * PAIR]
            factor = lax.rsqrt(head_means(values * values, head_dim) + EPS)
            scaled = values * factor * gain_ref[int(is_key) : int(is_key) + 1, :]
            turned = scaled * cos + half_partner(scaled, head_dim) * sin
            if is_key:
                crossed = pltpu.roll(turned, head_dim, 1)
                first = lanes(turned.shape) < head_dim
                key_ref[rows, :PAIR] = jnp.where(first, turned, crossed).astype(BF)
                key_ref[rows, PAIR:] = jnp.where(first, crossed, turned).astype(BF)
                values = raw[:, (group + 1) * PAIR :]
                crossed = pltpu.roll(values, head_dim, 1)
                value_ref[rows, :PAIR] = jnp.where(first, values, crossed).astype(BF)
                value_ref[rows, PAIR:] = jnp.where(first, crossed, values).astype(BF)
            else:
                query_ref[rows, group * PAIR : (group + 1) * PAIR] = (
                    turned * (1.0 / math.sqrt(head_dim))
                ).astype(BF)
        return carry

    lax.fori_loop(0, row_length // BLOCK, project, 0)


def attend_kernel(
    head_dim, low_ref, query_ref, key_ref, value_ref, start_ref, usable_ref, mixed_ref
):
    row_length = query_ref.shape[0]
    query_groups = query_ref.shape[1] // PAIR

    def attend(first_row, first_key, window):
        bias = mask_bias(start_ref, usable_ref, first_row, first_key, BLOCK, window)
        rows = pl.ds(first_row, BLOCK)
        keys = pl.ds(first_key, window)
        for group in range(query_groups):
            pair = slice(group * PAIR, (group + 1) * PAIR)
            stacked = stacked_heads(query_ref[rows, pair], head_dim)
            grown = jnp.exp(mm_nt(stacked, key_ref[keys, pair]) + bias)
            share = grown * (1.0 / jnp.sum(grown, axis=-1, keepdims=True))
            mixed = mm(share.astype(BF), value_ref[keys, pair])
            mixed_ref[rows, pair] = side_by_side(mixed, head_dim).astype(BF)

    each_block(low_ref, row_length, attend)


def middle_kernel(
    place_ref,
    x0_ref,
    x1_ref,
    x2_ref,
    x3_ref,
    o0_ref,
    o1_ref,
    o2_ref,
    o3_ref,
    w0_ref,
    w1_ref,
    w2_ref,
    w3_ref,
    unit_ref,
    here_ref,
    sum_ref,
):
    place = place_ref[0]
    rows_each, width = x0_ref.shape
    heads = o0_ref.shape[1]
    columns = w0_ref.shape[1]
    chunk = 64
    for index, piece in enumerate((x0_ref, x1_ref, x2_ref, x3_ref)):
        base = pl.multiple_of((place ^ index) * rows_each, rows_each)
        rows = pl.ds(base, rows_each)
        for part, weight in enumerate((w0_ref, w1_ref, w2_ref, w3_ref)):
            total = None
            for other, mixed in enumerate((o0_ref, o1_ref, o2_ref, o3_ref)):
                features = pl.ds(pl.multiple_of((place ^ other) * heads, heads), heads)
                term = mm(mixed[rows, :], weight[features, :])
                total = term if total is None else total + term
            spot = pl.multiple_of((place ^ part) * columns, columns)
            sum_ref[:, pl.ds(spot, columns)] = total

        def normalize(step, carry, piece=piece, base=base, index=index):
            part = pl.ds(pl.multiple_of(step * chunk, chunk), chunk)
            values = sum_ref[part, :] + piece[part, :].astype(F32)
            if index == 0:
                here_ref[part, :] = values
            factor = lax.rsqrt(jnp.mean(values * values, axis=-1, keepdims=True) + EPS)
            target = pl.ds(pl.multiple_of(index * rows_each + step * chunk, chunk), chunk)
            unit_ref[target, :] = (values * factor).astype(BF)
            return carry

        lax.fori_loop(0, rows_each // chunk, normalize, 0)


def hidden_kernel(offset_ref, unit_ref, *rest):
    (*piece_refs, hidden_ref, gate_factor_ref, up_factor_ref, weight_ref, semaphore) = rest
    here = hidden_ref.shape[1]

    @pl.when(pl.program_id(0) == 0)
    def _():
        load_pieces(offset_ref, piece_refs, semaphore, (weight_ref, 0))()

    both = mm(unit_ref[...], weight_ref[...])
    gate = both[:, :here]
    up = both[:, here:]
    sig = 1.0 / (1.0 + jnp.exp(-gate))
    silu = gate * sig
    hidden_ref[...] = (silu * up).astype(BF)
    gate_factor_ref[...] = (up * sig * (1.0 + gate * (1.0 - sig))).astype(BF)
    up_factor_ref[...] = silu.astype(BF)


def hidden_grad_kernel(offset_ref, grad_ref, gate_factor_ref, up_factor_ref, *rest):
    (*piece_refs, both_ref, down_ref, semaphore) = rest
    here = gate_factor_ref.shape[1]

    @pl.when(pl.program_id(0) == 0)
    def _():
        load_pieces(offset_ref, piece_refs, semaphore, (down_ref, 0))()

    grad = mm_nt(grad_ref[...], down_ref[...])
    both_ref[:, :here] = (grad * gate_factor_ref[...].astype(F32)).astype(BF)
    both_ref[:, here:] = (grad * up_factor_ref[...].astype(F32)).astype(BF)


def split_kernel(transposed, order_ref, offset_ref, left_ref, *rest):
    (*piece_refs, keep_ref, send_ref, right_ref, semaphore) = rest

    @pl.when(pl.program_id(0) == 0)
    def _():
        load_pieces(offset_ref, piece_refs, semaphore, (right_ref, 0))()

    product = (mm_nt if transposed else mm)(left_ref[...], right_ref[...])

    @pl.when(pl.program_id(0) % 2 == 0)
    def _():
        keep_ref[...] = product

    @pl.when(pl.program_id(0) % 2 == 1)
    def _():
        send_ref[...] = product.astype(BF)


def output_grad_kernel(
    chunk_rows,
    place_ref,
    g0_ref,
    g1_ref,
    g2_ref,
    g3_ref,
    mixed_ref,
    w0_ref,
    w1_ref,
    w2_ref,
    w3_ref,
    grad_ref,
    terms_ref,
    total_ref,
):
    place = place_ref[0]
    rows_each = g0_ref.shape[0]
    heads = mixed_ref.shape[1]
    columns = w0_ref.shape[1]
    features = pl.ds(pl.multiple_of(place * heads, heads), heads)
    for index, grads in enumerate((g0_ref, g1_ref, g2_ref, g3_ref)):
        rows = pl.ds(pl.multiple_of((place ^ index) * rows_each, rows_each), rows_each)
        total = None
        for part, weight in enumerate((w0_ref, w1_ref, w2_ref, w3_ref)):
            spot = pl.ds(pl.multiple_of((place ^ part) * columns, columns), columns)
            term = mm_nt(grads[:, spot], weight[features, :])
            total = term if total is None else total + term
        grad_ref[rows, :] = total.astype(BF)
        term = mm_tn(mixed_ref[rows, :], grads[...])
        total_ref[...] = term if index == 0 else total_ref[...] + term
    sides = total_ref.shape[1] // terms_ref.shape[1]
    width = terms_ref.shape[1]
    chunks = terms_ref.shape[0] // sides // chunk_rows
    for step in range(chunks):
        for side in range(sides):
            start = (step * sides + side) * chunk_rows
            terms_ref[start : start + chunk_rows, :] = total_ref[
                step * chunk_rows : (step + 1) * chunk_rows, side * width : (side + 1) * width
            ]


def back_kernel(head_dim, last, low_ref, *refs):
    (start_ref, usable_ref, grad_ref, query_ref, key_ref, value_ref, raw_ref) = refs[:7]
    (cos_ref, sin_ref, gain_ref) = refs[7:10]
    if last:
        (other_grad_ref, other_terms_ref, other_key_ref, other_value_ref, key_raw_ref) = refs[10:15]
        (out_ref, terms_ref, key_sum_ref, value_sum_ref) = refs[15:]
        query_lanes = slice(PAIR, 2 * PAIR)
        out_ref[:, :PAIR] = other_grad_ref[...]
        terms_ref[...] = other_terms_ref[...]
    else:
        (out_ref, terms_ref, key_sum_ref, value_sum_ref) = refs[10:]
        query_lanes = slice(0, PAIR)
        terms_ref[...] = jnp.zeros_like(terms_ref)
    row_length = grad_ref.shape[0]
    scale = 1.0 / math.sqrt(head_dim)
    key_sum_ref[...] = jnp.zeros_like(key_sum_ref)
    value_sum_ref[...] = jnp.zeros_like(value_sum_ref)

    def through_norm(rows, values, grad, kind):
        grad = grad.astype(BF).astype(F32)
        turned = grad * cos_ref[rows, :] - half_partner(grad, head_dim) * sin_ref[rows, :]
        factor = lax.rsqrt(head_means(values * values, head_dim) + EPS)
        unit = values * factor
        terms_ref[kind : kind + 1, :] += jnp.sum(turned * unit, axis=0, keepdims=True)
        scaled = turned * gain_ref[kind : kind + 1, :]
        return (factor * (scaled - unit * head_means(scaled * unit, head_dim))).astype(BF)

    def attend(first_row, first_key, window):
        bias = mask_bias(start_ref, usable_ref, first_row, first_key, BLOCK, window)
        rows = pl.ds(first_row, BLOCK)
        keys = pl.ds(first_key, window)
        stacked = stacked_heads(query_ref[rows, :], head_dim)
        grads = stacked_heads(grad_ref[rows, :], head_dim)
        grown = jnp.exp(mm_nt(stacked, key_ref[keys, :]) + bias)
        share = grown * (1.0 / jnp.sum(grown, axis=-1, keepdims=True))
        grad_share = mm_nt(grads, value_ref[keys, :])
        centre = jnp.sum(share * grad_share, axis=-1, keepdims=True)
        grad_score = (share * (grad_share - centre)).astype(BF)
        grad_query = side_by_side(mm(grad_score, key_ref[keys, :]), head_dim) * scale
        key_sum_ref[keys, :] += mm_tn(grad_score, stacked)
        value_sum_ref[keys, :] += mm_tn(share.astype(BF), grads)
        out_ref[rows, query_lanes] = through_norm(rows, raw_ref[rows, :], grad_query, 0)

    each_block(low_ref, row_length, attend)
    if not last:
        return

    def folded(first_ref, second_ref, rows):
        first = first_ref[rows, :]
        second = second_ref[rows, :]
        return jnp.where(
            lanes(first.shape) < head_dim,
            first + pltpu.roll(first, head_dim, 1),
            second + pltpu.roll(second, head_dim, 1),
        )

    def finish(step, carry):
        rows = pl.ds(pl.multiple_of(step * BLOCK, BLOCK), BLOCK)
        grad = folded(other_key_ref, key_sum_ref, rows)
        out_ref[rows, 2 * PAIR : 3 * PAIR] = through_norm(rows, key_raw_ref[rows, :], grad, 1)
        out_ref[rows, 3 * PAIR :] = folded(other_value_ref, value_sum_ref, rows).astype(BF)
        return carry

    lax.fori_loop(0, row_length // BLOCK, finish, 0)


def attention_pack_kernel(
    place_ref,
    gain_ref,
    query_ref,
    key_ref,
    value_ref,
    output_ref,
    pack_ref,
    wide_ref,
    semaphore,
):
    gain = gain_ref[...].astype(BF).astype(F32)
    weights = (query_ref, key_ref, value_ref, output_ref)
    start = 0
    copies = []
    for index, weight_ref in enumerate(weights):
        size = weight_ref.shape[1] // SEQ
        column = pl.multiple_of(place_ref[0] * size, size)
        copies.append(
            pltpu.make_async_copy(
                weight_ref.at[:, pl.ds(column, size)],
                wide_ref.at[:, start : start + size],
                semaphore.at[index],
            )
        )
        copies[-1].start()
        start += size
    start = 0
    for index, weight_ref in enumerate(weights):
        size = weight_ref.shape[1] // SEQ
        copies[index].wait()
        values = wide_ref[:, start : start + size].astype(BF)
        if index < len(weights) - 1:
            values = (values.astype(F32) * gain).astype(BF)
        pack_ref[:, start : start + size] = values
        start += size


def hidden_pack_kernel(
    pieces, place_ref, gain_ref, gate_ref, up_ref, pack_ref, wide_ref, semaphore
):
    piece = gate_ref.shape[1] // (pieces * SEQ)
    here = pieces * piece
    chunk = 32
    steps = gate_ref.shape[0] // chunk
    weights = (gate_ref, up_ref)

    def copy(index, part):
        rows = slice(index * chunk, (index + 1) * chunk)
        return pltpu.make_async_copy(
            weights[part].at[rows, :], wide_ref.at[part, rows, :], semaphore.at[part, index]
        )

    for index in range(steps):
        for part in range(2):
            copy(index, part).start()
    for index in range(steps):
        for part in range(2):
            copy(index, part).wait()
            rows = slice(index * chunk, (index + 1) * chunk)
            gain = gain_ref[rows, :].astype(BF).astype(F32)
            for place in range(SEQ):

                @pl.when(place_ref[0] == place)
                def _(place=place):
                    joined = jnp.concatenate(
                        [
                            wide_ref[part, rows, start : start + piece]
                            for start in range(place * piece, gate_ref.shape[1], SEQ * piece)
                        ],
                        axis=1,
                    )
                    pack_ref[rows, part * here : (part + 1) * here] = (
                        joined.astype(BF).astype(F32) * gain
                    ).astype(BF)


def hidden_owner_kernel(
    pieces, place_ref, sums_ref, gate_ref, up_ref, gain_ref, gate_grad_ref, up_grad_ref, terms_ref
):
    seq_count = sums_ref.shape[0]
    here = sums_ref.shape[2] // 2
    piece = here // pieces
    gain = gain_ref[...].astype(BF).astype(F32)
    total = None
    for part, (weight_ref, grad_ref) in enumerate(
        ((gate_ref, gate_grad_ref), (up_ref, up_grad_ref))
    ):
        sums = [sums_ref[seq].astype(F32) for seq in range(seq_count)]
        joined = jnp.concatenate(
            [
                sums[seq][:, part * here + step * piece : part * here + (step + 1) * piece]
                for step in range(pieces)
                for seq in range(seq_count)
            ],
            axis=1,
        )
        term = row_sums(weight_ref[...].astype(BF).astype(F32) * joined)
        total = term if total is None else total + term
        grad_ref[...] = joined * gain
    terms_ref[...] = total


def attention_owner_kernel(
    place_ref,
    s0_ref,
    s1_ref,
    s2_ref,
    s3_ref,
    query_ref,
    key_ref,
    value_ref,
    gain_ref,
    query_grad_ref,
    key_grad_ref,
    value_grad_ref,
    terms_ref,
):
    place = place_ref[0]
    gain = gain_ref[...].astype(BF).astype(F32)
    pieces = (s0_ref, s1_ref, s2_ref, s3_ref)
    rows = query_ref.shape[0]
    start = 0
    total = None
    for weight_ref, grad_ref in (
        (query_ref, query_grad_ref),
        (key_ref, key_grad_ref),
        (value_ref, value_grad_ref),
    ):
        size = weight_ref.shape[1] // len(pieces)
        for index, sums in enumerate(pieces):
            columns = pl.ds(pl.multiple_of((place ^ index) * size, size), size)
            values = sums[:rows, start : start + size].astype(F32)
            weight = weight_ref[:, columns].astype(BF).astype(F32)
            term = row_sums(weight * values)
            total = term if total is None else total + term
            grad_ref[:, columns] = values * gain
        start += size
    terms_ref[...] = total


def row_sums(values):
    ones = jnp.ones((8, values.shape[1]), BF)
    high = values.astype(BF)
    rest = (values - high.astype(F32)).astype(BF)
    return (mm_nt(ones, high) + mm_nt(ones, rest))[:1]


def placed_call(kernel, results, place_array, operands, blocks, vmem, flops=0, moved=0):
    return pl.pallas_call(
        kernel,
        out_shape=[jax.ShapeDtypeStruct(shape, kind) for shape, kind in results],
        grid_spec=pltpu.PrefetchScalarGridSpec(
            num_scalar_prefetch=1,
            grid=(1,),
            in_specs=[pl.BlockSpec(shape, index) for shape, index in blocks],
            out_specs=[
                pl.BlockSpec(shape, lambda i, place, rank=len(shape): (0,) * rank)
                for shape, _ in results
            ],
        ),
        compiler_params=pltpu.CompilerParams(vmem_limit_bytes=vmem * MEGA),
        cost_estimate=pl.CostEstimate(flops=flops, bytes_accessed=moved, transcendentals=0),
    )(place_array, *operands)


def own_rows_block(i, place):
    return (place[0], 0)


def everything(i, place):
    return (0, 0)


def call(
    kernel, results, scalar_count, operands, vmem, pieces=(), scratch=(), flops=0, moved=0
):
    return pl.pallas_call(
        kernel,
        out_shape=[jax.ShapeDtypeStruct(shape, kind) for shape, kind in results],
        in_specs=scalars(scalar_count)
        + whole_vmem(len(operands) - scalar_count)
        + [pl.BlockSpec(memory_space=pltpu.HBM)] * len(pieces),
        out_specs=whole_vmem(len(results)),
        scratch_shapes=list(scratch),
        compiler_params=pltpu.CompilerParams(vmem_limit_bytes=vmem * MEGA),
        cost_estimate=pl.CostEstimate(flops=flops, bytes_accessed=moved, transcendentals=0),
    )(*operands, *pieces)


def block_call(kernel, results, scalar_arrays, operands, vmem, pieces, scratch, flops, moved):
    return pl.pallas_call(
        kernel,
        out_shape=[jax.ShapeDtypeStruct(shape, kind) for shape, kind, _, _ in results],
        grid_spec=pltpu.PrefetchScalarGridSpec(
            num_scalar_prefetch=len(scalar_arrays),
            grid=(4,),
            in_specs=[pl.BlockSpec(shape, index) for _, shape, index in operands]
            + [pl.BlockSpec(memory_space=pltpu.HBM)] * len(pieces),
            out_specs=[pl.BlockSpec(shape, index) for _, _, shape, index in results],
            scratch_shapes=list(scratch),
        ),
        compiler_params=pltpu.CompilerParams(vmem_limit_bytes=vmem * MEGA),
        cost_estimate=pl.CostEstimate(flops=flops, bytes_accessed=moved, transcendentals=0),
    )(*scalar_arrays, *(array for array, _, _ in operands), *pieces)


def row_block(step, *scalar_refs):
    return (step, 0)


def half_block(step, *scalar_refs):
    return (step // 2, 0)


def first_block(step, *scalar_refs):
    return (0, 0)


def ordered_block(step, order_ref, *scalar_refs):
    return (order_ref[step], 0)


def split_product(left, right_shape, offsets, pieces, transposed, order):
    rows = left.shape[0] // 4
    width = right_shape[0] if transposed else right_shape[1]
    return block_call(
        functools.partial(split_kernel, transposed),
        [
            ((2 * rows, width), F32, (rows, width), half_block),
            ((2 * rows, width), BF, (rows, width), half_block),
        ],
        (order, offsets),
        [(left, (rows, left.shape[1]), ordered_block)],
        20,
        pieces,
        [pltpu.VMEM(right_shape, BF), pltpu.SemaphoreType.DMA((1, len(pieces)))],
        2 * left.shape[0] * left.shape[1] * width,
        2 * (left.size + right_shape[0] * right_shape[1]) + 6 * left.shape[0] * width,
    )


def swap(values, bit):
    count = lax.axis_size("seq")
    return lax.ppermute(values, "seq", [(i, i ^ bit) for i in range(count)])


def seq_pieces(values):
    far = swap(values, 2)
    near = swap(values, 1)
    return (values, near, far, swap(far, 1))


def after(values, *others):
    return lax.optimization_barrier((values, others))[0]


def ring_length():
    count = lax.axis_size("dp")
    return count if count % 2 == 0 and 4 <= count <= 8 else 0


def ring_order(count):
    return list(range(0, count, 2)) + list(range(count - 1, 0, -2))


def ring_sources(offsets):
    count = lax.axis_size("dp")
    place = lax.axis_index("dp")
    spot = jnp.where(place % 2 == 0, place // 2, count - 1 - place // 2)
    spot = (spot + jnp.asarray(offsets, jnp.int32) + count) % count
    return jnp.where(spot < count // 2, 2 * spot, 2 * (count - 1 - spot) + 1)


def ring_source(offset):
    count = lax.axis_size("dp")
    place = lax.axis_index("dp")
    spot = jnp.where(place % 2 == 0, place // 2, count - 1 - place // 2)
    spot = (spot + offset + count) % count
    return jnp.where(spot < count // 2, 2 * spot, 2 * (count - 1 - spot) + 1)


def ring_move(values, step):
    count = lax.axis_size("dp")
    order = ring_order(count)
    return lax.ppermute(
        values, "dp", [(order[i], order[(i + step) % count]) for i in range(count)]
    )


def half_of(rows):
    return rows // 32 * 16 or rows // 2


class GatherRing:
    def __init__(self, shard):
        self.count = ring_length()
        if not self.count:
            self.pieces = [lax.all_gather(shard, "dp", axis=0, tiled=True)]
            self.offsets = jnp.zeros((1,), jnp.int32)
            self.steps = 0
            return
        self.pieces = [shard]
        self.up = self.down = shard
        self.steps = self.count // 2
        self.taken = 0
        rows = shard.shape[0]
        steps = [0]
        for step in range(1, self.steps):
            steps += [-step, step]
        steps += [self.steps, self.steps]
        extra = [0] * (len(steps) - 1) + [half_of(rows)]
        self.offsets = ring_sources(steps) * rows + jnp.asarray(extra, jnp.int32)

    def step(self, *others):
        if not self.steps:
            return others
        self.up, self.down, others = lax.optimization_barrier((self.up, self.down, others))
        self.taken += 1
        half = half_of(self.up.shape[0])
        if self.taken == self.steps:
            self.up, self.down = (self.up[:half], self.down[half:])
        self.sent = (self.up, self.down)
        self.up = ring_move(self.up, 1)
        self.down = ring_move(self.down, -1)
        self.pieces += [self.up, self.down]
        return others

    def arrived(self):
        return (self.up, self.down) if self.steps else ()


class ScatterRing:
    def __init__(self, terms, shared=None):
        self.count = ring_length()
        self.terms = terms
        self.shared = shared
        if not self.count:
            size = lax.axis_size("dp")
            parts = [term.reshape(size, -1, term.shape[1]) for term in terms]
            if shared is not None:
                parts.append(jnp.broadcast_to(shared, (size, *shared.shape)))
            whole = self.joined(parts)
            self.sums = lax.psum_scatter(
                whole.reshape(-1, whole.shape[-1]).astype(BF), "dp", scatter_dimension=0, tiled=True
            ).astype(F32)
            self.steps = 0
            self.sent = ()
            return
        self.steps = self.count // 2
        self.taken = 0
        self.sent = ()

    def joined(self, parts):
        return parts[0] if len(parts) == 1 else jnp.concatenate(parts, axis=-2)

    def term(self, offset):
        parts = []
        for term in self.terms:
            rows = term.shape[0] // self.count
            parts.append(lax.dynamic_slice_in_dim(term, ring_source(offset) * rows, rows, 0))
        if self.shared is not None:
            parts.append(self.shared)
        return self.joined(parts)

    def step(self, *others):
        if not self.steps:
            return others
        self.taken += 1
        if self.taken == 1:
            self.terms, others = lax.optimization_barrier((self.terms, others))
            far = self.term(self.steps)
            half = half_of(far.shape[0])
            up, down = (far[:half], far[half:])
        else:
            self.up, self.down, others = lax.optimization_barrier((self.up, self.down, others))
            left = self.steps + 1 - self.taken
            up, down = (self.term(left), self.term(-left))
            if self.taken == 2:
                half = self.up.shape[0]
                up = jnp.concatenate([up[:half] + self.up.astype(F32), up[half:]])
                down = jnp.concatenate([down[:half], down[half:] + self.down.astype(F32)])
            else:
                up = up + self.up.astype(F32)
                down = down + self.down.astype(F32)
        self.sent = (up.astype(BF), down.astype(BF))
        self.up = ring_move(self.sent[0], 1)
        self.down = ring_move(self.sent[1], -1)
        return others

    def arrived(self):
        return (self.up, self.down) if self.steps else ()

    def result(self):
        if not self.steps:
            return self.sums
        return self.term(0) + self.up.astype(F32) + self.down.astype(F32)


def local(
    tokens,
    segments,
    valid_mask,
    attention_gain,
    query_weight,
    key_weight,
    value_weight,
    query_gain,
    key_gain,
    output_weight,
    feedforward_gain,
    gate_weight,
    up_weight,
    down_weight,
    cotangent,
):
    seq_count = lax.axis_size("seq")
    dp_count = lax.axis_size("dp")
    place = lax.axis_index("seq")
    local_rows = tokens.shape[1]
    row_length = segments.shape[1]
    head_dim = query_gain.shape[0]
    width = tokens.shape[2]
    hidden_width = gate_weight.shape[1]
    query_width = query_weight.shape[1]
    key_width = key_weight.shape[1]
    query_here = query_width // seq_count
    key_here = key_width // seq_count
    hidden_here = hidden_width // seq_count
    weight_rows = query_weight.shape[0]
    own_rows = weight_rows // seq_count
    segment_row = segments[0]
    valid_row = valid_mask[0]

    def low(weight):
        return weight.astype(BF).astype(F32)

    place_array = place.astype(jnp.int32).reshape(1)
    gain_one = attention_gain[:, None]
    gain_two = feedforward_gain[:, None]
    qkv_width = query_here + 2 * key_here
    piece = hidden_width // (dp_count * seq_count)
    kernels_fit = weight_rows % 32 == 0 and own_rows % 8 == 0 and dp_count <= 8

    pack_width = qkv_width + width // seq_count
    (attention_pack,) = call(
        attention_pack_kernel,
        [((weight_rows, pack_width), BF)],
        1,
        (place_array, gain_one),
        4,
        pieces=(query_weight, key_weight, value_weight, output_weight),
        scratch=[pltpu.VMEM((weight_rows, pack_width), F32), pltpu.SemaphoreType.DMA((4,))],
        moved=8 * weight_rows * width,
    )
    if kernels_fit:
        (gate_up_pack,) = call(
            functools.partial(hidden_pack_kernel, dp_count),
            [((weight_rows, 2 * hidden_here), BF)],
            1,
            (place_array, after(gain_two, attention_pack)),
            14,
            pieces=(gate_weight, up_weight),
            scratch=[
                pltpu.VMEM((2, weight_rows, hidden_width), F32),
                pltpu.SemaphoreType.DMA((2, weight_rows // 32)),
            ],
            moved=8 * weight_rows * hidden_width,
        )
    else:

        def hidden_columns(weight):
            split = weight.reshape(weight_rows, dp_count, seq_count, piece)
            mine = lax.dynamic_index_in_dim(split, place, 2, keepdims=False)
            return (low(mine.reshape(weight_rows, hidden_here)) * low(gain_two)).astype(BF)

        gate_up_pack = jnp.concatenate(
            [hidden_columns(gate_weight), hidden_columns(up_weight)], axis=1
        )
    down_pack = lax.dynamic_slice_in_dim(down_weight, place * piece, piece, 0).astype(BF)
    down_pack = after(down_pack, attention_pack)

    order = place ^ jnp.arange(4, dtype=jnp.int32)
    plain = jnp.arange(4, dtype=jnp.int32)

    token_far = swap(tokens[0], 2)
    token_near = swap(tokens[0], 1)
    attention_ring = GatherRing(attention_pack)
    attention_ring.step()
    positions = doc_positions(segment_row)
    starts = jnp.arange(row_length, dtype=jnp.int32) - positions
    cos_wide, sin_wide = rope_tables(positions, head_dim)
    repeats = PAIR // head_dim
    head_gains = jnp.tile(jnp.stack([query_gain, key_gain]), (1, repeats))
    row_starts = starts[:, None]
    usable = valid_row[None, :]
    starts, row_starts, head_gains = attention_ring.step(starts, row_starts, head_gains)
    block_lows = starts[::BLOCK]
    cos_wide, sin_wide = attention_ring.step(cos_wide, sin_wide)
    token_far, gate_up_pack = attention_ring.step(token_far, gate_up_pack)
    token_pieces = (tokens[0], token_near, token_far, swap(token_far, 1))
    grad_far = swap(after(cotangent[0], token_far), 2)
    grad_near = swap(after(cotangent[0], token_far), 1)

    gate_up_ring = GatherRing(after(gate_up_pack, attention_ring.arrived()))
    gate_up_ring.step()
    projected = call(
        functools.partial(project_kernel, head_dim),
        [
            ((row_length, width), BF),
            ((row_length, query_here + key_here), F32),
            ((row_length, query_here), BF),
            ((row_length, 2 * key_here), BF),
            ((row_length, 2 * key_here), BF),
            ((width, qkv_width), BF),
            ((query_width, width // seq_count), BF),
        ],
        2,
        (place_array, attention_ring.offsets, *token_pieces, cos_wide, sin_wide, head_gains),
        24,
        pieces=attention_ring.pieces,
        scratch=[pltpu.SemaphoreType.DMA((2, len(attention_ring.pieces)))],
        flops=2 * row_length * width * qkv_width,
        moved=12 * row_length * width,
    )
    projected, grad_far = gate_up_ring.step(projected, grad_far)
    unit_one, raw, queries, keys_two, values_two, qkv_weight, output_columns = projected
    grad_row_pieces = (cotangent[0], grad_near, grad_far, swap(grad_far, 1))
    output_far = swap(output_columns, 2)
    output_near = swap(output_columns, 1)
    (mixed_here,) = call(
        functools.partial(attend_kernel, head_dim),
        [((row_length, query_here), BF)],
        1,
        (block_lows, queries, keys_two, values_two, row_starts, usable),
        12,
        flops=row_length * width * qkv_width,
        moved=4 * row_length * width,
    )
    mixed_here, output_far = gate_up_ring.step(mixed_here, output_far)
    output_pieces = (output_columns, output_near, output_far, swap(output_far, 1))
    mixed_far = swap(mixed_here, 2)
    mixed_near = swap(mixed_here, 1)
    (mixed_far,) = gate_up_ring.step(mixed_far)
    down_ring = GatherRing(after(down_pack, mixed_far))
    down_ring.step()
    mixed_pieces = (mixed_here, mixed_near, mixed_far, swap(mixed_far, 1))
    unit_two, after_here = call(
        middle_kernel,
        [((row_length, width), BF), ((local_rows, width), F32)],
        1,
        (place_array, *token_pieces, *mixed_pieces, *output_pieces),
        18,
        scratch=[pltpu.VMEM((local_rows, width), F32)],
        flops=2 * row_length * width * width,
        moved=10 * row_length * width,
    )
    (unit_two,) = down_ring.step(unit_two)

    rows_each = row_length // 4
    hidden, gate_factor, up_factor = block_call(
        hidden_kernel,
        [((row_length, hidden_here), BF, (rows_each, hidden_here), row_block)] * 3,
        (gate_up_ring.offsets,),
        [(unit_two, (rows_each, width), row_block)],
        28,
        gate_up_ring.pieces,
        [
            pltpu.VMEM((width, 2 * hidden_here), BF),
            pltpu.SemaphoreType.DMA((1, len(gate_up_ring.pieces))),
        ],
        4 * row_length * width * hidden_here,
        8 * row_length * hidden_here + 4 * width * hidden_here,
    )
    hidden, gate_factor, up_factor = down_ring.step(hidden, gate_factor, up_factor)
    grad_rows = jnp.concatenate(grad_row_pieces)
    down_scatter = ScatterRing([mm_tn(hidden, grad_rows)])
    (down_scatter.terms,) = down_ring.step(down_scatter.terms)
    down_scatter.step()
    gate_up_grad, down_all = block_call(
        hidden_grad_kernel,
        [
            ((row_length, 2 * hidden_here), BF, (rows_each, 2 * hidden_here), row_block),
            ((hidden_here, width), BF, (hidden_here, width), first_block),
        ],
        (down_ring.offsets,),
        [
            (grad_rows, (rows_each, width), row_block),
            (gate_factor, (rows_each, hidden_here), row_block),
            (up_factor, (rows_each, hidden_here), row_block),
        ],
        24,
        down_ring.pieces,
        [pltpu.SemaphoreType.DMA((1, len(down_ring.pieces)))],
        2 * row_length * width * hidden_here,
        8 * row_length * hidden_here + 4 * width * hidden_here,
    )

    (gate_up_grad,) = down_scatter.step(gate_up_grad)
    keep, send = split_product(
        gate_up_grad, (width, 2 * hidden_here), gate_up_ring.offsets, gate_up_ring.pieces, True, plain
    )
    keep, send = down_scatter.step(keep, send)

    def halves(keep, near):
        pair = keep + near.astype(F32)
        return (pair[:local_rows], pair[local_rows:].astype(BF))

    half_sum, half_send = halves(keep, swap(send, 1))
    half_sum, half_send, unit_two = lax.optimization_barrier((half_sum, half_send, unit_two))
    arrived = swap(half_send, 2)
    gate_up_scatter = ScatterRing([mm_tn(unit_two, gate_up_grad).astype(BF)])
    (gate_up_scatter.terms,) = down_scatter.step(gate_up_scatter.terms)
    gate_up_scatter.step()
    unit_here, factor_here = rms_stats(after_here)
    grad_after = cotangent[0].astype(F32) + rms_back(
        half_sum + arrived.astype(F32), unit_here, factor_here
    )
    branch = grad_after.astype(BF)
    branch_far = swap(branch, 2)
    branch_near = swap(branch, 1)
    keep, send = split_product(
        after(hidden, branch, gate_up_scatter.sent),
        (hidden_here, width),
        jnp.zeros((1,), jnp.int32),
        [down_all],
        False,
        plain,
    )
    keep, send, branch_far = gate_up_scatter.step(keep, send, branch_far)
    branch_pieces = (branch, branch_near, branch_far, swap(branch_far, 1))
    half_sum, half_send = halves(keep, swap(send, 1))
    chunk_rows = query_width // (dp_count * seq_count)
    grad_mixed, output_terms = call(
        functools.partial(output_grad_kernel, chunk_rows),
        [
            ((row_length, query_here), BF),
            ((query_here * width // qkv_width, qkv_width), F32),
        ],
        1,
        (place_array, *branch_pieces, mixed_here, *output_pieces),
        14,
        scratch=[pltpu.VMEM((query_here, width), F32)],
        flops=4 * row_length * width * query_here,
        moved=8 * row_length * width,
    )

    def back(group, grad_mixed, others):
        last = group == query_here // PAIR - 1
        column = (row_length, PAIR)
        here = pl.BlockSpec(column, lambda i, low_ref: (0, group))
        first = pl.BlockSpec(column, lambda i, low_ref: (0, 0))
        whole = pl.BlockSpec(memory_space=pltpu.VMEM)
        operands = [row_starts, usable, grad_mixed, queries, keys_two, values_two, raw]
        operands += [cos_wide, sin_wide, head_gains, *others]
        specs = [whole] * 2 + [here] * 5 + [first] * 2 + [whole] * (1 + len(others))
        results = [(column, BF), ((8, PAIR), F32)] + [(column, F32)] * 2
        scratch = []
        if last:
            operands.append(raw)
            specs.append(pl.BlockSpec(column, lambda i, low_ref: (0, query_here // PAIR)))
            scratch = [pltpu.VMEM(shape, kind) for shape, kind in results[2:]]
            results = [((row_length, qkv_width), BF), results[1]]
        return pl.pallas_call(
            functools.partial(back_kernel, head_dim, last),
            out_shape=[jax.ShapeDtypeStruct(shape, kind) for shape, kind in results],
            grid_spec=pltpu.PrefetchScalarGridSpec(
                num_scalar_prefetch=1,
                grid=(1,),
                in_specs=specs,
                out_specs=[pl.BlockSpec(shape, lambda i, low_ref: (0, 0)) for shape, _ in results],
                scratch_shapes=scratch,
            ),
            compiler_params=pltpu.CompilerParams(vmem_limit_bytes=20 * MEGA),
            cost_estimate=pl.CostEstimate(
                flops=2 * row_length * width * qkv_width,
                bytes_accessed=6 * row_length * width,
                transcendentals=0,
            ),
        )(block_lows, *operands)

    others = back(0, grad_mixed, ())
    *others, grad_mixed = gate_up_scatter.step(*others, grad_mixed)
    half_sum, half_send = (half_sum, after(half_send, gate_up_scatter.sent))
    layer_out = (after_here + half_sum + swap(half_send, 2).astype(F32)).astype(BF)
    qkv_grad, gain_terms = back(1, grad_mixed, tuple(others))
    qkv_grad, gain_terms = gate_up_scatter.step(qkv_grad, gain_terms)
    gain_rows = jnp.concatenate([gain_terms[0:1], gain_terms[1:2]], axis=1)
    gain_rows = jnp.pad(gain_rows, ((0, 15), (0, qkv_width - 2 * PAIR)))
    attention_scatter = ScatterRing([mm_tn(unit_one, qkv_grad), output_terms], gain_rows)
    attention_scatter.step()
    keep, send = split_product(
        after(qkv_grad, attention_scatter.sent),
        (width, qkv_width),
        jnp.zeros((1,), jnp.int32),
        [qkv_weight],
        True,
        order,
    )
    keep, send = attention_scatter.step(keep, send)
    half_sum, half_send = halves(keep, swap(send, 1))
    half_sum, half_send = attention_scatter.step(half_sum, half_send)
    arrived = swap(half_send, 2)
    for _ in range(attention_scatter.steps - 3):
        attention_scatter.step()
    unit_tokens, factor_tokens = rms_stats(tokens[0].astype(F32))
    token_grad = (
        grad_after + rms_back(half_sum + arrived.astype(F32), unit_tokens, factor_tokens)
    ).astype(BF)

    down_sums = down_scatter.result()
    gate_up_sums = gate_up_scatter.result().astype(BF)
    attention_sums = attention_scatter.result().astype(BF)
    qkv_sums = attention_sums[:weight_rows]
    output_sums = jnp.concatenate(
        [
            attention_sums[weight_rows + part * chunk_rows : weight_rows + (part + 1) * chunk_rows]
            for part in range(width // qkv_width)
        ],
        axis=1,
    )

    def own(weight):
        return lax.dynamic_slice_in_dim(weight, place * own_rows, own_rows, 0)

    hidden_own = lax.all_to_all(
        gate_up_sums.reshape(seq_count, own_rows, -1), "seq", split_axis=0, concat_axis=0, tiled=True
    )
    gain_row = attention_sums[-16:]
    qkv_pieces = []
    for bits in range(4):
        part = lax.dynamic_slice_in_dim(qkv_sums, (place ^ bits) * own_rows, own_rows, 0)
        part = jnp.concatenate([part, gain_row])
        qkv_pieces.append(swap(part, bits) if bits else part)
    gain_sums = sum(piece[own_rows : own_rows + 1].astype(F32) for piece in qkv_pieces)
    gain_sums = jnp.sum(gain_sums[0, : 2 * PAIR].reshape(2, repeats, head_dim), axis=1)
    if kernels_fit:
        gate_grad, up_grad, feed_gain_grad = placed_call(
            functools.partial(hidden_owner_kernel, dp_count),
            [((own_rows, hidden_width), F32)] * 2 + [((1, own_rows), F32)],
            place_array,
            (hidden_own, gate_weight, up_weight, gain_two),
            [
                (hidden_own.shape, lambda i, place: (0, 0, 0)),
                ((own_rows, hidden_width), own_rows_block),
                ((own_rows, hidden_width), own_rows_block),
                ((own_rows, 1), own_rows_block),
            ],
            16,
            moved=20 * own_rows * hidden_width,
        )
        query_grad, key_grad, value_grad, attention_gain_grad = placed_call(
            attention_owner_kernel,
            [((own_rows, query_width), F32)]
            + [((own_rows, key_width), F32)] * 2
            + [((1, own_rows), F32)],
            place_array,
            (*qkv_pieces, query_weight, key_weight, value_weight, gain_one),
            [((own_rows + 16, qkv_width), everything)] * 4
            + [
                ((own_rows, query_width), own_rows_block),
                ((own_rows, key_width), own_rows_block),
                ((own_rows, key_width), own_rows_block),
                ((own_rows, 1), own_rows_block),
            ],
            6,
            moved=20 * own_rows * query_width,
        )
    else:
        spread = jnp.stack(qkv_pieces)[order, :own_rows].astype(F32)

        def joined(first, size):
            return jnp.swapaxes(spread[:, :, first : first + size], 0, 1).reshape(own_rows, -1)

        query_own = joined(0, query_here)
        key_own = joined(query_here, key_here)
        value_own = joined(query_here + key_here, key_here)
        attention_gain_grad = (
            jnp.sum(own(low(query_weight)) * query_own, axis=1)
            + jnp.sum(own(low(key_weight)) * key_own, axis=1)
            + jnp.sum(own(low(value_weight)) * value_own, axis=1)
        )
        gain_own = own(low(gain_one))
        query_grad, key_grad, value_grad = (
            query_own * gain_own,
            key_own * gain_own,
            value_own * gain_own,
        )
        hidden_own = hidden_own.reshape(seq_count, own_rows, 2, dp_count, piece)
        hidden_own = jnp.transpose(hidden_own, (2, 1, 3, 0, 4))
        hidden_own = hidden_own.reshape(2, own_rows, hidden_width).astype(F32)
        feed_gain_grad = jnp.sum(own(low(gate_weight)) * hidden_own[0], axis=1) + jnp.sum(
            own(low(up_weight)) * hidden_own[1], axis=1
        )
        gain_own = own(low(gain_two))
        gate_grad, up_grad = (hidden_own[0] * gain_own, hidden_own[1] * gain_own)

    moves = [
        (dp * seq_count + seq, seq * dp_count + dp)
        for dp in range(dp_count)
        for seq in range(seq_count)
    ]
    output_own = lax.ppermute(output_sums, ("dp", "seq"), moves).astype(F32)

    return (
        layer_out.reshape(1, local_rows, -1),
        token_grad.reshape(1, local_rows, -1),
        attention_gain_grad.reshape(own_rows),
        query_grad,
        key_grad,
        value_grad,
        gain_sums[0],
        gain_sums[1],
        output_own,
        feed_gain_grad.reshape(own_rows),
        gate_grad,
        up_grad,
        down_sums,
    )


def solution(mesh):
    in_specs = (
        P("dp", "seq", None),
        P("dp", None),
        P("dp", None),
        P("dp"),
        P("dp", None),
        P("dp", None),
        P("dp", None),
        P(),
        P(),
        P("dp", None),
        P("dp"),
        P("dp", None),
        P("dp", None),
        P("dp", None),
        P("dp", "seq", None),
    )
    out_specs = (
        P("dp", "seq", None),
        P("dp", "seq", None),
        P(("dp", "seq")),
        P(("dp", "seq"), None),
        P(("dp", "seq"), None),
        P(("dp", "seq"), None),
        P(),
        P(),
        P(("dp", "seq"), None),
        P(("dp", "seq")),
        P(("dp", "seq"), None),
        P(("dp", "seq"), None),
        P(("dp", "seq"), None),
    )
    return jax.shard_map(local, mesh=mesh, in_specs=in_specs, out_specs=out_specs, check_vma=False)
```

```python
import functools
import math

import jax
import jax.numpy as jnp
from jax import lax
from jax.experimental import pallas as pl
from jax.experimental.pallas import tpu as pltpu
from jax.sharding import PartitionSpec as P

EPS = 1e-05
ROPE_BASE = 1000000.0
NEG_FILL = -1e30
BF = jnp.bfloat16
F32 = jnp.float32
BLOCK = 128
PAIR = 128
SEQ = 4
MEGA = 1024 * 1024


def dot(left, right, dims):
    return lax.dot_general(left, right, (dims, ((), ())), preferred_element_type=F32)


def mm(left, right):
    return dot(left, right, ((1,), (0,)))


def mm_nt(left, right):
    return dot(left, right, ((1,), (1,)))


def mm_tn(left, right):
    return dot(left, right, ((0,), (0,)))


def rms_stats(values):
    factor = lax.rsqrt(jnp.mean(values * values, axis=-1, keepdims=True) + EPS)
    return (values * factor, factor)


def rms_back(grad_unit, unit_values, factor):
    return factor * (
        grad_unit - unit_values * jnp.mean(grad_unit * unit_values, axis=-1, keepdims=True)
    )


def doc_positions(segment_row):
    length = segment_row.shape[0]
    places = jnp.arange(length, dtype=jnp.int32)
    change = jnp.concatenate([jnp.ones((1,), dtype=jnp.bool_), segment_row[1:] != segment_row[:-1]])
    starts = lax.cummax(jnp.where(change, places, jnp.zeros_like(places)), axis=0)
    return places - starts


def rope_tables(positions, head_dim):
    half = head_dim // 2
    lane = jnp.arange(PAIR, dtype=jnp.int32)
    frequency = ROPE_BASE ** (-(lane % half).astype(F32) / half)
    angles = positions.astype(F32)[:, None] * frequency[None, :]
    sign = jnp.where(lane % head_dim < half, -1.0, 1.0)
    return (jnp.cos(angles), jnp.sin(angles) * sign[None, :])


def whole_vmem(count):
    return [pl.BlockSpec(memory_space=pltpu.VMEM)] * count


def scalars(count):
    return [pl.BlockSpec(memory_space=pltpu.SMEM)] * count


def lanes(shape):
    return lax.broadcasted_iota(jnp.int32, shape, 1)


def head_means(values, head_dim):
    width = values.shape[1]
    row = lax.broadcasted_iota(jnp.int32, (width, width), 0) // head_dim
    column = lax.broadcasted_iota(jnp.int32, (width, width), 1) // head_dim
    spread = jnp.where(row == column, 1.0 / head_dim, 0.0).astype(BF)
    high = values.astype(BF)
    rest = (values - high.astype(F32)).astype(BF)
    return mm(high, spread) + mm(rest, spread)


def half_partner(values, head_dim):
    half = head_dim // 2
    width = values.shape[1]
    upper = (lanes(values.shape) % head_dim) >= half
    return jnp.where(
        upper, pltpu.roll(values, half, 1), pltpu.roll(values, width - half, 1)
    )


def stacked_heads(pair, head_dim):
    first = lanes(pair.shape) < head_dim
    zero = jnp.zeros_like(pair)
    return jnp.concatenate([jnp.where(first, pair, zero), jnp.where(first, zero, pair)], axis=0)


def side_by_side(stacked, head_dim):
    rows = stacked.shape[0] // 2
    return jnp.where(
        lanes((rows, stacked.shape[1])) < head_dim, stacked[:rows], stacked[rows:]
    )


def mask_bias(start_ref, usable_ref, first_row, first_key, rows, window):
    row = first_row + lax.broadcasted_iota(jnp.int32, (rows, window), 0)
    key = first_key + lax.broadcasted_iota(jnp.int32, (rows, window), 1)
    start = start_ref[pl.ds(first_row, rows), :]
    usable = usable_ref[:, pl.ds(first_key, window)] > 0
    allowed = ((key >= start) & (key <= row) & usable) | (key == row)
    bias = jnp.where(allowed, 0.0, NEG_FILL)
    return jnp.concatenate([bias, bias], axis=0)


def each_block(low_ref, row_length, body):
    long_window = min(5 * BLOCK, row_length)

    def step(index, carry):
        first_row = pl.multiple_of(index * BLOCK, BLOCK)
        short_key = jnp.maximum(first_row - BLOCK, 0)
        is_short = low_ref[index] >= short_key

        @pl.when(is_short)
        def _():
            body(first_row, pl.multiple_of(short_key, BLOCK), 2 * BLOCK)

        @pl.when(jnp.logical_not(is_short))
        def _():
            long_key = jnp.maximum(first_row + BLOCK - long_window, 0)
            body(first_row, pl.multiple_of(long_key, BLOCK), long_window)

        return carry

    lax.fori_loop(0, row_length // BLOCK, step, 0)


def load_pieces(offset_ref, piece_refs, semaphore, *targets):
    copies = []
    for index, piece in enumerate(piece_refs):
        start = pl.multiple_of(offset_ref[index], 16)
        for part, (target, column) in enumerate(targets):
            rows = pl.ds(start, piece.shape[0])
            copies.append(
                pltpu.make_async_copy(
                    piece.at[:, column : column + target.shape[1]],
                    target.at[rows, :],
                    semaphore.at[part, index],
                )
            )
    for copy in copies:
        copy.start()

    def wait():
        for copy in copies:
            copy.wait()

    return wait


def columns_kernel(column, offset_ref, *rest):
    (*piece_refs, out_ref, semaphore) = rest
    load_pieces(offset_ref, piece_refs, semaphore, (out_ref, column))()


def project_kernel(
    head_dim,
    place_ref,
    offset_ref,
    x0_ref,
    x1_ref,
    x2_ref,
    x3_ref,
    cos_ref,
    sin_ref,
    gain_ref,
    *rest,
):
    (*piece_refs, unit_ref, raw_ref, query_ref, key_ref, value_ref, weight_ref) = rest[:-1]
    semaphore = rest[-1]
    wait = load_pieces(offset_ref, piece_refs, semaphore, (weight_ref, 0))
    place = place_ref[0]
    rows_each = x0_ref.shape[0]
    row_length = unit_ref.shape[0]
    query_groups = query_ref.shape[1] // PAIR
    for index, piece in enumerate((x0_ref, x1_ref, x2_ref, x3_ref)):
        values = piece[...].astype(F32)
        factor = lax.rsqrt(jnp.mean(values * values, axis=-1, keepdims=True) + EPS)
        rows = pl.ds(pl.multiple_of((place ^ index) * rows_each, rows_each), rows_each)
        unit_ref[rows, :] = (values * factor).astype(BF)
    wait()

    def project(step, carry):
        rows = pl.ds(pl.multiple_of(step * rows_each, rows_each), rows_each)
        raw = mm(unit_ref[rows, :], weight_ref[...])
        raw_ref[rows, :] = raw[:, : raw_ref.shape[1]]
        cos = cos_ref[rows, :]
        sin = sin_ref[rows, :]
        for group in range(query_groups + 1):
            is_key = group == query_groups
            values = raw[:, group * PAIR : (group + 1) * PAIR]
            factor = lax.rsqrt(head_means(values * values, head_dim) + EPS)
            scaled = values * factor * gain_ref[int(is_key) : int(is_key) + 1, :]
            turned = scaled * cos + half_partner(scaled, head_dim) * sin
            if is_key:
                crossed = pltpu.roll(turned, head_dim, 1)
                first = lanes(turned.shape) < head_dim
                key_ref[rows, :PAIR] = jnp.where(first, turned, crossed).astype(BF)
                key_ref[rows, PAIR:] = jnp.where(first, crossed, turned).astype(BF)
                values = raw[:, (group + 1) * PAIR :]
                crossed = pltpu.roll(values, head_dim, 1)
                value_ref[rows, :PAIR] = jnp.where(first, values, crossed).astype(BF)
                value_ref[rows, PAIR:] = jnp.where(first, crossed, values).astype(BF)
            else:
                query_ref[rows, group * PAIR : (group + 1) * PAIR] = (
                    turned * (1.0 / math.sqrt(head_dim))
                ).astype(BF)
        return carry

    lax.fori_loop(0, row_length // rows_each, project, 0)


def attend_kernel(
    head_dim, low_ref, query_ref, key_ref, value_ref, start_ref, usable_ref, mixed_ref
):
    row_length = query_ref.shape[0]
    query_groups = query_ref.shape[1] // PAIR

    def attend(first_row, first_key, window):
        bias = mask_bias(start_ref, usable_ref, first_row, first_key, BLOCK, window)
        rows = pl.ds(first_row, BLOCK)
        keys = pl.ds(first_key, window)
        for group in range(query_groups):
            pair = slice(group * PAIR, (group + 1) * PAIR)
            stacked = stacked_heads(query_ref[rows, pair], head_dim)
            grown = jnp.exp(mm_nt(stacked, key_ref[keys, pair]) + bias)
            mixed = mm(grown.astype(BF), value_ref[keys, pair])
            mixed = mixed * (1.0 / jnp.sum(grown, axis=-1, keepdims=True))
            mixed_ref[rows, pair] = side_by_side(mixed, head_dim).astype(BF)

    each_block(low_ref, row_length, attend)


def middle_kernel(
    place_ref,
    x0_ref,
    x1_ref,
    x2_ref,
    x3_ref,
    o0_ref,
    o1_ref,
    o2_ref,
    o3_ref,
    w0_ref,
    w1_ref,
    w2_ref,
    w3_ref,
    unit_ref,
    here_ref,
    sum_ref,
):
    place = place_ref[0]
    rows_each, width = x0_ref.shape
    heads = o0_ref.shape[1]
    columns = w0_ref.shape[1]
    for index, piece in enumerate((x0_ref, x1_ref, x2_ref, x3_ref)):
        base = pl.multiple_of((place ^ index) * rows_each, rows_each)
        rows = pl.ds(base, rows_each)
        for part, weight in enumerate((w0_ref, w1_ref, w2_ref, w3_ref)):
            total = None
            for other, mixed in enumerate((o0_ref, o1_ref, o2_ref, o3_ref)):
                features = pl.ds(pl.multiple_of((place ^ other) * heads, heads), heads)
                term = mm(mixed[rows, :], weight[features, :])
                total = term if total is None else total + term
            spot = pl.multiple_of((place ^ part) * columns, columns)
            sum_ref[:, pl.ds(spot, columns)] = total

        values = sum_ref[...] + piece[...].astype(F32)
        if index == 0:
            here_ref[...] = values
        factor = lax.rsqrt(jnp.mean(values * values, axis=-1, keepdims=True) + EPS)
        unit_ref[index * rows_each : (index + 1) * rows_each, :] = (values * factor).astype(BF)


def hidden_kernel(offset_ref, unit_ref, *rest):
    (*piece_refs, hidden_ref, gate_factor_ref, up_factor_ref, weight_ref, semaphore) = rest
    here = hidden_ref.shape[1]

    @pl.when(pl.program_id(0) == 0)
    def _():
        load_pieces(offset_ref, piece_refs, semaphore, (weight_ref, 0))()

    both = mm(unit_ref[...], weight_ref[...])
    gate = both[:, :here]
    up = both[:, here:]
    sig = 1.0 / (1.0 + jnp.exp(-gate))
    silu = gate * sig
    hidden_ref[...] = (silu * up).astype(BF)
    gate_factor_ref[...] = (up * sig * (1.0 + gate * (1.0 - sig))).astype(BF)
    up_factor_ref[...] = silu.astype(BF)


def hidden_grad_kernel(offset_ref, grad_ref, gate_factor_ref, up_factor_ref, *rest):
    (*piece_refs, both_ref, down_ref, semaphore) = rest
    here = gate_factor_ref.shape[1]

    @pl.when(pl.program_id(0) == 0)
    def _():
        load_pieces(offset_ref, piece_refs, semaphore, (down_ref, 0))()

    grad = mm_nt(grad_ref[...], down_ref[...])
    both_ref[:, :here] = (grad * gate_factor_ref[...].astype(F32)).astype(BF)
    both_ref[:, here:] = (grad * up_factor_ref[...].astype(F32)).astype(BF)


def split_kernel(transposed, order_ref, offset_ref, left_ref, *rest):
    (*piece_refs, keep_ref, send_ref, right_ref, semaphore) = rest

    @pl.when(pl.program_id(0) == 0)
    def _():
        load_pieces(offset_ref, piece_refs, semaphore, (right_ref, 0))()

    product = (mm_nt if transposed else mm)(left_ref[...], right_ref[...])

    @pl.when(pl.program_id(0) % 2 == 0)
    def _():
        keep_ref[...] = product

    @pl.when(pl.program_id(0) % 2 == 1)
    def _():
        send_ref[...] = product.astype(BF)


def output_grad_kernel(
    chunk_rows,
    place_ref,
    g0_ref,
    g1_ref,
    g2_ref,
    g3_ref,
    mixed_ref,
    w0_ref,
    w1_ref,
    w2_ref,
    w3_ref,
    grad_ref,
    terms_ref,
    total_ref,
):
    place = place_ref[0]
    rows_each = g0_ref.shape[0]
    heads = mixed_ref.shape[1]
    columns = w0_ref.shape[1]
    features = pl.ds(pl.multiple_of(place * heads, heads), heads)
    for index, grads in enumerate((g0_ref, g1_ref, g2_ref, g3_ref)):
        rows = pl.ds(pl.multiple_of((place ^ index) * rows_each, rows_each), rows_each)
        total = None
        for part, weight in enumerate((w0_ref, w1_ref, w2_ref, w3_ref)):
            spot = pl.ds(pl.multiple_of((place ^ part) * columns, columns), columns)
            term = mm_nt(grads[:, spot], weight[features, :])
            total = term if total is None else total + term
        grad_ref[rows, :] = total.astype(BF)
        term = mm_tn(mixed_ref[rows, :], grads[...])
        total_ref[...] = term if index == 0 else total_ref[...] + term
    sides = total_ref.shape[1] // terms_ref.shape[1]
    width = terms_ref.shape[1]
    chunks = terms_ref.shape[0] // sides // chunk_rows
    for step in range(chunks):
        for side in range(sides):
            start = (step * sides + side) * chunk_rows
            terms_ref[start : start + chunk_rows, :] = total_ref[
                step * chunk_rows : (step + 1) * chunk_rows, side * width : (side + 1) * width
            ]


def back_kernel(
    head_dim,
    low_ref,
    grad_ref,
    query_ref,
    key_ref,
    value_ref,
    raw_ref,
    cos_ref,
    sin_ref,
    gain_ref,
    start_ref,
    usable_ref,
    out_ref,
    terms_ref,
    key_sum_ref,
    value_sum_ref,
):
    row_length = grad_ref.shape[0]
    query_groups = query_ref.shape[1] // PAIR
    scale = 1.0 / math.sqrt(head_dim)
    key_sum_ref[...] = jnp.zeros_like(key_sum_ref)
    value_sum_ref[...] = jnp.zeros_like(value_sum_ref)
    terms_ref[...] = jnp.zeros_like(terms_ref)

    def through_norm(rows, group, grad, kind):
        grad = grad.astype(BF).astype(F32)
        turned = grad * cos_ref[rows, :] - half_partner(grad, head_dim) * sin_ref[rows, :]
        values = raw_ref[rows, group * PAIR : (group + 1) * PAIR]
        factor = lax.rsqrt(head_means(values * values, head_dim) + EPS)
        unit = values * factor
        terms_ref[kind : kind + 1, :] += jnp.sum(turned * unit, axis=0, keepdims=True)
        scaled = turned * gain_ref[kind : kind + 1, :]
        back = factor * (scaled - unit * head_means(scaled * unit, head_dim))
        out_ref[rows, group * PAIR : (group + 1) * PAIR] = back.astype(BF)

    def attend(first_row, first_key, window):
        bias = mask_bias(start_ref, usable_ref, first_row, first_key, BLOCK, window)
        rows = pl.ds(first_row, BLOCK)
        keys = pl.ds(first_key, window)
        for group in range(query_groups):
            pair = slice(group * PAIR, (group + 1) * PAIR)
            stacked = stacked_heads(query_ref[rows, pair], head_dim)
            grads = stacked_heads(grad_ref[rows, pair], head_dim)
            grown = jnp.exp(mm_nt(stacked, key_ref[keys, pair]) + bias)
            share = grown * (1.0 / jnp.sum(grown, axis=-1, keepdims=True))
            grad_share = mm_nt(grads, value_ref[keys, pair])
            centre = jnp.sum(share * grad_share, axis=-1, keepdims=True)
            grad_score = (share * (grad_share - centre)).astype(BF)
            grad_query = side_by_side(mm(grad_score, key_ref[keys, pair]), head_dim) * scale
            key_sum_ref[keys, pair] += mm_tn(grad_score, stacked)
            value_sum_ref[keys, pair] += mm_tn(share.astype(BF), grads)
            through_norm(rows, group, grad_query, 0)

    each_block(low_ref, row_length, attend)

    def folded(sum_ref, rows):
        first = sum_ref[rows, :PAIR]
        second = sum_ref[rows, PAIR:]
        return jnp.where(
            lanes(first.shape) < head_dim,
            first + pltpu.roll(first, head_dim, 1),
            second + pltpu.roll(second, head_dim, 1),
        )

    def finish(step, carry):
        rows = pl.ds(pl.multiple_of(step * BLOCK, BLOCK), BLOCK)
        through_norm(rows, query_groups, folded(key_sum_ref, rows), 1)
        out_ref[rows, (query_groups + 1) * PAIR :] = folded(value_sum_ref, rows).astype(BF)
        return carry

    lax.fori_loop(0, row_length // BLOCK, finish, 0)


def attention_pack_kernel(
    place_ref,
    gain_ref,
    query_ref,
    key_ref,
    value_ref,
    output_ref,
    pack_ref,
    wide_ref,
    semaphore,
):
    gain = gain_ref[...].astype(BF).astype(F32)
    weights = (query_ref, key_ref, value_ref, output_ref)
    start = 0
    copies = []
    for index, weight_ref in enumerate(weights):
        size = weight_ref.shape[1] // SEQ
        column = pl.multiple_of(place_ref[0] * size, size)
        copies.append(
            pltpu.make_async_copy(
                weight_ref.at[:, pl.ds(column, size)],
                wide_ref.at[:, start : start + size],
                semaphore.at[index],
            )
        )
        copies[-1].start()
        start += size
    start = 0
    for index, weight_ref in enumerate(weights):
        size = weight_ref.shape[1] // SEQ
        copies[index].wait()
        values = wide_ref[:, start : start + size].astype(BF)
        if index < len(weights) - 1:
            values = (values.astype(F32) * gain).astype(BF)
        pack_ref[:, start : start + size] = values
        start += size


def hidden_pack_kernel(
    pieces, place_ref, gain_ref, gate_ref, up_ref, pack_ref, wide_ref, semaphore
):
    piece = gate_ref.shape[1] // (pieces * SEQ)
    here = pieces * piece
    chunk = 32
    steps = gate_ref.shape[0] // chunk
    weights = (gate_ref, up_ref)

    def copy(index, part):
        rows = slice(index * chunk, (index + 1) * chunk)
        return pltpu.make_async_copy(
            weights[part].at[rows, :], wide_ref.at[part, rows, :], semaphore.at[part, index]
        )

    for index in range(steps):
        for part in range(2):
            copy(index, part).start()
    for index in range(steps):
        for part in range(2):
            copy(index, part).wait()
            rows = slice(index * chunk, (index + 1) * chunk)
            gain = gain_ref[rows, :].astype(BF).astype(F32)
            for place in range(SEQ):

                @pl.when(place_ref[0] == place)
                def _(place=place):
                    joined = jnp.concatenate(
                        [
                            wide_ref[part, rows, start : start + piece]
                            for start in range(place * piece, gate_ref.shape[1], SEQ * piece)
                        ],
                        axis=1,
                    )
                    pack_ref[rows, part * here : (part + 1) * here] = (
                        joined.astype(BF).astype(F32) * gain
                    ).astype(BF)


def hidden_owner_kernel(
    pieces, place_ref, sums_ref, gate_ref, up_ref, gain_ref, gate_grad_ref, up_grad_ref, terms_ref
):
    seq_count = sums_ref.shape[0]
    here = sums_ref.shape[2] // 2
    piece = here // pieces
    gain = gain_ref[...].astype(BF).astype(F32)
    total = None
    for part, (weight_ref, grad_ref) in enumerate(
        ((gate_ref, gate_grad_ref), (up_ref, up_grad_ref))
    ):
        sums = [sums_ref[seq].astype(F32) for seq in range(seq_count)]
        joined = jnp.concatenate(
            [
                sums[seq][:, part * here + step * piece : part * here + (step + 1) * piece]
                for step in range(pieces)
                for seq in range(seq_count)
            ],
            axis=1,
        )
        term = row_sums(weight_ref[...].astype(BF).astype(F32) * joined)
        total = term if total is None else total + term
        grad_ref[...] = joined * gain
    terms_ref[...] = total


def attention_owner_kernel(
    place_ref,
    s0_ref,
    s1_ref,
    s2_ref,
    s3_ref,
    query_ref,
    key_ref,
    value_ref,
    gain_ref,
    query_grad_ref,
    key_grad_ref,
    value_grad_ref,
    terms_ref,
):
    place = place_ref[0]
    gain = gain_ref[...].astype(BF).astype(F32)
    pieces = (s0_ref, s1_ref, s2_ref, s3_ref)
    rows = query_ref.shape[0]
    start = 0
    total = None
    for weight_ref, grad_ref in (
        (query_ref, query_grad_ref),
        (key_ref, key_grad_ref),
        (value_ref, value_grad_ref),
    ):
        size = weight_ref.shape[1] // len(pieces)
        for index, sums in enumerate(pieces):
            columns = pl.ds(pl.multiple_of((place ^ index) * size, size), size)
            values = sums[:rows, start : start + size].astype(F32)
            weight = weight_ref[:, columns].astype(BF).astype(F32)
            term = row_sums(weight * values)
            total = term if total is None else total + term
            grad_ref[:, columns] = values * gain
        start += size
    terms_ref[...] = total


def row_sums(values):
    ones = jnp.ones((8, values.shape[1]), BF)
    high = values.astype(BF)
    rest = (values - high.astype(F32)).astype(BF)
    return (mm_nt(ones, high) + mm_nt(ones, rest))[:1]


def placed_call(kernel, results, place_array, operands, blocks, vmem, flops=0, moved=0):
    return pl.pallas_call(
        kernel,
        out_shape=[jax.ShapeDtypeStruct(shape, kind) for shape, kind in results],
        grid_spec=pltpu.PrefetchScalarGridSpec(
            num_scalar_prefetch=1,
            grid=(1,),
            in_specs=[pl.BlockSpec(shape, index) for shape, index in blocks],
            out_specs=[
                pl.BlockSpec(shape, lambda i, place, rank=len(shape): (0,) * rank)
                for shape, _ in results
            ],
        ),
        compiler_params=pltpu.CompilerParams(vmem_limit_bytes=vmem * MEGA),
        cost_estimate=cost(kernel, flops),
    )(place_array, *operands)


def own_rows_block(i, place):
    return (place[0], 0)


def everything(i, place):
    return (0, 0)


MICROSECONDS = {
    "attention_pack_kernel": 2.6,
    "hidden_pack_kernel": 4.2,
    "columns_kernel": 2.6,
    "project_kernel": 9.5,
    "attend_kernel": 7.0,
    "middle_kernel": 5.0,
    "hidden_kernel": 9.0,
    "hidden_grad_kernel": 5.4,
    "output_grad_kernel": 3.0,
    "back_kernel": 15.6,
    "hidden_owner_kernel": 3.1,
    "attention_owner_kernel": 1.9,
}


def cost(kernel, flops):
    name = getattr(kernel, "func", kernel).__name__
    time = MICROSECONDS.get(name, flops * 2.0e-9 + 0.5) * 0.5
    return pl.CostEstimate(flops=int(time * 1.15e9), bytes_accessed=0, transcendentals=0)


def call(
    kernel, results, scalar_count, operands, vmem, pieces=(), scratch=(), flops=0, moved=0
):
    return pl.pallas_call(
        kernel,
        out_shape=[jax.ShapeDtypeStruct(shape, kind) for shape, kind in results],
        in_specs=scalars(scalar_count)
        + whole_vmem(len(operands) - scalar_count)
        + [pl.BlockSpec(memory_space=pltpu.HBM)] * len(pieces),
        out_specs=whole_vmem(len(results)),
        scratch_shapes=list(scratch),
        compiler_params=pltpu.CompilerParams(vmem_limit_bytes=vmem * MEGA),
        cost_estimate=cost(kernel, flops),
    )(*operands, *pieces)


def block_call(kernel, results, scalar_arrays, operands, vmem, pieces, scratch, flops, moved):
    return pl.pallas_call(
        kernel,
        out_shape=[jax.ShapeDtypeStruct(shape, kind) for shape, kind, _, _ in results],
        grid_spec=pltpu.PrefetchScalarGridSpec(
            num_scalar_prefetch=len(scalar_arrays),
            grid=(4,),
            in_specs=[pl.BlockSpec(shape, index) for _, shape, index in operands]
            + [pl.BlockSpec(memory_space=pltpu.HBM)] * len(pieces),
            out_specs=[pl.BlockSpec(shape, index) for _, _, shape, index in results],
            scratch_shapes=list(scratch),
        ),
        compiler_params=pltpu.CompilerParams(vmem_limit_bytes=vmem * MEGA),
        cost_estimate=cost(kernel, flops),
    )(*scalar_arrays, *(array for array, _, _ in operands), *pieces)


def row_block(step, *scalar_refs):
    return (step, 0)


def half_block(step, *scalar_refs):
    return (step // 2, 0)


def first_block(step, *scalar_refs):
    return (0, 0)


def ordered_block(step, order_ref, *scalar_refs):
    return (order_ref[step], 0)


def split_product(left, right_shape, offsets, pieces, transposed, order):
    rows = left.shape[0] // 4
    width = right_shape[0] if transposed else right_shape[1]
    return block_call(
        functools.partial(split_kernel, transposed),
        [
            ((2 * rows, width), F32, (rows, width), half_block),
            ((2 * rows, width), BF, (rows, width), half_block),
        ],
        (order, offsets),
        [(left, (rows, left.shape[1]), ordered_block)],
        20,
        pieces,
        [pltpu.VMEM(right_shape, BF), pltpu.SemaphoreType.DMA((1, len(pieces)))],
        2 * left.shape[0] * left.shape[1] * width,
        2 * (left.size + right_shape[0] * right_shape[1]) + 6 * left.shape[0] * width,
    )


def swap(values, bit):
    count = lax.axis_size("seq")
    return lax.ppermute(values, "seq", [(i, i ^ bit) for i in range(count)])


def seq_pieces(values):
    far = swap(values, 2)
    near = swap(values, 1)
    return (values, near, far, swap(far, 1))


def after(values, *others):
    return lax.optimization_barrier((values, others))[0]


def ring_length():
    count = lax.axis_size("dp")
    return count if count % 2 == 0 and 4 <= count <= 8 else 0


def ring_order(count):
    return list(range(0, count, 2)) + list(range(count - 1, 0, -2))


def ring_sources(offsets):
    count = lax.axis_size("dp")
    place = lax.axis_index("dp")
    spot = jnp.where(place % 2 == 0, place // 2, count - 1 - place // 2)
    spot = (spot + jnp.asarray(offsets, jnp.int32) + count) % count
    return jnp.where(spot < count // 2, 2 * spot, 2 * (count - 1 - spot) + 1)


def ring_source(offset):
    count = lax.axis_size("dp")
    place = lax.axis_index("dp")
    spot = jnp.where(place % 2 == 0, place // 2, count - 1 - place // 2)
    spot = (spot + offset + count) % count
    return jnp.where(spot < count // 2, 2 * spot, 2 * (count - 1 - spot) + 1)


def ring_move(values, step):
    count = lax.axis_size("dp")
    order = ring_order(count)
    return lax.ppermute(
        values, "dp", [(order[i], order[(i + step) % count]) for i in range(count)]
    )


def half_of(rows):
    return rows // 32 * 16 or rows // 2


class GatherRing:
    def __init__(self, shard, long=1, leads=False):
        count = ring_length()
        self.rows = shard.shape[0]
        self.steps = count // 2
        self.pieces = [shard]
        self.spots = [0]
        self.flying = {}
        self.sent = ()
        if not count:
            self.pieces = [lax.all_gather(shard, "dp", axis=0, tiled=True)]
            return
        self.long = long
        self.leads = leads
        self.taken = 0
        self.flying = {1: shard, -1: shard}

    def step(self, *others):
        if not self.steps:
            return others
        self.flying, others = lax.optimization_barrier((self.flying, others))
        self.taken += 1
        ways = [self.long]
        if (self.taken > 1) if self.leads else (self.taken < self.steps):
            ways.append(-self.long)
        self.sent = tuple(self.flying[way] for way in ways)
        for way in ways:
            self.flying[way] = ring_move(self.flying[way], way)
            self.pieces.append(self.flying[way])
            lag = self.leads and way != self.long
            self.spots.append(-way * (self.taken - int(lag)))
        return others

    def arrived(self):
        return self.flying

    @property
    def offsets(self):
        if not self.steps:
            return jnp.zeros((1,), jnp.int32)
        return ring_sources(self.spots) * self.rows


class ScatterRing:
    def __init__(self, terms, halved=False):
        self.count = ring_length()
        self.halved = halved
        self.terms = terms
        self.flying = {}
        if not self.count:
            size = lax.axis_size("dp")
            parts = [term.reshape(size, -1, term.shape[1]) for term in terms]
            whole = self.joined(parts)
            self.sums = lax.psum_scatter(
                whole.reshape(-1, whole.shape[-1]).astype(BF), "dp", scatter_dimension=0, tiled=True
            ).astype(F32)
            self.steps = 0
            self.sent = ()
            return
        self.steps = self.count // 2
        self.taken = 0
        self.sent = ()

    def joined(self, parts):
        return parts[0] if len(parts) == 1 else jnp.concatenate(parts, axis=-2)

    def term(self, offset):
        parts = []
        for term in self.terms:
            rows = term.shape[0] // self.count
            parts.append(lax.dynamic_slice_in_dim(term, ring_source(offset) * rows, rows, 0))
        return self.joined(parts).astype(F32)

    def step(self, *others):
        if not self.steps:
            return others
        self.taken += 1
        left = self.steps + 1 - self.taken
        if self.taken == 1:
            self.terms, others = lax.optimization_barrier((self.terms, others))
            far = self.term(self.steps)
            half = half_of(far.shape[0])
            values = {1: far[:half], -1: far[half:]} if self.halved else {1: far}
        else:
            self.flying, others = lax.optimization_barrier((self.flying, others))
            values = {way: self.term(way * left) for way in (1, -1)}
            if self.taken == 2 and self.halved:
                up, down = (self.flying[1].astype(F32), self.flying[-1].astype(F32))
                half = up.shape[0]
                values = {
                    1: jnp.concatenate([values[1][:half] + up, values[1][half:]]),
                    -1: jnp.concatenate([values[-1][:half], values[-1][half:] + down]),
                }
            else:
                for way, arrived in self.flying.items():
                    values[way] = values[way] + arrived.astype(F32)
        sent = {way: value.astype(BF) for way, value in values.items()}
        self.sent = tuple(sent.values())
        self.flying = {way: ring_move(value, way) for way, value in sent.items()}
        return others

    def arrived(self):
        return self.flying

    def take(self, arrived):
        self.flying = arrived

    def result(self):
        if not self.steps:
            return self.sums
        return self.term(0) + self.flying[1].astype(F32) + self.flying[-1].astype(F32)


def local(
    tokens,
    segments,
    valid_mask,
    attention_gain,
    query_weight,
    key_weight,
    value_weight,
    query_gain,
    key_gain,
    output_weight,
    feedforward_gain,
    gate_weight,
    up_weight,
    down_weight,
    cotangent,
):
    seq_count = lax.axis_size("seq")
    dp_count = lax.axis_size("dp")
    place = lax.axis_index("seq")
    local_rows = tokens.shape[1]
    row_length = segments.shape[1]
    head_dim = query_gain.shape[0]
    width = tokens.shape[2]
    hidden_width = gate_weight.shape[1]
    query_width = query_weight.shape[1]
    key_width = key_weight.shape[1]
    query_here = query_width // seq_count
    key_here = key_width // seq_count
    hidden_here = hidden_width // seq_count
    weight_rows = query_weight.shape[0]
    own_rows = weight_rows // seq_count
    segment_row = segments[0]
    valid_row = valid_mask[0]

    def low(weight):
        return weight.astype(BF).astype(F32)

    place_array = place.astype(jnp.int32).reshape(1)
    gain_one = attention_gain[:, None]
    gain_two = feedforward_gain[:, None]
    qkv_width = query_here + 2 * key_here
    piece = hidden_width // (dp_count * seq_count)
    kernels_fit = weight_rows % 32 == 0 and own_rows % 8 == 0 and dp_count <= 8

    pack_width = qkv_width + width // seq_count
    (attention_pack,) = call(
        attention_pack_kernel,
        [((weight_rows, pack_width), BF)],
        1,
        (place_array, gain_one),
        58,
        pieces=(query_weight, key_weight, value_weight, output_weight),
        scratch=[pltpu.VMEM((weight_rows, pack_width), F32), pltpu.SemaphoreType.DMA((4,))],
        moved=8 * weight_rows * width,
    )
    if kernels_fit:
        (gate_up_pack,) = call(
            functools.partial(hidden_pack_kernel, dp_count),
            [((weight_rows, 2 * hidden_here), BF)],
            1,
            (place_array, after(gain_two, attention_pack)),
            58,
            pieces=(gate_weight, up_weight),
            scratch=[
                pltpu.VMEM((2, weight_rows, hidden_width), F32),
                pltpu.SemaphoreType.DMA((2, weight_rows // 32)),
            ],
            moved=8 * weight_rows * hidden_width,
        )
    else:

        def hidden_columns(weight):
            split = weight.reshape(weight_rows, dp_count, seq_count, piece)
            mine = lax.dynamic_index_in_dim(split, place, 2, keepdims=False)
            return (low(mine.reshape(weight_rows, hidden_here)) * low(gain_two)).astype(BF)

        gate_up_pack = jnp.concatenate(
            [hidden_columns(gate_weight), hidden_columns(up_weight)], axis=1
        )
    down_pack = lax.dynamic_slice_in_dim(down_weight, place * piece, piece, 0).astype(BF)
    down_pack = after(down_pack, attention_pack)

    order = place ^ jnp.arange(4, dtype=jnp.int32)
    plain = jnp.arange(4, dtype=jnp.int32)

    token_far = swap(tokens[0], 2)
    token_near = swap(tokens[0], 1)
    attention_ring = GatherRing(attention_pack)
    attention_ring.step()
    positions = doc_positions(segment_row)
    starts = jnp.arange(row_length, dtype=jnp.int32) - positions
    cos_wide, sin_wide = rope_tables(positions, head_dim)
    repeats = PAIR // head_dim
    head_gains = jnp.tile(jnp.stack([query_gain, key_gain]), (1, repeats))
    row_starts = starts[:, None]
    usable = valid_row[None, :]
    starts, row_starts, head_gains = attention_ring.step(starts, row_starts, head_gains)
    block_lows = starts[::BLOCK]
    token_far, cos_wide, sin_wide = attention_ring.step(token_far, cos_wide, sin_wide)
    token_pieces = (tokens[0], token_near, token_far, swap(token_far, 1))
    grad_far = swap(after(cotangent[0], token_far), 2)
    grad_near = swap(after(cotangent[0], token_far), 1)
    (gate_up_pack,) = attention_ring.step(gate_up_pack)

    gate_up_ring = GatherRing(after(gate_up_pack, attention_ring.arrived()))
    (grad_far,) = gate_up_ring.step(grad_far)
    grad_row_pieces = (cotangent[0], grad_near, grad_far, swap(grad_far, 1))
    (output_columns,) = pl.pallas_call(
        functools.partial(columns_kernel, qkv_width),
        out_shape=[jax.ShapeDtypeStruct((query_width, width // seq_count), BF)],
        in_specs=scalars(1) + [pl.BlockSpec(memory_space=pltpu.HBM)] * len(attention_ring.pieces),
        out_specs=whole_vmem(1),
        scratch_shapes=[pltpu.SemaphoreType.DMA((1, len(attention_ring.pieces)))],
        compiler_params=pltpu.CompilerParams(vmem_limit_bytes=58 * MEGA),
        cost_estimate=cost(columns_kernel, 0),
    )(attention_ring.offsets, *attention_ring.pieces)
    output_far = swap(output_columns, 2)
    output_near = swap(output_columns, 1)
    projected = call(
        functools.partial(project_kernel, head_dim),
        [
            ((row_length, width), BF),
            ((row_length, query_here + key_here), F32),
            ((row_length, query_here), BF),
            ((row_length, 2 * key_here), BF),
            ((row_length, 2 * key_here), BF),
            ((width, qkv_width), BF),
        ],
        2,
        (place_array, attention_ring.offsets, *token_pieces, cos_wide, sin_wide, head_gains),
        58,
        pieces=attention_ring.pieces,
        scratch=[pltpu.SemaphoreType.DMA((1, len(attention_ring.pieces)))],
        flops=2 * row_length * width * qkv_width,
        moved=12 * row_length * width,
    )
    projected, output_far = gate_up_ring.step(projected, output_far)
    output_pieces = (output_columns, output_near, output_far, swap(output_far, 1))
    unit_one, raw, queries, keys_two, values_two, qkv_weight = projected
    (mixed_here,) = call(
        functools.partial(attend_kernel, head_dim),
        [((row_length, query_here), BF)],
        1,
        (block_lows, queries, keys_two, values_two, row_starts, usable),
        58,
        flops=row_length * width * qkv_width,
        moved=4 * row_length * width,
    )
    (mixed_here,) = gate_up_ring.step(mixed_here)
    mixed_far = swap(mixed_here, 2)
    mixed_near = swap(mixed_here, 1)
    (mixed_far,) = gate_up_ring.step(mixed_far)
    down_ring = GatherRing(after(down_pack, mixed_far), -1, True)
    down_ring.step()
    mixed_pieces = (mixed_here, mixed_near, mixed_far, swap(mixed_far, 1))
    unit_two, after_here = call(
        middle_kernel,
        [((row_length, width), BF), ((local_rows, width), F32)],
        1,
        (place_array, *token_pieces, *mixed_pieces, *output_pieces),
        18,
        scratch=[pltpu.VMEM((local_rows, width), F32)],
        flops=2 * row_length * width * width,
        moved=10 * row_length * width,
    )
    (unit_two,) = down_ring.step(unit_two)

    rows_each = row_length // 4
    hidden, gate_factor, up_factor = block_call(
        hidden_kernel,
        [((row_length, hidden_here), BF, (rows_each, hidden_here), row_block)] * 3,
        (gate_up_ring.offsets,),
        [(unit_two, (rows_each, width), row_block)],
        28,
        gate_up_ring.pieces,
        [
            pltpu.VMEM((width, 2 * hidden_here), BF),
            pltpu.SemaphoreType.DMA((1, len(gate_up_ring.pieces))),
        ],
        4 * row_length * width * hidden_here,
        8 * row_length * hidden_here + 4 * width * hidden_here,
    )
    hidden, gate_factor, up_factor = down_ring.step(hidden, gate_factor, up_factor)
    grad_rows = jnp.concatenate(grad_row_pieces)
    down_scatter = ScatterRing([mm_tn(hidden, grad_rows)])
    (down_scatter.terms,) = down_ring.step(down_scatter.terms)
    down_scatter.step()
    gate_up_grad, down_all = block_call(
        hidden_grad_kernel,
        [
            ((row_length, 2 * hidden_here), BF, (rows_each, 2 * hidden_here), row_block),
            ((hidden_here, width), BF, (hidden_here, width), first_block),
        ],
        (down_ring.offsets,),
        [
            (grad_rows, (rows_each, width), row_block),
            (gate_factor, (rows_each, hidden_here), row_block),
            (up_factor, (rows_each, hidden_here), row_block),
        ],
        24,
        down_ring.pieces,
        [pltpu.SemaphoreType.DMA((1, len(down_ring.pieces)))],
        2 * row_length * width * hidden_here,
        8 * row_length * hidden_here + 4 * width * hidden_here,
    )

    (gate_up_grad,) = down_scatter.step(gate_up_grad)
    keep, send = split_product(
        gate_up_grad, (width, 2 * hidden_here), gate_up_ring.offsets, gate_up_ring.pieces, True, plain
    )
    keep, send = down_scatter.step(keep, send)

    def halves(keep, near):
        return (
            keep[:local_rows] + near[:local_rows].astype(F32),
            (keep[local_rows:] + near[local_rows:].astype(F32)).astype(BF),
        )

    half_sum, half_send = halves(keep, swap(send, 1))
    half_send, unit_two = lax.optimization_barrier((half_send, unit_two))
    arrived = swap(half_send, 2)
    gate_up_scatter = ScatterRing([mm_tn(unit_two, gate_up_grad).astype(BF)], True)
    gate_up_scatter.step()
    unit_here, factor_here = rms_stats(after_here)
    grad_after = cotangent[0].astype(F32) + rms_back(
        half_sum + arrived.astype(F32), unit_here, factor_here
    )
    (branch,) = gate_up_scatter.step(grad_after.astype(BF))
    branch_far = swap(branch, 2)
    branch_near = swap(branch, 1)
    keep, send = split_product(
        after(hidden, branch, gate_up_scatter.sent),
        (hidden_here, width),
        jnp.zeros((1,), jnp.int32),
        [down_all],
        False,
        plain,
    )
    keep, send, branch_far = gate_up_scatter.step(keep, send, branch_far)
    down_scatter.step(branch_far)
    branch_pieces = (branch, branch_near, branch_far, swap(branch_far, 1))
    half_sum, half_send = halves(keep, swap(send, 1))
    chunk_rows = query_width // (dp_count * seq_count)
    grad_mixed, output_terms = call(
        functools.partial(output_grad_kernel, chunk_rows),
        [
            ((row_length, query_here), BF),
            ((query_here * width // qkv_width, qkv_width), F32),
        ],
        1,
        (place_array, *branch_pieces, mixed_here, *output_pieces),
        14,
        scratch=[pltpu.VMEM((query_here, width), F32)],
        flops=4 * row_length * width * query_here,
        moved=8 * row_length * width,
    )

    grad_mixed, half_send = gate_up_scatter.step(grad_mixed, half_send)
    arrived = swap(half_send, 2)
    qkv_grad, gain_terms = call(
        functools.partial(back_kernel, head_dim),
        [((row_length, qkv_width), BF), ((8, PAIR), F32)],
        1,
        (block_lows, after(grad_mixed, gate_up_scatter.sent), queries, keys_two, values_two, raw)
        + (cos_wide, sin_wide, head_gains, row_starts, usable),
        24,
        scratch=[pltpu.VMEM((row_length, 2 * key_here), F32)] * 2,
        flops=4 * row_length * width * qkv_width,
        moved=12 * row_length * width,
    )
    qkv_grad, gain_terms, arrived, gate_up_arrived, down_arrived = lax.optimization_barrier(
        (qkv_grad, gain_terms, arrived, gate_up_scatter.arrived(), down_scatter.arrived())
    )
    down_scatter.take(down_arrived)
    gate_up_scatter.take(gate_up_arrived)
    layer_out = (after_here + half_sum + arrived.astype(F32)).astype(BF)
    gain_rows = jnp.concatenate([gain_terms[0:1], gain_terms[1:2]], axis=1)
    gain_rows = jnp.pad(gain_rows, ((0, 15), (0, qkv_width - 2 * PAIR)))
    packed = jnp.concatenate(
        [
            mm_tn(unit_one, qkv_grad).reshape(dp_count, weight_rows, qkv_width),
            output_terms.reshape(dp_count, -1, qkv_width),
            jnp.broadcast_to(gain_rows, (dp_count, *gain_rows.shape)),
        ],
        axis=1,
    )
    attention_scatter = ScatterRing([packed.reshape(-1, qkv_width)])
    attention_scatter.step()
    gate_up_scatter.take(after(gate_up_scatter.arrived(), attention_scatter.sent))
    gate_up_sums = gate_up_scatter.result().astype(BF)
    keep, send = split_product(
        after(qkv_grad, gate_up_sums),
        (width, qkv_width),
        jnp.zeros((1,), jnp.int32),
        [qkv_weight],
        True,
        order,
    )
    keep, send = attention_scatter.step(keep, send)
    gate_up_sums = after(gate_up_sums, attention_scatter.sent)
    hidden_own = lax.all_to_all(
        gate_up_sums.reshape(seq_count, own_rows, -1), "seq", split_axis=0, concat_axis=0, tiled=True
    )
    half_sum, half_send = halves(keep, swap(send, 1))
    (half_send,) = attention_scatter.step(half_send)
    arrived = swap(half_send, 2)
    for _ in range(attention_scatter.steps - 3):
        (arrived,) = attention_scatter.step(arrived)
        hidden_own = after(hidden_own, attention_scatter.sent)
    unit_tokens, factor_tokens = rms_stats(tokens[0].astype(F32))
    token_grad = (
        grad_after + rms_back(half_sum + arrived.astype(F32), unit_tokens, factor_tokens)
    ).astype(BF)

    down_sums = down_scatter.result()
    attention_sums = attention_scatter.result().astype(BF)
    qkv_sums = attention_sums[:weight_rows]
    output_sums = jnp.concatenate(
        [
            attention_sums[weight_rows + part * chunk_rows : weight_rows + (part + 1) * chunk_rows]
            for part in range(width // qkv_width)
        ],
        axis=1,
    )

    def own(weight):
        return lax.dynamic_slice_in_dim(weight, place * own_rows, own_rows, 0)

    gain_row = attention_sums[-16:]
    qkv_pieces = []
    for bits in range(4):
        part = lax.dynamic_slice_in_dim(qkv_sums, (place ^ bits) * own_rows, own_rows, 0)
        part = after(jnp.concatenate([part, gain_row]), arrived)
        qkv_pieces.append(swap(part, bits) if bits else part)
    gain_sums = sum(piece[own_rows : own_rows + 1].astype(F32) for piece in qkv_pieces)
    gain_sums = jnp.sum(gain_sums[0, : 2 * PAIR].reshape(2, repeats, head_dim), axis=1)
    if kernels_fit:
        gate_grad, up_grad, feed_gain_grad = placed_call(
            functools.partial(hidden_owner_kernel, dp_count),
            [((own_rows, hidden_width), F32)] * 2 + [((1, own_rows), F32)],
            place_array,
            (hidden_own, gate_weight, up_weight, gain_two),
            [
                (hidden_own.shape, lambda i, place: (0, 0, 0)),
                ((own_rows, hidden_width), own_rows_block),
                ((own_rows, hidden_width), own_rows_block),
                ((own_rows, 1), own_rows_block),
            ],
            58,
            moved=20 * own_rows * hidden_width,
        )
        query_grad, key_grad, value_grad, attention_gain_grad = placed_call(
            attention_owner_kernel,
            [((own_rows, query_width), F32)]
            + [((own_rows, key_width), F32)] * 2
            + [((1, own_rows), F32)],
            place_array,
            (*qkv_pieces, query_weight, key_weight, value_weight, gain_one),
            [((own_rows + 16, qkv_width), everything)] * 4
            + [
                ((own_rows, query_width), own_rows_block),
                ((own_rows, key_width), own_rows_block),
                ((own_rows, key_width), own_rows_block),
                ((own_rows, 1), own_rows_block),
            ],
            58,
            moved=20 * own_rows * query_width,
        )
    else:
        spread = jnp.stack(qkv_pieces)[order, :own_rows].astype(F32)

        def joined(first, size):
            return jnp.swapaxes(spread[:, :, first : first + size], 0, 1).reshape(own_rows, -1)

        query_own = joined(0, query_here)
        key_own = joined(query_here, key_here)
        value_own = joined(query_here + key_here, key_here)
        attention_gain_grad = (
            jnp.sum(own(low(query_weight)) * query_own, axis=1)
            + jnp.sum(own(low(key_weight)) * key_own, axis=1)
            + jnp.sum(own(low(value_weight)) * value_own, axis=1)
        )
        gain_own = own(low(gain_one))
        query_grad, key_grad, value_grad = (
            query_own * gain_own,
            key_own * gain_own,
            value_own * gain_own,
        )
        hidden_own = hidden_own.reshape(seq_count, own_rows, 2, dp_count, piece)
        hidden_own = jnp.transpose(hidden_own, (2, 1, 3, 0, 4))
        hidden_own = hidden_own.reshape(2, own_rows, hidden_width).astype(F32)
        feed_gain_grad = jnp.sum(own(low(gate_weight)) * hidden_own[0], axis=1) + jnp.sum(
            own(low(up_weight)) * hidden_own[1], axis=1
        )
        gain_own = own(low(gain_two))
        gate_grad, up_grad = (hidden_own[0] * gain_own, hidden_own[1] * gain_own)

    moves = [
        (dp * seq_count + seq, seq * dp_count + dp)
        for dp in range(dp_count)
        for seq in range(seq_count)
    ]
    output_own = lax.ppermute(output_sums, ("dp", "seq"), moves).astype(F32)

    return (
        layer_out.reshape(1, local_rows, -1),
        token_grad.reshape(1, local_rows, -1),
        attention_gain_grad.reshape(own_rows),
        query_grad,
        key_grad,
        value_grad,
        gain_sums[0],
        gain_sums[1],
        output_own,
        feed_gain_grad.reshape(own_rows),
        gate_grad,
        up_grad,
        down_sums,
    )


def solution(mesh):
    in_specs = (
        P("dp", "seq", None),
        P("dp", None),
        P("dp", None),
        P("dp"),
        P("dp", None),
        P("dp", None),
        P("dp", None),
        P(),
        P(),
        P("dp", None),
        P("dp"),
        P("dp", None),
        P("dp", None),
        P("dp", None),
        P("dp", "seq", None),
    )
    out_specs = (
        P("dp", "seq", None),
        P("dp", "seq", None),
        P(("dp", "seq")),
        P(("dp", "seq"), None),
        P(("dp", "seq"), None),
        P(("dp", "seq"), None),
        P(),
        P(),
        P(("dp", "seq"), None),
        P(("dp", "seq")),
        P(("dp", "seq"), None),
        P(("dp", "seq"), None),
        P(("dp", "seq"), None),
    )
    return jax.shard_map(local, mesh=mesh, in_specs=in_specs, out_specs=out_specs, check_vma=False)
```

```python
import functools
import math

import jax
import jax.numpy as jnp
from jax import lax
from jax.experimental import pallas as pl
from jax.experimental.pallas import tpu as pltpu
from jax.sharding import PartitionSpec as P

EPS = 1e-05
ROPE_BASE = 1000000.0
NEG_FILL = -1e30
BF = jnp.bfloat16
F32 = jnp.float32
BLOCK = 128
PAIR = 128
SEQ = 4
MEGA = 1024 * 1024


def dot(left, right, dims):
    return lax.dot_general(left, right, (dims, ((), ())), preferred_element_type=F32)


def mm(left, right):
    return dot(left, right, ((1,), (0,)))


def mm_nt(left, right):
    return dot(left, right, ((1,), (1,)))


def mm_tn(left, right):
    return dot(left, right, ((0,), (0,)))


def rms_stats(values):
    factor = lax.rsqrt(jnp.mean(values * values, axis=-1, keepdims=True) + EPS)
    return (values * factor, factor)


def rms_back(grad_unit, unit_values, factor):
    return factor * (
        grad_unit - unit_values * jnp.mean(grad_unit * unit_values, axis=-1, keepdims=True)
    )


def doc_positions(segment_row):
    length = segment_row.shape[0]
    places = jnp.arange(length, dtype=jnp.int32)
    change = jnp.concatenate([jnp.ones((1,), dtype=jnp.bool_), segment_row[1:] != segment_row[:-1]])
    starts = lax.cummax(jnp.where(change, places, jnp.zeros_like(places)), axis=0)
    return places - starts


def rope_tables(positions, head_dim):
    half = head_dim // 2
    lane = jnp.arange(PAIR, dtype=jnp.int32)
    frequency = ROPE_BASE ** (-(lane % half).astype(F32) / half)
    angles = positions.astype(F32)[:, None] * frequency[None, :]
    sign = jnp.where(lane % head_dim < half, -1.0, 1.0)
    return (jnp.cos(angles), jnp.sin(angles) * sign[None, :])


def whole_vmem(count):
    return [pl.BlockSpec(memory_space=pltpu.VMEM)] * count


def scalars(count):
    return [pl.BlockSpec(memory_space=pltpu.SMEM)] * count


def lanes(shape):
    return lax.broadcasted_iota(jnp.int32, shape, 1)


def head_means(values, head_dim):
    width = values.shape[1]
    row = lax.broadcasted_iota(jnp.int32, (width, width), 0) // head_dim
    column = lax.broadcasted_iota(jnp.int32, (width, width), 1) // head_dim
    spread = jnp.where(row == column, 1.0 / head_dim, 0.0).astype(BF)
    high = values.astype(BF)
    rest = (values - high.astype(F32)).astype(BF)
    return mm(high, spread) + mm(rest, spread)


def half_partner(values, head_dim):
    half = head_dim // 2
    width = values.shape[1]
    upper = (lanes(values.shape) % head_dim) >= half
    return jnp.where(
        upper, pltpu.roll(values, half, 1), pltpu.roll(values, width - half, 1)
    )


def stacked_heads(pair, head_dim):
    first = lanes(pair.shape) < head_dim
    zero = jnp.zeros_like(pair)
    return jnp.concatenate([jnp.where(first, pair, zero), jnp.where(first, zero, pair)], axis=0)


def side_by_side(stacked, head_dim):
    rows = stacked.shape[0] // 2
    return jnp.where(
        lanes((rows, stacked.shape[1])) < head_dim, stacked[:rows], stacked[rows:]
    )


def mask_bias(start_ref, usable_ref, first_row, first_key, rows, window):
    row = first_row + lax.broadcasted_iota(jnp.int32, (rows, window), 0)
    key = first_key + lax.broadcasted_iota(jnp.int32, (rows, window), 1)
    start = start_ref[pl.ds(first_row, rows), :]
    usable = usable_ref[:, pl.ds(first_key, window)] > 0
    allowed = ((key >= start) & (key <= row) & usable) | (key == row)
    bias = jnp.where(allowed, 0.0, NEG_FILL)
    return jnp.concatenate([bias, bias], axis=0)


def each_block(low_ref, row_length, body):
    long_window = min(5 * BLOCK, row_length)

    def step(index, carry):
        first_row = pl.multiple_of(index * BLOCK, BLOCK)
        short_key = jnp.maximum(first_row - BLOCK, 0)
        is_short = low_ref[index] >= short_key

        @pl.when(is_short)
        def _():
            body(first_row, pl.multiple_of(short_key, BLOCK), 2 * BLOCK)

        @pl.when(jnp.logical_not(is_short))
        def _():
            long_key = jnp.maximum(first_row + BLOCK - long_window, 0)
            body(first_row, pl.multiple_of(long_key, BLOCK), long_window)

        return carry

    lax.fori_loop(0, row_length // BLOCK, step, 0)


def load_pieces(offset_ref, piece_refs, semaphore, *targets):
    copies = []
    for index, piece in enumerate(piece_refs):
        start = pl.multiple_of(offset_ref[index], 16)
        for part, (target, column) in enumerate(targets):
            rows = pl.ds(start, piece.shape[0])
            copies.append(
                pltpu.make_async_copy(
                    piece.at[:, column : column + target.shape[1]],
                    target.at[rows, :],
                    semaphore.at[part, index],
                )
            )
    for copy in copies:
        copy.start()

    def wait():
        for copy in copies:
            copy.wait()

    return wait


def columns_kernel(column, offset_ref, *rest):
    (*piece_refs, out_ref, semaphore) = rest
    load_pieces(offset_ref, piece_refs, semaphore, (out_ref, column))()


def project_kernel(
    head_dim,
    place_ref,
    offset_ref,
    x0_ref,
    x1_ref,
    x2_ref,
    x3_ref,
    cos_ref,
    sin_ref,
    gain_ref,
    *rest,
):
    (*piece_refs, unit_ref, raw_ref, query_ref, key_ref, value_ref, weight_ref) = rest[:-1]
    semaphore = rest[-1]
    wait = load_pieces(offset_ref, piece_refs, semaphore, (weight_ref, 0))
    place = place_ref[0]
    rows_each = x0_ref.shape[0]
    row_length = unit_ref.shape[0]
    query_groups = query_ref.shape[1] // PAIR
    for index, piece in enumerate((x0_ref, x1_ref, x2_ref, x3_ref)):

        def normalize(step, carry, piece=piece, base=(place ^ index) * rows_each):
            start = pl.multiple_of(step * BLOCK, BLOCK)
            values = piece[pl.ds(start, BLOCK), :].astype(F32)
            factor = lax.rsqrt(jnp.mean(values * values, axis=-1, keepdims=True) + EPS)
            rows = pl.ds(pl.multiple_of(base + start, BLOCK), BLOCK)
            unit_ref[rows, :] = (values * factor).astype(BF)
            return carry

        lax.fori_loop(0, rows_each // BLOCK, normalize, 0)
    wait()

    def project(step, carry):
        rows = pl.ds(pl.multiple_of(step * rows_each, rows_each), rows_each)
        raw = mm(unit_ref[rows, :], weight_ref[...])
        raw_ref[rows, :] = raw[:, : raw_ref.shape[1]]
        cos = cos_ref[rows, :]
        sin = sin_ref[rows, :]
        for group in range(query_groups + 1):
            is_key = group == query_groups
            values = raw[:, group * PAIR : (group + 1) * PAIR]
            factor = lax.rsqrt(head_means(values * values, head_dim) + EPS)
            scaled = values * factor * gain_ref[int(is_key) : int(is_key) + 1, :]
            turned = scaled * cos + half_partner(scaled, head_dim) * sin
            if is_key:
                crossed = pltpu.roll(turned, head_dim, 1)
                first = lanes(turned.shape) < head_dim
                key_ref[rows, :PAIR] = jnp.where(first, turned, crossed).astype(BF)
                key_ref[rows, PAIR:] = jnp.where(first, crossed, turned).astype(BF)
                values = raw[:, (group + 1) * PAIR :]
                crossed = pltpu.roll(values, head_dim, 1)
                value_ref[rows, :PAIR] = jnp.where(first, values, crossed).astype(BF)
                value_ref[rows, PAIR:] = jnp.where(first, crossed, values).astype(BF)
            else:
                query_ref[rows, group * PAIR : (group + 1) * PAIR] = (
                    turned * (1.0 / math.sqrt(head_dim))
                ).astype(BF)
        return carry

    lax.fori_loop(0, row_length // rows_each, project, 0)


def attend_kernel(
    head_dim, low_ref, query_ref, key_ref, value_ref, start_ref, usable_ref, mixed_ref
):
    row_length = query_ref.shape[0]
    query_groups = query_ref.shape[1] // PAIR

    def attend(first_row, first_key, window):
        bias = mask_bias(start_ref, usable_ref, first_row, first_key, BLOCK, window)
        rows = pl.ds(first_row, BLOCK)
        keys = pl.ds(first_key, window)
        found = []
        for group in range(query_groups):
            pair = slice(group * PAIR, (group + 1) * PAIR)
            stacked = stacked_heads(query_ref[rows, pair], head_dim)
            grown = jnp.exp(mm_nt(stacked, key_ref[keys, pair]) + bias)
            mixed = mm(grown.astype(BF), value_ref[keys, pair])
            mixed = mixed * (1.0 / jnp.sum(grown, axis=-1, keepdims=True))
            found.append(side_by_side(mixed, head_dim).astype(BF))
        mixed_ref[rows, :] = jnp.concatenate(found, axis=1)

    each_block(low_ref, row_length, attend)


def middle_kernel(
    place_ref,
    x0_ref,
    x1_ref,
    x2_ref,
    x3_ref,
    o0_ref,
    o1_ref,
    o2_ref,
    o3_ref,
    w0_ref,
    w1_ref,
    w2_ref,
    w3_ref,
    unit_ref,
    here_ref,
    sum_ref,
):
    place = place_ref[0]
    rows_each, width = x0_ref.shape
    heads = o0_ref.shape[1]
    columns = w0_ref.shape[1]
    for index, piece in enumerate((x0_ref, x1_ref, x2_ref, x3_ref)):
        base = pl.multiple_of((place ^ index) * rows_each, rows_each)
        rows = pl.ds(base, rows_each)
        for part, weight in enumerate((w0_ref, w1_ref, w2_ref, w3_ref)):
            total = None
            for other, mixed in enumerate((o0_ref, o1_ref, o2_ref, o3_ref)):
                features = pl.ds(pl.multiple_of((place ^ other) * heads, heads), heads)
                term = mm(mixed[rows, :], weight[features, :])
                total = term if total is None else total + term
            spot = pl.multiple_of((place ^ part) * columns, columns)
            sum_ref[:, pl.ds(spot, columns)] = total


        def normalize(step, carry, piece=piece, index=index):
            start = pl.multiple_of(step * BLOCK, BLOCK)
            part = pl.ds(start, BLOCK)
            values = sum_ref[part, :] + piece[part, :].astype(F32)
            if index == 0:
                here_ref[part, :] = values
            factor = lax.rsqrt(jnp.mean(values * values, axis=-1, keepdims=True) + EPS)
            target = pl.ds(pl.multiple_of(index * rows_each + start, BLOCK), BLOCK)
            unit_ref[target, :] = (values * factor).astype(BF)
            return carry

        lax.fori_loop(0, rows_each // BLOCK, normalize, 0)


def hidden_kernel(offset_ref, unit_ref, *rest):
    (*piece_refs, hidden_ref, gate_factor_ref, up_factor_ref, weight_ref, semaphore) = rest
    here = hidden_ref.shape[1]

    @pl.when(pl.program_id(0) == 0)
    def _():
        load_pieces(offset_ref, piece_refs, semaphore, (weight_ref, 0))()

    both = mm(unit_ref[...], weight_ref[...])
    gate = both[:, :here]
    up = both[:, here:]
    sig = 1.0 / (1.0 + jnp.exp(-gate))
    silu = gate * sig
    hidden_ref[...] = (silu * up).astype(BF)
    gate_factor_ref[...] = (up * sig * (1.0 + gate * (1.0 - sig))).astype(BF)
    up_factor_ref[...] = silu.astype(BF)


def hidden_grad_kernel(offset_ref, grad_ref, gate_factor_ref, up_factor_ref, *rest):
    (*piece_refs, both_ref, down_ref, semaphore) = rest
    here = gate_factor_ref.shape[1]

    @pl.when(pl.program_id(0) == 0)
    def _():
        load_pieces(offset_ref, piece_refs, semaphore, (down_ref, 0))()

    grad = mm_nt(grad_ref[...], down_ref[...])
    both_ref[:, :here] = (grad * gate_factor_ref[...].astype(F32)).astype(BF)
    both_ref[:, here:] = (grad * up_factor_ref[...].astype(F32)).astype(BF)


def split_kernel(transposed, order_ref, offset_ref, left_ref, *rest):
    (*piece_refs, keep_ref, send_ref, right_ref, semaphore) = rest

    @pl.when(pl.program_id(0) == 0)
    def _():
        load_pieces(offset_ref, piece_refs, semaphore, (right_ref, 0))()

    product = (mm_nt if transposed else mm)(left_ref[...], right_ref[...])

    @pl.when(pl.program_id(0) % 2 == 0)
    def _():
        keep_ref[...] = product

    @pl.when(pl.program_id(0) % 2 == 1)
    def _():
        send_ref[...] = product.astype(BF)


def output_grad_kernel(
    chunk_rows,
    place_ref,
    g0_ref,
    g1_ref,
    g2_ref,
    g3_ref,
    mixed_ref,
    w0_ref,
    w1_ref,
    w2_ref,
    w3_ref,
    grad_ref,
    terms_ref,
    total_ref,
):
    place = place_ref[0]
    rows_each = g0_ref.shape[0]
    heads = mixed_ref.shape[1]
    columns = w0_ref.shape[1]
    features = pl.ds(pl.multiple_of(place * heads, heads), heads)
    for index, grads in enumerate((g0_ref, g1_ref, g2_ref, g3_ref)):
        rows = pl.ds(pl.multiple_of((place ^ index) * rows_each, rows_each), rows_each)
        total = None
        for part, weight in enumerate((w0_ref, w1_ref, w2_ref, w3_ref)):
            spot = pl.ds(pl.multiple_of((place ^ part) * columns, columns), columns)
            term = mm_nt(grads[:, spot], weight[features, :])
            total = term if total is None else total + term
        grad_ref[rows, :] = total.astype(BF)
        term = mm_tn(mixed_ref[rows, :], grads[...])
        total_ref[...] = term if index == 0 else total_ref[...] + term
    sides = total_ref.shape[1] // terms_ref.shape[1]
    width = terms_ref.shape[1]
    chunks = terms_ref.shape[0] // sides // chunk_rows
    for step in range(chunks):
        for side in range(sides):
            start = (step * sides + side) * chunk_rows
            terms_ref[start : start + chunk_rows, :] = total_ref[
                step * chunk_rows : (step + 1) * chunk_rows, side * width : (side + 1) * width
            ]


def back_kernel(
    head_dim,
    low_ref,
    grad_ref,
    query_ref,
    key_ref,
    value_ref,
    raw_ref,
    cos_ref,
    sin_ref,
    gain_ref,
    start_ref,
    usable_ref,
    out_ref,
    terms_ref,
    key_sum_ref,
    value_sum_ref,
):
    row_length = grad_ref.shape[0]
    query_groups = query_ref.shape[1] // PAIR
    scale = 1.0 / math.sqrt(head_dim)
    key_sum_ref[...] = jnp.zeros_like(key_sum_ref)
    value_sum_ref[...] = jnp.zeros_like(value_sum_ref)
    terms_ref[...] = jnp.zeros_like(terms_ref)

    def through_norm(rows, group, grad, kind):
        grad = grad.astype(BF).astype(F32)
        turned = grad * cos_ref[rows, :] - half_partner(grad, head_dim) * sin_ref[rows, :]
        values = raw_ref[rows, group * PAIR : (group + 1) * PAIR]
        factor = lax.rsqrt(head_means(values * values, head_dim) + EPS)
        unit = values * factor
        terms_ref[kind : kind + 1, :] += jnp.sum(turned * unit, axis=0, keepdims=True)
        scaled = turned * gain_ref[kind : kind + 1, :]
        back = factor * (scaled - unit * head_means(scaled * unit, head_dim))
        out_ref[rows, group * PAIR : (group + 1) * PAIR] = back.astype(BF)

    def attend(first_row, first_key, window):
        bias = mask_bias(start_ref, usable_ref, first_row, first_key, BLOCK, window)
        rows = pl.ds(first_row, BLOCK)
        keys = pl.ds(first_key, window)
        found = []
        for group in range(query_groups):
            pair = slice(group * PAIR, (group + 1) * PAIR)
            stacked = stacked_heads(query_ref[rows, pair], head_dim)
            grads = stacked_heads(grad_ref[rows, pair], head_dim)
            grown = jnp.exp(mm_nt(stacked, key_ref[keys, pair]) + bias)
            share = grown * (1.0 / jnp.sum(grown, axis=-1, keepdims=True))
            grad_share = mm_nt(grads, value_ref[keys, pair])
            centre = jnp.sum(share * grad_share, axis=-1, keepdims=True)
            grad_score = (share * (grad_share - centre)).astype(BF)
            grad_query = side_by_side(mm(grad_score, key_ref[keys, pair]), head_dim) * scale
            key_term = mm_tn(grad_score, stacked)
            found.append((grad_query, key_term, mm_tn(share.astype(BF), grads)))
        for group, (grad_query, key_term, value_term) in enumerate(found):
            pair = slice(group * PAIR, (group + 1) * PAIR)
            key_sum_ref[keys, pair] += key_term
            value_sum_ref[keys, pair] += value_term
            through_norm(rows, group, grad_query, 0)

    each_block(low_ref, row_length, attend)

    def folded(sum_ref, rows):
        first = sum_ref[rows, :PAIR]
        second = sum_ref[rows, PAIR:]
        return jnp.where(
            lanes(first.shape) < head_dim,
            first + pltpu.roll(first, head_dim, 1),
            second + pltpu.roll(second, head_dim, 1),
        )

    def finish(step, carry):
        rows = pl.ds(pl.multiple_of(step * BLOCK, BLOCK), BLOCK)
        through_norm(rows, query_groups, folded(key_sum_ref, rows), 1)
        out_ref[rows, (query_groups + 1) * PAIR :] = folded(value_sum_ref, rows).astype(BF)
        return carry

    lax.fori_loop(0, row_length // BLOCK, finish, 0)


def attention_pack_kernel(
    place_ref,
    gain_ref,
    query_ref,
    key_ref,
    value_ref,
    output_ref,
    pack_ref,
    wide_ref,
    semaphore,
):
    gain = gain_ref[...].astype(BF).astype(F32)
    weights = (query_ref, key_ref, value_ref, output_ref)
    start = 0
    copies = []
    for index, weight_ref in enumerate(weights):
        size = weight_ref.shape[1] // SEQ
        column = pl.multiple_of(place_ref[0] * size, size)
        copies.append(
            pltpu.make_async_copy(
                weight_ref.at[:, pl.ds(column, size)],
                wide_ref.at[:, start : start + size],
                semaphore.at[index],
            )
        )
        copies[-1].start()
        start += size
    start = 0
    for index, weight_ref in enumerate(weights):
        size = weight_ref.shape[1] // SEQ
        copies[index].wait()
        values = wide_ref[:, start : start + size].astype(BF)
        if index < len(weights) - 1:
            values = (values.astype(F32) * gain).astype(BF)
        pack_ref[:, start : start + size] = values
        start += size


def hidden_pack_kernel(
    pieces, place_ref, gain_ref, gate_ref, up_ref, pack_ref, wide_ref, semaphore
):
    piece = gate_ref.shape[1] // (pieces * SEQ)
    here = pieces * piece
    chunk = 32
    steps = gate_ref.shape[0] // chunk
    weights = (gate_ref, up_ref)

    def copy(index, part):
        rows = pl.ds(pl.multiple_of(index * chunk, chunk), chunk)
        return pltpu.make_async_copy(
            weights[part].at[rows, :], wide_ref.at[part, rows, :], semaphore.at[part, index]
        )

    for index in range(steps):
        for part in range(2):
            copy(index, part).start()
    for place in range(SEQ):

        @pl.when(place_ref[0] == place)
        def _(place=place):
            def step(index, carry):
                rows = pl.ds(pl.multiple_of(index * chunk, chunk), chunk)
                gain = gain_ref[rows, :].astype(BF).astype(F32)
                for part in range(2):
                    copy(index, part).wait()
                    joined = jnp.concatenate(
                        [
                            wide_ref[part, rows, start : start + piece]
                            for start in range(place * piece, gate_ref.shape[1], SEQ * piece)
                        ],
                        axis=1,
                    )
                    pack_ref[rows, part * here : (part + 1) * here] = (
                        joined.astype(BF).astype(F32) * gain
                    ).astype(BF)
                return carry

            lax.fori_loop(0, steps, step, 0)


def hidden_owner_kernel(
    pieces, place_ref, sums_ref, gate_ref, up_ref, gain_ref, gate_grad_ref, up_grad_ref, terms_ref
):
    seq_count = sums_ref.shape[0]
    here = sums_ref.shape[2] // 2
    piece = here // pieces
    gain = gain_ref[...].astype(BF).astype(F32)
    total = None
    for part, (weight_ref, grad_ref) in enumerate(
        ((gate_ref, gate_grad_ref), (up_ref, up_grad_ref))
    ):
        sums = [sums_ref[seq].astype(F32) for seq in range(seq_count)]
        joined = jnp.concatenate(
            [
                sums[seq][:, part * here + step * piece : part * here + (step + 1) * piece]
                for step in range(pieces)
                for seq in range(seq_count)
            ],
            axis=1,
        )
        term = row_sums(weight_ref[...].astype(BF).astype(F32) * joined)
        total = term if total is None else total + term
        grad_ref[...] = joined * gain
    terms_ref[...] = total


def attention_owner_kernel(
    place_ref,
    s0_ref,
    s1_ref,
    s2_ref,
    s3_ref,
    query_ref,
    key_ref,
    value_ref,
    gain_ref,
    query_grad_ref,
    key_grad_ref,
    value_grad_ref,
    terms_ref,
):
    place = place_ref[0]
    gain = gain_ref[...].astype(BF).astype(F32)
    pieces = (s0_ref, s1_ref, s2_ref, s3_ref)
    rows = query_ref.shape[0]
    start = 0
    total = None
    for weight_ref, grad_ref in (
        (query_ref, query_grad_ref),
        (key_ref, key_grad_ref),
        (value_ref, value_grad_ref),
    ):
        size = weight_ref.shape[1] // len(pieces)
        for index, sums in enumerate(pieces):
            columns = pl.ds(pl.multiple_of((place ^ index) * size, size), size)
            values = sums[:rows, start : start + size].astype(F32)
            weight = weight_ref[:, columns].astype(BF).astype(F32)
            term = row_sums(weight * values)
            total = term if total is None else total + term
            grad_ref[:, columns] = values * gain
        start += size
    terms_ref[...] = total


def row_sums(values):
    ones = jnp.ones((8, values.shape[1]), BF)
    high = values.astype(BF)
    rest = (values - high.astype(F32)).astype(BF)
    return (mm_nt(ones, high) + mm_nt(ones, rest))[:1]


def placed_call(kernel, results, place_array, operands, blocks, vmem, flops=0, moved=0):
    return pl.pallas_call(
        kernel,
        out_shape=[jax.ShapeDtypeStruct(shape, kind) for shape, kind in results],
        grid_spec=pltpu.PrefetchScalarGridSpec(
            num_scalar_prefetch=1,
            grid=(1,),
            in_specs=[pl.BlockSpec(shape, index) for shape, index in blocks],
            out_specs=[
                pl.BlockSpec(shape, lambda i, place, rank=len(shape): (0,) * rank)
                for shape, _ in results
            ],
        ),
        compiler_params=pltpu.CompilerParams(vmem_limit_bytes=vmem * MEGA),
        cost_estimate=cost(kernel, flops),
    )(place_array, *operands)


def own_rows_block(i, place):
    return (place[0], 0)


def everything(i, place):
    return (0, 0)


MICROSECONDS = {
    "attention_pack_kernel": 2.6,
    "hidden_pack_kernel": 4.2,
    "columns_kernel": 2.6,
    "project_kernel": 9.5,
    "attend_kernel": 7.0,
    "middle_kernel": 5.0,
    "hidden_kernel": 9.0,
    "hidden_grad_kernel": 5.4,
    "output_grad_kernel": 3.0,
    "back_kernel": 15.6,
    "hidden_owner_kernel": 3.1,
    "attention_owner_kernel": 1.9,
}


def cost(kernel, flops):
    name = getattr(kernel, "func", kernel).__name__
    time = MICROSECONDS.get(name, flops * 2.0e-9 + 0.5) * 0.5
    return pl.CostEstimate(flops=int(time * 1.15e9), bytes_accessed=0, transcendentals=0)


def call(
    kernel, results, scalar_count, operands, vmem, pieces=(), scratch=(), flops=0, moved=0
):
    return pl.pallas_call(
        kernel,
        out_shape=[jax.ShapeDtypeStruct(shape, kind) for shape, kind in results],
        in_specs=scalars(scalar_count)
        + whole_vmem(len(operands) - scalar_count)
        + [pl.BlockSpec(memory_space=pltpu.HBM)] * len(pieces),
        out_specs=whole_vmem(len(results)),
        scratch_shapes=list(scratch),
        compiler_params=pltpu.CompilerParams(vmem_limit_bytes=vmem * MEGA),
        cost_estimate=cost(kernel, flops),
    )(*operands, *pieces)


def block_call(kernel, results, scalar_arrays, operands, vmem, pieces, scratch, flops, moved):
    return pl.pallas_call(
        kernel,
        out_shape=[jax.ShapeDtypeStruct(shape, kind) for shape, kind, _, _ in results],
        grid_spec=pltpu.PrefetchScalarGridSpec(
            num_scalar_prefetch=len(scalar_arrays),
            grid=(4,),
            in_specs=[pl.BlockSpec(shape, index) for _, shape, index in operands]
            + [pl.BlockSpec(memory_space=pltpu.HBM)] * len(pieces),
            out_specs=[pl.BlockSpec(shape, index) for _, _, shape, index in results],
            scratch_shapes=list(scratch),
        ),
        compiler_params=pltpu.CompilerParams(vmem_limit_bytes=vmem * MEGA),
        cost_estimate=cost(kernel, flops),
    )(*scalar_arrays, *(array for array, _, _ in operands), *pieces)


def row_block(step, *scalar_refs):
    return (step, 0)


def half_block(step, *scalar_refs):
    return (step // 2, 0)


def first_block(step, *scalar_refs):
    return (0, 0)


def ordered_block(step, order_ref, *scalar_refs):
    return (order_ref[step], 0)


def split_product(left, right_shape, offsets, pieces, transposed, order):
    rows = left.shape[0] // 4
    width = right_shape[0] if transposed else right_shape[1]
    return block_call(
        functools.partial(split_kernel, transposed),
        [
            ((2 * rows, width), F32, (rows, width), half_block),
            ((2 * rows, width), BF, (rows, width), half_block),
        ],
        (order, offsets),
        [(left, (rows, left.shape[1]), ordered_block)],
        20,
        pieces,
        [pltpu.VMEM(right_shape, BF), pltpu.SemaphoreType.DMA((1, len(pieces)))],
        2 * left.shape[0] * left.shape[1] * width,
        2 * (left.size + right_shape[0] * right_shape[1]) + 6 * left.shape[0] * width,
    )


def swap(values, bit):
    count = lax.axis_size("seq")
    return lax.ppermute(values, "seq", [(i, i ^ bit) for i in range(count)])


def seq_pieces(values):
    far = swap(values, 2)
    near = swap(values, 1)
    return (values, near, far, swap(far, 1))


def after(values, *others):
    return lax.optimization_barrier((values, others))[0]


def ring_length():
    count = lax.axis_size("dp")
    return count if count % 2 == 0 and 4 <= count <= 8 else 0


def ring_order(count):
    return list(range(0, count, 2)) + list(range(count - 1, 0, -2))


def ring_sources(offsets):
    count = lax.axis_size("dp")
    place = lax.axis_index("dp")
    spot = jnp.where(place % 2 == 0, place // 2, count - 1 - place // 2)
    spot = (spot + jnp.asarray(offsets, jnp.int32) + count) % count
    return jnp.where(spot < count // 2, 2 * spot, 2 * (count - 1 - spot) + 1)


def ring_source(offset):
    count = lax.axis_size("dp")
    place = lax.axis_index("dp")
    spot = jnp.where(place % 2 == 0, place // 2, count - 1 - place // 2)
    spot = (spot + offset + count) % count
    return jnp.where(spot < count // 2, 2 * spot, 2 * (count - 1 - spot) + 1)


def ring_move(values, step):
    count = lax.axis_size("dp")
    order = ring_order(count)
    return lax.ppermute(
        values, "dp", [(order[i], order[(i + step) % count]) for i in range(count)]
    )


def half_of(rows):
    return rows // 32 * 16 or rows // 2


class GatherRing:
    def __init__(self, shard, long=1, leads=False):
        count = ring_length()
        self.rows = shard.shape[0]
        self.steps = count // 2
        self.pieces = [shard]
        self.spots = [0]
        self.flying = {}
        self.sent = ()
        if not count:
            self.pieces = [lax.all_gather(shard, "dp", axis=0, tiled=True)]
            return
        self.long = long
        self.leads = leads
        self.taken = 0
        self.flying = {1: shard, -1: shard}

    def step(self, *others):
        if not self.steps:
            return others
        self.flying, others = lax.optimization_barrier((self.flying, others))
        self.taken += 1
        ways = [self.long]
        if (self.taken > 1) if self.leads else (self.taken < self.steps):
            ways.append(-self.long)
        self.sent = tuple(self.flying[way] for way in ways)
        for way in ways:
            self.flying[way] = ring_move(self.flying[way], way)
            self.pieces.append(self.flying[way])
            lag = self.leads and way != self.long
            self.spots.append(-way * (self.taken - int(lag)))
        return others

    def arrived(self):
        return self.flying

    @property
    def offsets(self):
        if not self.steps:
            return jnp.zeros((1,), jnp.int32)
        return ring_sources(self.spots) * self.rows


class ScatterRing:
    def __init__(self, terms, halved=False):
        self.count = ring_length()
        self.halved = halved
        self.terms = terms
        self.flying = {}
        if not self.count:
            size = lax.axis_size("dp")
            parts = [term.reshape(size, -1, term.shape[1]) for term in terms]
            whole = self.joined(parts)
            self.sums = lax.psum_scatter(
                whole.reshape(-1, whole.shape[-1]).astype(BF), "dp", scatter_dimension=0, tiled=True
            ).astype(F32)
            self.steps = 0
            self.sent = ()
            return
        self.steps = self.count // 2
        self.taken = 0
        self.sent = ()

    def joined(self, parts):
        return parts[0] if len(parts) == 1 else jnp.concatenate(parts, axis=-2)

    def term(self, offset):
        parts = []
        for term in self.terms:
            rows = term.shape[0] // self.count
            parts.append(lax.dynamic_slice_in_dim(term, ring_source(offset) * rows, rows, 0))
        return self.joined(parts).astype(F32)

    def step(self, *others):
        if not self.steps:
            return others
        self.taken += 1
        left = self.steps + 1 - self.taken
        if self.taken == 1:
            self.terms, others = lax.optimization_barrier((self.terms, others))
            far = self.term(self.steps)
            half = half_of(far.shape[0])
            values = {1: far[:half], -1: far[half:]} if self.halved else {1: far}
        else:
            self.flying, others = lax.optimization_barrier((self.flying, others))
            values = {way: self.term(way * left) for way in (1, -1)}
            if self.taken == 2 and self.halved:
                up, down = (self.flying[1].astype(F32), self.flying[-1].astype(F32))
                half = up.shape[0]
                values = {
                    1: jnp.concatenate([values[1][:half] + up, values[1][half:]]),
                    -1: jnp.concatenate([values[-1][:half], values[-1][half:] + down]),
                }
            else:
                for way, arrived in self.flying.items():
                    values[way] = values[way] + arrived.astype(F32)
        sent = {way: value.astype(BF) for way, value in values.items()}
        self.sent = tuple(sent.values())
        self.flying = {way: ring_move(value, way) for way, value in sent.items()}
        return others

    def arrived(self):
        return self.flying

    def take(self, arrived):
        self.flying = arrived

    def result(self):
        if not self.steps:
            return self.sums
        return self.term(0) + self.flying[1].astype(F32) + self.flying[-1].astype(F32)


def local(
    tokens,
    segments,
    valid_mask,
    attention_gain,
    query_weight,
    key_weight,
    value_weight,
    query_gain,
    key_gain,
    output_weight,
    feedforward_gain,
    gate_weight,
    up_weight,
    down_weight,
    cotangent,
):
    seq_count = lax.axis_size("seq")
    dp_count = lax.axis_size("dp")
    place = lax.axis_index("seq")
    local_rows = tokens.shape[1]
    row_length = segments.shape[1]
    head_dim = query_gain.shape[0]
    width = tokens.shape[2]
    hidden_width = gate_weight.shape[1]
    query_width = query_weight.shape[1]
    key_width = key_weight.shape[1]
    query_here = query_width // seq_count
    key_here = key_width // seq_count
    hidden_here = hidden_width // seq_count
    weight_rows = query_weight.shape[0]
    own_rows = weight_rows // seq_count
    segment_row = segments[0]
    valid_row = valid_mask[0]

    def low(weight):
        return weight.astype(BF).astype(F32)

    place_array = place.astype(jnp.int32).reshape(1)
    gain_one = attention_gain[:, None]
    gain_two = feedforward_gain[:, None]
    qkv_width = query_here + 2 * key_here
    piece = hidden_width // (dp_count * seq_count)
    kernels_fit = weight_rows % 32 == 0 and own_rows % 8 == 0 and dp_count <= 8

    pack_width = qkv_width + width // seq_count
    (attention_pack,) = call(
        attention_pack_kernel,
        [((weight_rows, pack_width), BF)],
        1,
        (place_array, gain_one),
        58,
        pieces=(query_weight, key_weight, value_weight, output_weight),
        scratch=[pltpu.VMEM((weight_rows, pack_width), F32), pltpu.SemaphoreType.DMA((4,))],
        moved=8 * weight_rows * width,
    )
    if kernels_fit:
        (gate_up_pack,) = call(
            functools.partial(hidden_pack_kernel, dp_count),
            [((weight_rows, 2 * hidden_here), BF)],
            1,
            (place_array, after(gain_two, attention_pack)),
            58,
            pieces=(gate_weight, up_weight),
            scratch=[
                pltpu.VMEM((2, weight_rows, hidden_width), F32),
                pltpu.SemaphoreType.DMA((2, weight_rows // 32)),
            ],
            moved=8 * weight_rows * hidden_width,
        )
    else:

        def hidden_columns(weight):
            split = weight.reshape(weight_rows, dp_count, seq_count, piece)
            mine = lax.dynamic_index_in_dim(split, place, 2, keepdims=False)
            return (low(mine.reshape(weight_rows, hidden_here)) * low(gain_two)).astype(BF)

        gate_up_pack = jnp.concatenate(
            [hidden_columns(gate_weight), hidden_columns(up_weight)], axis=1
        )
    down_pack = lax.dynamic_slice_in_dim(down_weight, place * piece, piece, 0).astype(BF)
    down_pack = after(down_pack, attention_pack)

    order = place ^ jnp.arange(4, dtype=jnp.int32)
    plain = jnp.arange(4, dtype=jnp.int32)

    token_far = swap(tokens[0], 2)
    token_near = swap(tokens[0], 1)
    attention_ring = GatherRing(attention_pack)
    attention_ring.step()
    positions = doc_positions(segment_row)
    starts = jnp.arange(row_length, dtype=jnp.int32) - positions
    cos_wide, sin_wide = rope_tables(positions, head_dim)
    repeats = PAIR // head_dim
    head_gains = jnp.tile(jnp.stack([query_gain, key_gain]), (1, repeats))
    row_starts = starts[:, None]
    usable = valid_row[None, :]
    starts, row_starts, head_gains = attention_ring.step(starts, row_starts, head_gains)
    block_lows = starts[::BLOCK]
    token_far, cos_wide, sin_wide = attention_ring.step(token_far, cos_wide, sin_wide)
    token_pieces = (tokens[0], token_near, token_far, swap(token_far, 1))
    grad_far = swap(after(cotangent[0], token_far), 2)
    grad_near = swap(after(cotangent[0], token_far), 1)
    (gate_up_pack,) = attention_ring.step(gate_up_pack)

    gate_up_ring = GatherRing(after(gate_up_pack, attention_ring.arrived()))
    (grad_far,) = gate_up_ring.step(grad_far)
    grad_row_pieces = (cotangent[0], grad_near, grad_far, swap(grad_far, 1))
    (output_columns,) = pl.pallas_call(
        functools.partial(columns_kernel, qkv_width),
        out_shape=[jax.ShapeDtypeStruct((query_width, width // seq_count), BF)],
        in_specs=scalars(1) + [pl.BlockSpec(memory_space=pltpu.HBM)] * len(attention_ring.pieces),
        out_specs=whole_vmem(1),
        scratch_shapes=[pltpu.SemaphoreType.DMA((1, len(attention_ring.pieces)))],
        compiler_params=pltpu.CompilerParams(vmem_limit_bytes=58 * MEGA),
        cost_estimate=cost(columns_kernel, 0),
    )(attention_ring.offsets, *attention_ring.pieces)
    output_far = swap(output_columns, 2)
    output_near = swap(output_columns, 1)
    projected = call(
        functools.partial(project_kernel, head_dim),
        [
            ((row_length, width), BF),
            ((row_length, query_here + key_here), F32),
            ((row_length, query_here), BF),
            ((row_length, 2 * key_here), BF),
            ((row_length, 2 * key_here), BF),
            ((width, qkv_width), BF),
        ],
        2,
        (place_array, attention_ring.offsets, *token_pieces, cos_wide, sin_wide, head_gains),
        58,
        pieces=attention_ring.pieces,
        scratch=[pltpu.SemaphoreType.DMA((1, len(attention_ring.pieces)))],
        flops=2 * row_length * width * qkv_width,
        moved=12 * row_length * width,
    )
    projected, output_far = gate_up_ring.step(projected, output_far)
    output_pieces = (output_columns, output_near, output_far, swap(output_far, 1))
    unit_one, raw, queries, keys_two, values_two, qkv_weight = projected
    (mixed_here,) = call(
        functools.partial(attend_kernel, head_dim),
        [((row_length, query_here), BF)],
        1,
        (block_lows, queries, keys_two, values_two, row_starts, usable),
        58,
        flops=row_length * width * qkv_width,
        moved=4 * row_length * width,
    )
    mixed_far = swap(mixed_here, 2)
    mixed_near = swap(mixed_here, 1)
    gate_up_ring.step(mixed_here)
    (mixed_far,) = gate_up_ring.step(mixed_far)
    down_ring = GatherRing(after(down_pack, mixed_far), -1, True)
    down_ring.step()
    mixed_pieces = (mixed_here, mixed_near, mixed_far, swap(mixed_far, 1))
    unit_two, after_here = call(
        middle_kernel,
        [((row_length, width), BF), ((local_rows, width), F32)],
        1,
        (place_array, *token_pieces, *mixed_pieces, *output_pieces),
        18,
        scratch=[pltpu.VMEM((local_rows, width), F32)],
        flops=2 * row_length * width * width,
        moved=10 * row_length * width,
    )
    (unit_two,) = down_ring.step(unit_two)

    rows_each = row_length // 4
    hidden, gate_factor, up_factor = block_call(
        hidden_kernel,
        [((row_length, hidden_here), BF, (rows_each, hidden_here), row_block)] * 3,
        (gate_up_ring.offsets,),
        [(unit_two, (rows_each, width), row_block)],
        28,
        gate_up_ring.pieces,
        [
            pltpu.VMEM((width, 2 * hidden_here), BF),
            pltpu.SemaphoreType.DMA((1, len(gate_up_ring.pieces))),
        ],
        4 * row_length * width * hidden_here,
        8 * row_length * hidden_here + 4 * width * hidden_here,
    )
    hidden, gate_factor, up_factor = down_ring.step(hidden, gate_factor, up_factor)
    grad_rows = jnp.concatenate(grad_row_pieces)
    down_scatter = ScatterRing([mm_tn(hidden, grad_rows)])
    (down_scatter.terms,) = down_ring.step(down_scatter.terms)
    down_scatter.step()
    gate_up_grad, down_all = block_call(
        hidden_grad_kernel,
        [
            ((row_length, 2 * hidden_here), BF, (rows_each, 2 * hidden_here), row_block),
            ((hidden_here, width), BF, (hidden_here, width), first_block),
        ],
        (down_ring.offsets,),
        [
            (grad_rows, (rows_each, width), row_block),
            (gate_factor, (rows_each, hidden_here), row_block),
            (up_factor, (rows_each, hidden_here), row_block),
        ],
        24,
        down_ring.pieces,
        [pltpu.SemaphoreType.DMA((1, len(down_ring.pieces)))],
        2 * row_length * width * hidden_here,
        8 * row_length * hidden_here + 4 * width * hidden_here,
    )

    (gate_up_grad,) = down_scatter.step(gate_up_grad)
    keep, send = split_product(
        gate_up_grad, (width, 2 * hidden_here), gate_up_ring.offsets, gate_up_ring.pieces, True, plain
    )
    keep, send = down_scatter.step(keep, send)

    def halves(keep, near):
        return (
            keep[:local_rows] + near[:local_rows].astype(F32),
            (keep[local_rows:] + near[local_rows:].astype(F32)).astype(BF),
        )

    half_sum, half_send = halves(keep, swap(send, 1))
    half_send, unit_two = lax.optimization_barrier((half_send, unit_two))
    arrived = swap(half_send, 2)
    gate_up_scatter = ScatterRing([mm_tn(unit_two, gate_up_grad).astype(BF)], True)
    gate_up_scatter.step()
    unit_here, factor_here = rms_stats(after_here)
    grad_after = cotangent[0].astype(F32) + rms_back(
        half_sum + arrived.astype(F32), unit_here, factor_here
    )
    branch = grad_after.astype(BF)
    branch_far = swap(branch, 2)
    branch_near = swap(branch, 1)
    gate_up_scatter.step(branch)
    keep, send = split_product(
        after(hidden, branch, gate_up_scatter.sent),
        (hidden_here, width),
        jnp.zeros((1,), jnp.int32),
        [down_all],
        False,
        plain,
    )
    keep, send, branch_far = gate_up_scatter.step(keep, send, branch_far)
    down_scatter.step(branch_far)
    branch_pieces = (branch, branch_near, branch_far, swap(branch_far, 1))
    half_sum, half_send = halves(keep, swap(send, 1))
    chunk_rows = query_width // (dp_count * seq_count)
    grad_mixed, output_terms = call(
        functools.partial(output_grad_kernel, chunk_rows),
        [
            ((row_length, query_here), BF),
            ((query_here * width // qkv_width, qkv_width), F32),
        ],
        1,
        (place_array, *branch_pieces, mixed_here, *output_pieces),
        14,
        scratch=[pltpu.VMEM((query_here, width), F32)],
        flops=4 * row_length * width * query_here,
        moved=8 * row_length * width,
    )

    grad_mixed, half_send = gate_up_scatter.step(grad_mixed, half_send)
    arrived = swap(half_send, 2)
    qkv_grad, gain_terms = call(
        functools.partial(back_kernel, head_dim),
        [((row_length, qkv_width), BF), ((8, PAIR), F32)],
        1,
        (block_lows, after(grad_mixed, gate_up_scatter.sent), queries, keys_two, values_two, raw)
        + (cos_wide, sin_wide, head_gains, row_starts, usable),
        24,
        scratch=[pltpu.VMEM((row_length, 2 * key_here), F32)] * 2,
        flops=4 * row_length * width * qkv_width,
        moved=12 * row_length * width,
    )
    qkv_grad, gain_terms, arrived, gate_up_arrived, down_arrived = lax.optimization_barrier(
        (qkv_grad, gain_terms, arrived, gate_up_scatter.arrived(), down_scatter.arrived())
    )
    down_scatter.take(down_arrived)
    gate_up_scatter.take(gate_up_arrived)
    layer_out = (after_here + half_sum + arrived.astype(F32)).astype(BF)
    gain_rows = jnp.concatenate([gain_terms[0:1], gain_terms[1:2]], axis=1)
    gain_rows = jnp.pad(gain_rows, ((0, 15), (0, qkv_width - 2 * PAIR)))
    packed = jnp.concatenate(
        [
            mm_tn(unit_one, qkv_grad).reshape(dp_count, weight_rows, qkv_width),
            output_terms.reshape(dp_count, -1, qkv_width),
            jnp.broadcast_to(gain_rows, (dp_count, *gain_rows.shape)),
        ],
        axis=1,
    )
    attention_scatter = ScatterRing([packed.reshape(-1, qkv_width)])
    attention_scatter.step()
    gate_up_scatter.take(after(gate_up_scatter.arrived(), attention_scatter.sent))
    gate_up_sums = gate_up_scatter.result().astype(BF)
    keep, send = split_product(
        after(qkv_grad, gate_up_sums),
        (width, qkv_width),
        jnp.zeros((1,), jnp.int32),
        [qkv_weight],
        True,
        order,
    )
    keep, send = attention_scatter.step(keep, send)
    gate_up_sums = after(gate_up_sums, attention_scatter.sent)
    hidden_own = lax.all_to_all(
        gate_up_sums.reshape(seq_count, own_rows, -1), "seq", split_axis=0, concat_axis=0, tiled=True
    )
    half_sum, half_send = halves(keep, swap(send, 1))
    (half_send,) = attention_scatter.step(half_send)
    arrived = swap(half_send, 2)
    for _ in range(attention_scatter.steps - 3):
        (arrived,) = attention_scatter.step(arrived)
        hidden_own = after(hidden_own, attention_scatter.sent)
    unit_tokens, factor_tokens = rms_stats(tokens[0].astype(F32))
    token_grad = (
        grad_after + rms_back(half_sum + arrived.astype(F32), unit_tokens, factor_tokens)
    ).astype(BF)

    down_sums = down_scatter.result()
    attention_sums = attention_scatter.result().astype(BF)
    qkv_sums = attention_sums[:weight_rows]
    output_sums = jnp.concatenate(
        [
            attention_sums[weight_rows + part * chunk_rows : weight_rows + (part + 1) * chunk_rows]
            for part in range(width // qkv_width)
        ],
        axis=1,
    )

    def own(weight):
        return lax.dynamic_slice_in_dim(weight, place * own_rows, own_rows, 0)

    gain_row = attention_sums[-16:]
    qkv_pieces = []
    for bits in range(4):
        part = lax.dynamic_slice_in_dim(qkv_sums, (place ^ bits) * own_rows, own_rows, 0)
        part = after(jnp.concatenate([part, gain_row]), arrived)
        qkv_pieces.append(swap(part, bits) if bits else part)
    gain_sums = sum(piece[own_rows : own_rows + 1].astype(F32) for piece in qkv_pieces)
    gain_sums = jnp.sum(gain_sums[0, : 2 * PAIR].reshape(2, repeats, head_dim), axis=1)
    if kernels_fit:
        gate_grad, up_grad, feed_gain_grad = placed_call(
            functools.partial(hidden_owner_kernel, dp_count),
            [((own_rows, hidden_width), F32)] * 2 + [((1, own_rows), F32)],
            place_array,
            (hidden_own, gate_weight, up_weight, gain_two),
            [
                (hidden_own.shape, lambda i, place: (0, 0, 0)),
                ((own_rows, hidden_width), own_rows_block),
                ((own_rows, hidden_width), own_rows_block),
                ((own_rows, 1), own_rows_block),
            ],
            58,
            moved=20 * own_rows * hidden_width,
        )
        query_grad, key_grad, value_grad, attention_gain_grad = placed_call(
            attention_owner_kernel,
            [((own_rows, query_width), F32)]
            + [((own_rows, key_width), F32)] * 2
            + [((1, own_rows), F32)],
            place_array,
            (*qkv_pieces, query_weight, key_weight, value_weight, gain_one),
            [((own_rows + 16, qkv_width), everything)] * 4
            + [
                ((own_rows, query_width), own_rows_block),
                ((own_rows, key_width), own_rows_block),
                ((own_rows, key_width), own_rows_block),
                ((own_rows, 1), own_rows_block),
            ],
            58,
            moved=20 * own_rows * query_width,
        )
    else:
        spread = jnp.stack(qkv_pieces)[order, :own_rows].astype(F32)

        def joined(first, size):
            return jnp.swapaxes(spread[:, :, first : first + size], 0, 1).reshape(own_rows, -1)

        query_own = joined(0, query_here)
        key_own = joined(query_here, key_here)
        value_own = joined(query_here + key_here, key_here)
        attention_gain_grad = (
            jnp.sum(own(low(query_weight)) * query_own, axis=1)
            + jnp.sum(own(low(key_weight)) * key_own, axis=1)
            + jnp.sum(own(low(value_weight)) * value_own, axis=1)
        )
        gain_own = own(low(gain_one))
        query_grad, key_grad, value_grad = (
            query_own * gain_own,
            key_own * gain_own,
            value_own * gain_own,
        )
        hidden_own = hidden_own.reshape(seq_count, own_rows, 2, dp_count, piece)
        hidden_own = jnp.transpose(hidden_own, (2, 1, 3, 0, 4))
        hidden_own = hidden_own.reshape(2, own_rows, hidden_width).astype(F32)
        feed_gain_grad = jnp.sum(own(low(gate_weight)) * hidden_own[0], axis=1) + jnp.sum(
            own(low(up_weight)) * hidden_own[1], axis=1
        )
        gain_own = own(low(gain_two))
        gate_grad, up_grad = (hidden_own[0] * gain_own, hidden_own[1] * gain_own)

    moves = [
        (dp * seq_count + seq, seq * dp_count + dp)
        for dp in range(dp_count)
        for seq in range(seq_count)
    ]
    output_own = lax.ppermute(output_sums, ("dp", "seq"), moves).astype(F32)

    return (
        layer_out.reshape(1, local_rows, -1),
        token_grad.reshape(1, local_rows, -1),
        attention_gain_grad.reshape(own_rows),
        query_grad,
        key_grad,
        value_grad,
        gain_sums[0],
        gain_sums[1],
        output_own,
        feed_gain_grad.reshape(own_rows),
        gate_grad,
        up_grad,
        down_sums,
    )


def solution(mesh):
    in_specs = (
        P("dp", "seq", None),
        P("dp", None),
        P("dp", None),
        P("dp"),
        P("dp", None),
        P("dp", None),
        P("dp", None),
        P(),
        P(),
        P("dp", None),
        P("dp"),
        P("dp", None),
        P("dp", None),
        P("dp", None),
        P("dp", "seq", None),
    )
    out_specs = (
        P("dp", "seq", None),
        P("dp", "seq", None),
        P(("dp", "seq")),
        P(("dp", "seq"), None),
        P(("dp", "seq"), None),
        P(("dp", "seq"), None),
        P(),
        P(),
        P(("dp", "seq"), None),
        P(("dp", "seq")),
        P(("dp", "seq"), None),
        P(("dp", "seq"), None),
        P(("dp", "seq"), None),
    )
    return jax.shard_map(local, mesh=mesh, in_specs=in_specs, out_specs=out_specs, check_vma=False)
```

```python
import functools
import math

import jax
import jax.numpy as jnp
from jax import lax
from jax.experimental import pallas as pl
from jax.experimental.pallas import tpu as pltpu
from jax.sharding import PartitionSpec as P

EPS = 1e-05
ROPE_BASE = 1000000.0
NEG_FILL = -1e30
BF = jnp.bfloat16
F32 = jnp.float32
BLOCK = 128
PAIR = 128
SEQ = 4
MEGA = 1024 * 1024


def dot(left, right, dims):
    return lax.dot_general(left, right, (dims, ((), ())), preferred_element_type=F32)


def mm(left, right):
    return dot(left, right, ((1,), (0,)))


def mm_nt(left, right):
    return dot(left, right, ((1,), (1,)))


def mm_tn(left, right):
    return dot(left, right, ((0,), (0,)))


def rms_stats(values):
    factor = lax.rsqrt(jnp.mean(values * values, axis=-1, keepdims=True) + EPS)
    return (values * factor, factor)


def rms_back(grad_unit, unit_values, factor):
    return factor * (
        grad_unit - unit_values * jnp.mean(grad_unit * unit_values, axis=-1, keepdims=True)
    )


def doc_positions(segment_row):
    length = segment_row.shape[0]
    places = jnp.arange(length, dtype=jnp.int32)
    change = jnp.concatenate([jnp.ones((1,), dtype=jnp.bool_), segment_row[1:] != segment_row[:-1]])
    starts = lax.cummax(jnp.where(change, places, jnp.zeros_like(places)), axis=0)
    return places - starts


def rope_tables(positions, head_dim):
    half = head_dim // 2
    lane = jnp.arange(PAIR, dtype=jnp.int32)
    frequency = ROPE_BASE ** (-(lane % half).astype(F32) / half)
    angles = positions.astype(F32)[:, None] * frequency[None, :]
    sign = jnp.where(lane % head_dim < half, -1.0, 1.0)
    return (jnp.cos(angles), jnp.sin(angles) * sign[None, :])


def whole_vmem(count):
    return [pl.BlockSpec(memory_space=pltpu.VMEM)] * count


def scalars(count):
    return [pl.BlockSpec(memory_space=pltpu.SMEM)] * count


def lanes(shape):
    return lax.broadcasted_iota(jnp.int32, shape, 1)


def head_means(values, head_dim):
    width = values.shape[1]
    row = lax.broadcasted_iota(jnp.int32, (width, width), 0) // head_dim
    column = lax.broadcasted_iota(jnp.int32, (width, width), 1) // head_dim
    spread = jnp.where(row == column, 1.0 / head_dim, 0.0).astype(BF)
    high = values.astype(BF)
    rest = (values - high.astype(F32)).astype(BF)
    return mm(high, spread) + mm(rest, spread)


def half_partner(values, head_dim):
    half = head_dim // 2
    width = values.shape[1]
    upper = (lanes(values.shape) % head_dim) >= half
    return jnp.where(
        upper, pltpu.roll(values, half, 1), pltpu.roll(values, width - half, 1)
    )


def stacked_heads(pair, head_dim):
    first = lanes(pair.shape) < head_dim
    zero = jnp.zeros_like(pair)
    return jnp.concatenate([jnp.where(first, pair, zero), jnp.where(first, zero, pair)], axis=0)


def side_by_side(stacked, head_dim):
    rows = stacked.shape[0] // 2
    return jnp.where(
        lanes((rows, stacked.shape[1])) < head_dim, stacked[:rows], stacked[rows:]
    )


def mask_bias(start_ref, usable_ref, first_row, first_key, rows, window):
    row = first_row + lax.broadcasted_iota(jnp.int32, (rows, window), 0)
    key = first_key + lax.broadcasted_iota(jnp.int32, (rows, window), 1)
    start = start_ref[pl.ds(first_row, rows), :]
    usable = usable_ref[:, pl.ds(first_key, window)] > 0
    allowed = ((key >= start) & (key <= row) & usable) | (key == row)
    bias = jnp.where(allowed, 0.0, NEG_FILL)
    return jnp.concatenate([bias, bias], axis=0)


def each_block(low_ref, row_length, body):
    long_window = min(5 * BLOCK, row_length)

    def step(index, carry):
        first_row = pl.multiple_of(index * BLOCK, BLOCK)
        short_key = jnp.maximum(first_row - BLOCK, 0)
        is_short = low_ref[index] >= short_key

        @pl.when(is_short)
        def _():
            body(first_row, pl.multiple_of(short_key, BLOCK), 2 * BLOCK)

        @pl.when(jnp.logical_not(is_short))
        def _():
            long_key = jnp.maximum(first_row + BLOCK - long_window, 0)
            body(first_row, pl.multiple_of(long_key, BLOCK), long_window)

        return carry

    lax.fori_loop(0, row_length // BLOCK, step, 0)


def load_pieces(offset_ref, piece_refs, semaphore, *targets):
    copies = []
    for index, piece in enumerate(piece_refs):
        start = pl.multiple_of(offset_ref[index], 16)
        for part, (target, column) in enumerate(targets):
            rows = pl.ds(start, piece.shape[0])
            copies.append(
                pltpu.make_async_copy(
                    piece.at[:, column : column + target.shape[1]],
                    target.at[rows, :],
                    semaphore.at[part, index],
                )
            )
    for copy in copies:
        copy.start()

    def wait():
        for copy in copies:
            copy.wait()

    return wait


def columns_kernel(column, offset_ref, *rest):
    (*piece_refs, out_ref, semaphore) = rest
    load_pieces(offset_ref, piece_refs, semaphore, (out_ref, column))()


def project_kernel(
    head_dim,
    place_ref,
    offset_ref,
    x0_ref,
    x1_ref,
    x2_ref,
    x3_ref,
    cos_ref,
    sin_ref,
    gain_ref,
    *rest,
):
    (*piece_refs, unit_ref, raw_ref, query_ref, key_ref, value_ref, weight_ref) = rest[:-1]
    semaphore = rest[-1]
    wait = load_pieces(offset_ref, piece_refs, semaphore, (weight_ref, 0))
    place = place_ref[0]
    rows_each = x0_ref.shape[0]
    row_length = unit_ref.shape[0]
    query_groups = query_ref.shape[1] // PAIR
    for index, piece in enumerate((x0_ref, x1_ref, x2_ref, x3_ref)):

        def normalize(step, carry, piece=piece, base=(place ^ index) * rows_each):
            start = pl.multiple_of(step * BLOCK, BLOCK)
            values = piece[pl.ds(start, BLOCK), :].astype(F32)
            factor = lax.rsqrt(jnp.mean(values * values, axis=-1, keepdims=True) + EPS)
            rows = pl.ds(pl.multiple_of(base + start, BLOCK), BLOCK)
            unit_ref[rows, :] = (values * factor).astype(BF)
            return carry

        lax.fori_loop(0, rows_each // BLOCK, normalize, 0)
    wait()

    def project(step, carry):
        rows = pl.ds(pl.multiple_of(step * rows_each, rows_each), rows_each)
        raw = mm(unit_ref[rows, :], weight_ref[...])
        raw_ref[rows, :] = raw[:, : raw_ref.shape[1]]
        cos = cos_ref[rows, :]
        sin = sin_ref[rows, :]
        for group in range(query_groups + 1):
            is_key = group == query_groups
            values = raw[:, group * PAIR : (group + 1) * PAIR]
            factor = lax.rsqrt(head_means(values * values, head_dim) + EPS)
            scaled = values * factor * gain_ref[int(is_key) : int(is_key) + 1, :]
            turned = scaled * cos + half_partner(scaled, head_dim) * sin
            if is_key:
                crossed = pltpu.roll(turned, head_dim, 1)
                first = lanes(turned.shape) < head_dim
                key_ref[rows, :PAIR] = jnp.where(first, turned, crossed).astype(BF)
                key_ref[rows, PAIR:] = jnp.where(first, crossed, turned).astype(BF)
                values = raw[:, (group + 1) * PAIR :]
                crossed = pltpu.roll(values, head_dim, 1)
                value_ref[rows, :PAIR] = jnp.where(first, values, crossed).astype(BF)
                value_ref[rows, PAIR:] = jnp.where(first, crossed, values).astype(BF)
            else:
                query_ref[rows, group * PAIR : (group + 1) * PAIR] = (
                    turned * (1.0 / math.sqrt(head_dim))
                ).astype(BF)
        return carry

    lax.fori_loop(0, row_length // rows_each, project, 0)


def attend_kernel(
    head_dim, low_ref, query_ref, key_ref, value_ref, start_ref, usable_ref, mixed_ref
):
    row_length = query_ref.shape[0]
    query_groups = query_ref.shape[1] // PAIR

    def attend(first_row, first_key, window):
        bias = mask_bias(start_ref, usable_ref, first_row, first_key, BLOCK, window)
        rows = pl.ds(first_row, BLOCK)
        keys = pl.ds(first_key, window)
        found = []
        for group in range(query_groups):
            pair = slice(group * PAIR, (group + 1) * PAIR)
            stacked = stacked_heads(query_ref[rows, pair], head_dim)
            grown = jnp.exp(mm_nt(stacked, key_ref[keys, pair]) + bias)
            mixed = mm(grown.astype(BF), value_ref[keys, pair])
            mixed = mixed * (1.0 / jnp.sum(grown, axis=-1, keepdims=True))
            found.append(side_by_side(mixed, head_dim).astype(BF))
        mixed_ref[rows, :] = jnp.concatenate(found, axis=1)

    each_block(low_ref, row_length, attend)


def middle_kernel(
    place_ref,
    x0_ref,
    x1_ref,
    x2_ref,
    x3_ref,
    o0_ref,
    o1_ref,
    o2_ref,
    o3_ref,
    w0_ref,
    w1_ref,
    w2_ref,
    w3_ref,
    unit_ref,
    here_ref,
    sum_ref,
):
    place = place_ref[0]
    rows_each, width = x0_ref.shape
    heads = o0_ref.shape[1]
    columns = w0_ref.shape[1]
    for index, piece in enumerate((x0_ref, x1_ref, x2_ref, x3_ref)):
        base = pl.multiple_of((place ^ index) * rows_each, rows_each)
        rows = pl.ds(base, rows_each)
        for part, weight in enumerate((w0_ref, w1_ref, w2_ref, w3_ref)):
            total = None
            for other, mixed in enumerate((o0_ref, o1_ref, o2_ref, o3_ref)):
                features = pl.ds(pl.multiple_of((place ^ other) * heads, heads), heads)
                term = mm(mixed[rows, :], weight[features, :])
                total = term if total is None else total + term
            spot = pl.multiple_of((place ^ part) * columns, columns)
            sum_ref[:, pl.ds(spot, columns)] = total

        values = sum_ref[...] + piece[...].astype(F32)
        if index == 0:
            here_ref[...] = values
        factor = lax.rsqrt(jnp.mean(values * values, axis=-1, keepdims=True) + EPS)
        unit_ref[index * rows_each : (index + 1) * rows_each, :] = (values * factor).astype(BF)


def hidden_kernel(offset_ref, unit_ref, *rest):
    (*piece_refs, hidden_ref, gate_factor_ref, up_factor_ref, weight_ref, semaphore) = rest
    here = hidden_ref.shape[1]

    @pl.when(pl.program_id(0) == 0)
    def _():
        load_pieces(offset_ref, piece_refs, semaphore, (weight_ref, 0))()

    both = mm(unit_ref[...], weight_ref[...])
    gate = both[:, :here]
    up = both[:, here:]
    sig = 1.0 / (1.0 + jnp.exp(-gate))
    silu = gate * sig
    hidden_ref[...] = (silu * up).astype(BF)
    gate_factor_ref[...] = (up * sig * (1.0 + gate * (1.0 - sig))).astype(BF)
    up_factor_ref[...] = silu.astype(BF)


def hidden_grad_kernel(offset_ref, grad_ref, gate_factor_ref, up_factor_ref, *rest):
    (*piece_refs, both_ref, down_ref, semaphore) = rest
    here = gate_factor_ref.shape[1]

    @pl.when(pl.program_id(0) == 0)
    def _():
        load_pieces(offset_ref, piece_refs, semaphore, (down_ref, 0))()

    grad = mm_nt(grad_ref[...], down_ref[...])
    both_ref[:, :here] = (grad * gate_factor_ref[...].astype(F32)).astype(BF)
    both_ref[:, here:] = (grad * up_factor_ref[...].astype(F32)).astype(BF)


def split_kernel(transposed, order_ref, offset_ref, left_ref, *rest):
    (*piece_refs, keep_ref, send_ref, right_ref, semaphore) = rest

    @pl.when(pl.program_id(0) == 0)
    def _():
        load_pieces(offset_ref, piece_refs, semaphore, (right_ref, 0))()

    product = (mm_nt if transposed else mm)(left_ref[...], right_ref[...])

    @pl.when(pl.program_id(0) % 2 == 0)
    def _():
        keep_ref[...] = product

    @pl.when(pl.program_id(0) % 2 == 1)
    def _():
        send_ref[...] = product.astype(BF)


def output_grad_kernel(
    chunk_rows,
    place_ref,
    g0_ref,
    g1_ref,
    g2_ref,
    g3_ref,
    mixed_ref,
    w0_ref,
    w1_ref,
    w2_ref,
    w3_ref,
    grad_ref,
    terms_ref,
    total_ref,
):
    place = place_ref[0]
    rows_each = g0_ref.shape[0]
    heads = mixed_ref.shape[1]
    columns = w0_ref.shape[1]
    features = pl.ds(pl.multiple_of(place * heads, heads), heads)
    for index, grads in enumerate((g0_ref, g1_ref, g2_ref, g3_ref)):
        rows = pl.ds(pl.multiple_of((place ^ index) * rows_each, rows_each), rows_each)
        total = None
        for part, weight in enumerate((w0_ref, w1_ref, w2_ref, w3_ref)):
            spot = pl.ds(pl.multiple_of((place ^ part) * columns, columns), columns)
            term = mm_nt(grads[:, spot], weight[features, :])
            total = term if total is None else total + term
        grad_ref[rows, :] = total.astype(BF)
        term = mm_tn(mixed_ref[rows, :], grads[...])
        total_ref[...] = term if index == 0 else total_ref[...] + term
    sides = total_ref.shape[1] // terms_ref.shape[1]
    width = terms_ref.shape[1]
    chunks = terms_ref.shape[0] // sides // chunk_rows
    for step in range(chunks):
        for side in range(sides):
            start = (step * sides + side) * chunk_rows
            terms_ref[start : start + chunk_rows, :] = total_ref[
                step * chunk_rows : (step + 1) * chunk_rows, side * width : (side + 1) * width
            ]


def back_kernel(
    head_dim,
    low_ref,
    grad_ref,
    query_ref,
    key_ref,
    value_ref,
    raw_ref,
    cos_ref,
    sin_ref,
    gain_ref,
    start_ref,
    usable_ref,
    out_ref,
    terms_ref,
    key_sum_ref,
    value_sum_ref,
):
    row_length = grad_ref.shape[0]
    query_groups = query_ref.shape[1] // PAIR
    scale = 1.0 / math.sqrt(head_dim)
    key_sum_ref[...] = jnp.zeros_like(key_sum_ref)
    value_sum_ref[...] = jnp.zeros_like(value_sum_ref)
    terms_ref[...] = jnp.zeros_like(terms_ref)

    def through_norm(rows, group, grad, kind):
        grad = grad.astype(BF).astype(F32)
        turned = grad * cos_ref[rows, :] - half_partner(grad, head_dim) * sin_ref[rows, :]
        values = raw_ref[rows, group * PAIR : (group + 1) * PAIR]
        factor = lax.rsqrt(head_means(values * values, head_dim) + EPS)
        unit = values * factor
        terms_ref[kind : kind + 1, :] += jnp.sum(turned * unit, axis=0, keepdims=True)
        scaled = turned * gain_ref[kind : kind + 1, :]
        back = factor * (scaled - unit * head_means(scaled * unit, head_dim))
        out_ref[rows, group * PAIR : (group + 1) * PAIR] = back.astype(BF)

    def attend(first_row, first_key, window):
        bias = mask_bias(start_ref, usable_ref, first_row, first_key, BLOCK, window)
        rows = pl.ds(first_row, BLOCK)
        keys = pl.ds(first_key, window)
        found = []
        for group in range(query_groups):
            pair = slice(group * PAIR, (group + 1) * PAIR)
            stacked = stacked_heads(query_ref[rows, pair], head_dim)
            grads = stacked_heads(grad_ref[rows, pair], head_dim)
            grown = jnp.exp(mm_nt(stacked, key_ref[keys, pair]) + bias)
            share = grown * (1.0 / jnp.sum(grown, axis=-1, keepdims=True))
            grad_share = mm_nt(grads, value_ref[keys, pair])
            centre = jnp.sum(share * grad_share, axis=-1, keepdims=True)
            grad_score = (share * (grad_share - centre)).astype(BF)
            grad_query = side_by_side(mm(grad_score, key_ref[keys, pair]), head_dim) * scale
            key_term = mm_tn(grad_score, stacked)
            found.append((grad_query, key_term, mm_tn(share.astype(BF), grads)))
        for group, (grad_query, key_term, value_term) in enumerate(found):
            pair = slice(group * PAIR, (group + 1) * PAIR)
            key_sum_ref[keys, pair] += key_term
            value_sum_ref[keys, pair] += value_term
            through_norm(rows, group, grad_query, 0)

    each_block(low_ref, row_length, attend)

    def folded(sum_ref, rows):
        first = sum_ref[rows, :PAIR]
        second = sum_ref[rows, PAIR:]
        return jnp.where(
            lanes(first.shape) < head_dim,
            first + pltpu.roll(first, head_dim, 1),
            second + pltpu.roll(second, head_dim, 1),
        )

    def finish(step, carry):
        rows = pl.ds(pl.multiple_of(step * BLOCK, BLOCK), BLOCK)
        through_norm(rows, query_groups, folded(key_sum_ref, rows), 1)
        out_ref[rows, (query_groups + 1) * PAIR :] = folded(value_sum_ref, rows).astype(BF)
        return carry

    lax.fori_loop(0, row_length // BLOCK, finish, 0)


def as_column(values):
    if values.shape[1] == 1:
        return values
    count = values.shape[1]
    return jnp.transpose(jnp.broadcast_to(values, (count, count)))[:, :1]


def attention_pack_kernel(
    place_ref,
    gain_ref,
    query_ref,
    key_ref,
    value_ref,
    output_ref,
    pack_ref,
    wide_ref,
    semaphore,
):
    gain = as_column(gain_ref[...]).astype(BF).astype(F32)
    weights = (query_ref, key_ref, value_ref, output_ref)
    start = 0
    copies = []
    for index, weight_ref in enumerate(weights):
        size = weight_ref.shape[1] // SEQ
        column = pl.multiple_of(place_ref[0] * size, size)
        copies.append(
            pltpu.make_async_copy(
                weight_ref.at[:, pl.ds(column, size)],
                wide_ref.at[:, start : start + size],
                semaphore.at[index],
            )
        )
        copies[-1].start()
        start += size
    start = 0
    for index, weight_ref in enumerate(weights):
        size = weight_ref.shape[1] // SEQ
        copies[index].wait()
        values = wide_ref[:, start : start + size].astype(BF)
        if index < len(weights) - 1:
            values = (values.astype(F32) * gain).astype(BF)
        pack_ref[:, start : start + size] = values
        start += size


def hidden_pack_kernel(
    pieces, place_ref, gain_ref, gate_ref, up_ref, pack_ref, wide_ref, semaphore
):
    piece = gate_ref.shape[1] // (pieces * SEQ)
    here = pieces * piece
    chunk = 32
    steps = gate_ref.shape[0] // chunk
    weights = (gate_ref, up_ref)

    def copy(index, part):
        rows = pl.ds(pl.multiple_of(index * chunk, chunk), chunk)
        return pltpu.make_async_copy(
            weights[part].at[rows, :], wide_ref.at[part, rows, :], semaphore.at[part, index]
        )

    for index in range(steps):
        for part in range(2):
            copy(index, part).start()
    for place in range(SEQ):

        @pl.when(place_ref[0] == place)
        def _(place=place):
            def step(index, carry):
                rows = pl.ds(pl.multiple_of(index * chunk, chunk), chunk)
                gain = gain_ref[rows, :].astype(BF).astype(F32)
                for part in range(2):
                    copy(index, part).wait()
                    joined = jnp.concatenate(
                        [
                            wide_ref[part, rows, start : start + piece]
                            for start in range(place * piece, gate_ref.shape[1], SEQ * piece)
                        ],
                        axis=1,
                    )
                    pack_ref[rows, part * here : (part + 1) * here] = (
                        joined.astype(BF).astype(F32) * gain
                    ).astype(BF)
                return carry

            lax.fori_loop(0, steps, step, 0)


def hidden_owner_kernel(
    pieces, place_ref, sums_ref, gate_ref, up_ref, gain_ref, gate_grad_ref, up_grad_ref, terms_ref
):
    seq_count = sums_ref.shape[0]
    here = sums_ref.shape[2] // 2
    piece = here // pieces
    gain = gain_ref[...].astype(BF).astype(F32)
    total = None
    for part, (weight_ref, grad_ref) in enumerate(
        ((gate_ref, gate_grad_ref), (up_ref, up_grad_ref))
    ):
        sums = [sums_ref[seq].astype(F32) for seq in range(seq_count)]
        joined = jnp.concatenate(
            [
                sums[seq][:, part * here + step * piece : part * here + (step + 1) * piece]
                for step in range(pieces)
                for seq in range(seq_count)
            ],
            axis=1,
        )
        term = row_sums(weight_ref[...].astype(BF).astype(F32) * joined)
        total = term if total is None else total + term
        grad_ref[...] = joined * gain
    terms_ref[...] = total


def attention_owner_kernel(
    place_ref,
    s0_ref,
    s1_ref,
    s2_ref,
    s3_ref,
    query_ref,
    key_ref,
    value_ref,
    gain_ref,
    query_grad_ref,
    key_grad_ref,
    value_grad_ref,
    terms_ref,
):
    place = place_ref[0]
    gain = gain_ref[...].astype(BF).astype(F32)
    pieces = (s0_ref, s1_ref, s2_ref, s3_ref)
    rows = query_ref.shape[0]
    start = 0
    total = None
    for weight_ref, grad_ref in (
        (query_ref, query_grad_ref),
        (key_ref, key_grad_ref),
        (value_ref, value_grad_ref),
    ):
        size = weight_ref.shape[1] // len(pieces)
        for index, sums in enumerate(pieces):
            columns = pl.ds(pl.multiple_of((place ^ index) * size, size), size)
            values = sums[:rows, start : start + size].astype(F32)
            weight = weight_ref[:, columns].astype(BF).astype(F32)
            term = row_sums(weight * values)
            total = term if total is None else total + term
            grad_ref[:, columns] = values * gain
        start += size
    terms_ref[...] = total


def row_sums(values):
    ones = jnp.ones((8, values.shape[1]), BF)
    high = values.astype(BF)
    rest = (values - high.astype(F32)).astype(BF)
    return (mm_nt(ones, high) + mm_nt(ones, rest))[:1]


def placed_call(kernel, results, place_array, operands, blocks, vmem, flops=0, moved=0):
    return pl.pallas_call(
        kernel,
        out_shape=[jax.ShapeDtypeStruct(shape, kind) for shape, kind in results],
        grid_spec=pltpu.PrefetchScalarGridSpec(
            num_scalar_prefetch=1,
            grid=(1,),
            in_specs=[pl.BlockSpec(shape, index) for shape, index in blocks],
            out_specs=[
                pl.BlockSpec(shape, lambda i, place, rank=len(shape): (0,) * rank)
                for shape, _ in results
            ],
        ),
        compiler_params=pltpu.CompilerParams(vmem_limit_bytes=vmem * MEGA),
        cost_estimate=cost(kernel, flops),
    )(place_array, *operands)


def own_rows_block(i, place):
    return (place[0], 0)


def everything(i, place):
    return (0, 0)


MICROSECONDS = {
    "attention_pack_kernel": 2.6,
    "hidden_pack_kernel": 4.2,
    "columns_kernel": 2.6,
    "project_kernel": 9.5,
    "attend_kernel": 7.0,
    "middle_kernel": 5.0,
    "hidden_kernel": 9.0,
    "hidden_grad_kernel": 5.4,
    "output_grad_kernel": 3.0,
    "back_kernel": 15.6,
    "hidden_owner_kernel": 3.1,
    "attention_owner_kernel": 1.9,
}


def cost(kernel, flops):
    name = getattr(kernel, "func", kernel).__name__
    time = MICROSECONDS.get(name, flops * 2.0e-9 + 0.5) * 0.5
    return pl.CostEstimate(flops=int(time * 1.15e9), bytes_accessed=0, transcendentals=0)


def call(
    kernel, results, scalar_count, operands, vmem, pieces=(), scratch=(), flops=0, moved=0
):
    return pl.pallas_call(
        kernel,
        out_shape=[jax.ShapeDtypeStruct(shape, kind) for shape, kind in results],
        in_specs=scalars(scalar_count)
        + whole_vmem(len(operands) - scalar_count)
        + [pl.BlockSpec(memory_space=pltpu.HBM)] * len(pieces),
        out_specs=whole_vmem(len(results)),
        scratch_shapes=list(scratch),
        compiler_params=pltpu.CompilerParams(vmem_limit_bytes=vmem * MEGA),
        cost_estimate=cost(kernel, flops),
    )(*operands, *pieces)


def block_call(kernel, results, scalar_arrays, operands, vmem, pieces, scratch, flops, moved):
    return pl.pallas_call(
        kernel,
        out_shape=[jax.ShapeDtypeStruct(shape, kind) for shape, kind, _, _ in results],
        grid_spec=pltpu.PrefetchScalarGridSpec(
            num_scalar_prefetch=len(scalar_arrays),
            grid=(4,),
            in_specs=[pl.BlockSpec(shape, index) for _, shape, index in operands]
            + [pl.BlockSpec(memory_space=pltpu.HBM)] * len(pieces),
            out_specs=[pl.BlockSpec(shape, index) for _, _, shape, index in results],
            scratch_shapes=list(scratch),
        ),
        compiler_params=pltpu.CompilerParams(vmem_limit_bytes=vmem * MEGA),
        cost_estimate=cost(kernel, flops),
    )(*scalar_arrays, *(array for array, _, _ in operands), *pieces)


def row_block(step, *scalar_refs):
    return (step, 0)


def half_block(step, *scalar_refs):
    return (step // 2, 0)


def first_block(step, *scalar_refs):
    return (0, 0)


def ordered_block(step, order_ref, *scalar_refs):
    return (order_ref[step], 0)


def split_product(left, right_shape, offsets, pieces, transposed, order):
    rows = left.shape[0] // 4
    width = right_shape[0] if transposed else right_shape[1]
    return block_call(
        functools.partial(split_kernel, transposed),
        [
            ((2 * rows, width), F32, (rows, width), half_block),
            ((2 * rows, width), BF, (rows, width), half_block),
        ],
        (order, offsets),
        [(left, (rows, left.shape[1]), ordered_block)],
        20,
        pieces,
        [pltpu.VMEM(right_shape, BF), pltpu.SemaphoreType.DMA((1, len(pieces)))],
        2 * left.shape[0] * left.shape[1] * width,
        2 * (left.size + right_shape[0] * right_shape[1]) + 6 * left.shape[0] * width,
    )


def swap(values, bit):
    count = lax.axis_size("seq")
    return lax.ppermute(values, "seq", [(i, i ^ bit) for i in range(count)])


def seq_pieces(values):
    far = swap(values, 2)
    near = swap(values, 1)
    return (values, near, far, swap(far, 1))


def after(values, *others):
    return lax.optimization_barrier((values, others))[0]


def ring_length():
    count = lax.axis_size("dp")
    return count if count % 2 == 0 and 4 <= count <= 8 else 0


def ring_order(count):
    return list(range(0, count, 2)) + list(range(count - 1, 0, -2))


def ring_sources(offsets):
    count = lax.axis_size("dp")
    place = lax.axis_index("dp")
    spot = jnp.where(place % 2 == 0, place // 2, count - 1 - place // 2)
    spot = (spot + jnp.asarray(offsets, jnp.int32) + count) % count
    return jnp.where(spot < count // 2, 2 * spot, 2 * (count - 1 - spot) + 1)


def ring_source(offset):
    count = lax.axis_size("dp")
    place = lax.axis_index("dp")
    spot = jnp.where(place % 2 == 0, place // 2, count - 1 - place // 2)
    spot = (spot + offset + count) % count
    return jnp.where(spot < count // 2, 2 * spot, 2 * (count - 1 - spot) + 1)


def ring_move(values, step):
    count = lax.axis_size("dp")
    order = ring_order(count)
    return lax.ppermute(
        values, "dp", [(order[i], order[(i + step) % count]) for i in range(count)]
    )


def half_of(rows):
    return rows // 32 * 16 or rows // 2


class GatherRing:
    def __init__(self, shard, long=1, leads=False):
        count = ring_length()
        self.rows = shard.shape[0]
        self.steps = count // 2
        self.pieces = [shard]
        self.spots = [0]
        self.flying = {}
        self.sent = ()
        if not count:
            self.pieces = [lax.all_gather(shard, "dp", axis=0, tiled=True)]
            return
        self.long = long
        self.leads = leads
        self.taken = 0
        self.flying = {1: shard, -1: shard}

    def step(self, *others):
        if not self.steps:
            return others
        self.flying, others = lax.optimization_barrier((self.flying, others))
        self.taken += 1
        ways = [self.long]
        if (self.taken > 1) if self.leads else (self.taken < self.steps):
            ways.append(-self.long)
        self.sent = tuple(self.flying[way] for way in ways)
        for way in ways:
            self.flying[way] = ring_move(self.flying[way], way)
            self.pieces.append(self.flying[way])
            lag = self.leads and way != self.long
            self.spots.append(-way * (self.taken - int(lag)))
        return others

    def arrived(self):
        return self.flying

    @property
    def offsets(self):
        if not self.steps:
            return jnp.zeros((1,), jnp.int32)
        return ring_sources(self.spots) * self.rows


class ScatterRing:
    def __init__(self, terms, halved=False):
        self.count = ring_length()
        self.halved = halved
        self.terms = terms
        self.flying = {}
        if not self.count:
            size = lax.axis_size("dp")
            parts = [term.reshape(size, -1, term.shape[1]) for term in terms]
            whole = self.joined(parts)
            self.sums = lax.psum_scatter(
                whole.reshape(-1, whole.shape[-1]).astype(BF), "dp", scatter_dimension=0, tiled=True
            ).astype(F32)
            self.steps = 0
            self.sent = ()
            return
        self.steps = self.count // 2
        self.taken = 0
        self.sent = ()

    def joined(self, parts):
        return parts[0] if len(parts) == 1 else jnp.concatenate(parts, axis=-2)

    def term(self, offset):
        parts = []
        for term in self.terms:
            rows = term.shape[0] // self.count
            parts.append(lax.dynamic_slice_in_dim(term, ring_source(offset) * rows, rows, 0))
        return self.joined(parts).astype(F32)

    def step(self, *others):
        if not self.steps:
            return others
        self.taken += 1
        left = self.steps + 1 - self.taken
        if self.taken == 1:
            self.terms, others = lax.optimization_barrier((self.terms, others))
            far = self.term(self.steps)
            half = half_of(far.shape[0])
            values = {1: far[:half], -1: far[half:]} if self.halved else {1: far}
        else:
            self.flying, others = lax.optimization_barrier((self.flying, others))
            values = {way: self.term(way * left) for way in (1, -1)}
            if self.taken == 2 and self.halved:
                up, down = (self.flying[1].astype(F32), self.flying[-1].astype(F32))
                half = up.shape[0]
                values = {
                    1: jnp.concatenate([values[1][:half] + up, values[1][half:]]),
                    -1: jnp.concatenate([values[-1][:half], values[-1][half:] + down]),
                }
            else:
                for way, arrived in self.flying.items():
                    values[way] = values[way] + arrived.astype(F32)
        sent = {way: value.astype(BF) for way, value in values.items()}
        self.sent = tuple(sent.values())
        self.flying = {way: ring_move(value, way) for way, value in sent.items()}
        return others

    def arrived(self):
        return self.flying

    def take(self, arrived):
        self.flying = arrived

    def result(self):
        if not self.steps:
            return self.sums
        return self.term(0) + self.flying[1].astype(F32) + self.flying[-1].astype(F32)


def local(
    tokens,
    segments,
    valid_mask,
    attention_gain,
    query_weight,
    key_weight,
    value_weight,
    query_gain,
    key_gain,
    output_weight,
    feedforward_gain,
    gate_weight,
    up_weight,
    down_weight,
    cotangent,
):
    seq_count = lax.axis_size("seq")
    dp_count = lax.axis_size("dp")
    place = lax.axis_index("seq")
    local_rows = tokens.shape[1]
    row_length = segments.shape[1]
    head_dim = query_gain.shape[0]
    width = tokens.shape[2]
    hidden_width = gate_weight.shape[1]
    query_width = query_weight.shape[1]
    key_width = key_weight.shape[1]
    query_here = query_width // seq_count
    key_here = key_width // seq_count
    hidden_here = hidden_width // seq_count
    weight_rows = query_weight.shape[0]
    own_rows = weight_rows // seq_count
    segment_row = segments[0]
    valid_row = valid_mask[0]

    def low(weight):
        return weight.astype(BF).astype(F32)

    place_array = place.astype(jnp.int32).reshape(1)
    gain_one = attention_gain[:, None]
    gain_two = feedforward_gain[:, None]
    qkv_width = query_here + 2 * key_here
    piece = hidden_width // (dp_count * seq_count)
    kernels_fit = weight_rows % 32 == 0 and own_rows % 8 == 0 and dp_count <= 8

    pack_width = qkv_width + width // seq_count
    (attention_pack,) = call(
        attention_pack_kernel,
        [((weight_rows, pack_width), BF)],
        1,
        (place_array, attention_gain[None, :] if weight_rows % PAIR == 0 else gain_one),
        58,
        pieces=(query_weight, key_weight, value_weight, output_weight),
        scratch=[pltpu.VMEM((weight_rows, pack_width), F32), pltpu.SemaphoreType.DMA((4,))],
        moved=8 * weight_rows * width,
    )
    if kernels_fit:
        (gate_up_pack,) = call(
            functools.partial(hidden_pack_kernel, dp_count),
            [((weight_rows, 2 * hidden_here), BF)],
            1,
            (place_array, after(gain_two, attention_pack)),
            58,
            pieces=(gate_weight, up_weight),
            scratch=[
                pltpu.VMEM((2, weight_rows, hidden_width), F32),
                pltpu.SemaphoreType.DMA((2, weight_rows // 32)),
            ],
            moved=8 * weight_rows * hidden_width,
        )
    else:

        def hidden_columns(weight):
            split = weight.reshape(weight_rows, dp_count, seq_count, piece)
            mine = lax.dynamic_index_in_dim(split, place, 2, keepdims=False)
            return (low(mine.reshape(weight_rows, hidden_here)) * low(gain_two)).astype(BF)

        gate_up_pack = jnp.concatenate(
            [hidden_columns(gate_weight), hidden_columns(up_weight)], axis=1
        )
    down_pack = lax.dynamic_slice_in_dim(down_weight, place * piece, piece, 0).astype(BF)
    down_pack = after(down_pack, attention_pack)

    order = place ^ jnp.arange(4, dtype=jnp.int32)
    plain = jnp.arange(4, dtype=jnp.int32)

    token_far = swap(tokens[0], 2)
    token_near = swap(tokens[0], 1)
    attention_ring = GatherRing(attention_pack)
    attention_ring.step()
    positions = doc_positions(segment_row)
    starts = jnp.arange(row_length, dtype=jnp.int32) - positions
    cos_wide, sin_wide = rope_tables(positions, head_dim)
    repeats = PAIR // head_dim
    head_gains = jnp.tile(jnp.stack([query_gain, key_gain]), (1, repeats))
    row_starts = starts[:, None]
    usable = valid_row[None, :]
    starts, row_starts, head_gains = attention_ring.step(starts, row_starts, head_gains)
    block_lows = starts[::BLOCK]
    token_far, cos_wide, sin_wide = attention_ring.step(token_far, cos_wide, sin_wide)
    token_pieces = (tokens[0], token_near, token_far, swap(token_far, 1))
    grad_far = swap(after(cotangent[0], token_far), 2)
    grad_near = swap(after(cotangent[0], token_far), 1)
    (gate_up_pack,) = attention_ring.step(gate_up_pack)

    gate_up_ring = GatherRing(after(gate_up_pack, attention_ring.arrived()))
    (grad_far,) = gate_up_ring.step(grad_far)
    grad_row_pieces = (cotangent[0], grad_near, grad_far, swap(grad_far, 1))
    (output_columns,) = pl.pallas_call(
        functools.partial(columns_kernel, qkv_width),
        out_shape=[jax.ShapeDtypeStruct((query_width, width // seq_count), BF)],
        in_specs=scalars(1) + [pl.BlockSpec(memory_space=pltpu.HBM)] * len(attention_ring.pieces),
        out_specs=whole_vmem(1),
        scratch_shapes=[pltpu.SemaphoreType.DMA((1, len(attention_ring.pieces)))],
        compiler_params=pltpu.CompilerParams(vmem_limit_bytes=58 * MEGA),
        cost_estimate=cost(columns_kernel, 0),
    )(attention_ring.offsets, *attention_ring.pieces)
    output_far = swap(output_columns, 2)
    output_near = swap(output_columns, 1)
    projected = call(
        functools.partial(project_kernel, head_dim),
        [
            ((row_length, width), BF),
            ((row_length, query_here + key_here), F32),
            ((row_length, query_here), BF),
            ((row_length, 2 * key_here), BF),
            ((row_length, 2 * key_here), BF),
            ((width, qkv_width), BF),
        ],
        2,
        (place_array, attention_ring.offsets, *token_pieces, cos_wide, sin_wide, head_gains),
        58,
        pieces=attention_ring.pieces,
        scratch=[pltpu.SemaphoreType.DMA((1, len(attention_ring.pieces)))],
        flops=2 * row_length * width * qkv_width,
        moved=12 * row_length * width,
    )
    projected, output_far = gate_up_ring.step(projected, output_far)
    output_pieces = (output_columns, output_near, output_far, swap(output_far, 1))
    unit_one, raw, queries, keys_two, values_two, qkv_weight = projected
    (mixed_here,) = call(
        functools.partial(attend_kernel, head_dim),
        [((row_length, query_here), BF)],
        1,
        (block_lows, queries, keys_two, values_two, row_starts, usable),
        58,
        flops=row_length * width * qkv_width,
        moved=4 * row_length * width,
    )
    mixed_far = swap(mixed_here, 2)
    mixed_near = swap(mixed_here, 1)
    gate_up_ring.step(mixed_here)
    (mixed_far,) = gate_up_ring.step(mixed_far)
    down_ring = GatherRing(after(down_pack, mixed_far), -1, True)
    down_ring.step()
    mixed_pieces = (mixed_here, mixed_near, mixed_far, swap(mixed_far, 1))
    unit_two, after_here = call(
        middle_kernel,
        [((row_length, width), BF), ((local_rows, width), F32)],
        1,
        (place_array, *token_pieces, *mixed_pieces, *output_pieces),
        18,
        scratch=[pltpu.VMEM((local_rows, width), F32)],
        flops=2 * row_length * width * width,
        moved=10 * row_length * width,
    )
    (unit_two,) = down_ring.step(unit_two)

    rows_each = row_length // 4
    hidden, gate_factor, up_factor = block_call(
        hidden_kernel,
        [((row_length, hidden_here), BF, (rows_each, hidden_here), row_block)] * 3,
        (gate_up_ring.offsets,),
        [(unit_two, (rows_each, width), row_block)],
        28,
        gate_up_ring.pieces,
        [
            pltpu.VMEM((width, 2 * hidden_here), BF),
            pltpu.SemaphoreType.DMA((1, len(gate_up_ring.pieces))),
        ],
        4 * row_length * width * hidden_here,
        8 * row_length * hidden_here + 4 * width * hidden_here,
    )
    hidden, gate_factor, up_factor = down_ring.step(hidden, gate_factor, up_factor)
    grad_rows = jnp.concatenate(grad_row_pieces)
    down_scatter = ScatterRing([mm_tn(hidden, grad_rows)], True)
    (down_scatter.terms,) = down_ring.step(down_scatter.terms)
    down_scatter.step()
    gate_up_grad, down_all = block_call(
        hidden_grad_kernel,
        [
            ((row_length, 2 * hidden_here), BF, (rows_each, 2 * hidden_here), row_block),
            ((hidden_here, width), BF, (hidden_here, width), first_block),
        ],
        (down_ring.offsets,),
        [
            (grad_rows, (rows_each, width), row_block),
            (gate_factor, (rows_each, hidden_here), row_block),
            (up_factor, (rows_each, hidden_here), row_block),
        ],
        24,
        down_ring.pieces,
        [pltpu.SemaphoreType.DMA((1, len(down_ring.pieces)))],
        2 * row_length * width * hidden_here,
        8 * row_length * hidden_here + 4 * width * hidden_here,
    )

    (gate_up_grad,) = down_scatter.step(gate_up_grad)
    keep, send = split_product(
        gate_up_grad, (width, 2 * hidden_here), gate_up_ring.offsets, gate_up_ring.pieces, True, plain
    )
    keep, send = down_scatter.step(keep, send)

    def halves(keep, near):
        return (
            keep[:local_rows] + near[:local_rows].astype(F32),
            (keep[local_rows:] + near[local_rows:].astype(F32)).astype(BF),
        )

    half_sum, half_send = halves(keep, swap(send, 1))
    half_send, unit_two = lax.optimization_barrier((half_send, unit_two))
    arrived = swap(half_send, 2)
    gate_up_scatter = ScatterRing([mm_tn(unit_two, gate_up_grad).astype(BF)], True)
    gate_up_scatter.step()
    unit_here, factor_here = rms_stats(after_here)
    grad_after = cotangent[0].astype(F32) + rms_back(
        half_sum + arrived.astype(F32), unit_here, factor_here
    )
    branch = grad_after.astype(BF)
    branch_far = swap(branch, 2)
    branch_near = swap(branch, 1)
    gate_up_scatter.step(branch)
    keep, send = split_product(
        after(hidden, branch, gate_up_scatter.sent),
        (hidden_here, width),
        jnp.zeros((1,), jnp.int32),
        [down_all],
        False,
        plain,
    )
    keep, send, branch_far = gate_up_scatter.step(keep, send, branch_far)
    branch_pieces = (branch, branch_near, branch_far, swap(branch_far, 1))
    half_sum, half_send = halves(keep, swap(send, 1))
    chunk_rows = query_width // (dp_count * seq_count)
    grad_mixed, output_terms = call(
        functools.partial(output_grad_kernel, chunk_rows),
        [
            ((row_length, query_here), BF),
            ((query_here * width // qkv_width, qkv_width), F32),
        ],
        1,
        (place_array, *branch_pieces, mixed_here, *output_pieces),
        14,
        scratch=[pltpu.VMEM((query_here, width), F32)],
        flops=4 * row_length * width * query_here,
        moved=8 * row_length * width,
    )

    down_scatter.step(grad_mixed)
    grad_mixed, half_send = gate_up_scatter.step(grad_mixed, half_send)
    arrived = swap(half_send, 2)
    qkv_grad, gain_terms = call(
        functools.partial(back_kernel, head_dim),
        [((row_length, qkv_width), BF), ((8, PAIR), F32)],
        1,
        (block_lows, after(grad_mixed, gate_up_scatter.sent), queries, keys_two, values_two, raw)
        + (cos_wide, sin_wide, head_gains, row_starts, usable),
        24,
        scratch=[pltpu.VMEM((row_length, 2 * key_here), F32)] * 2,
        flops=4 * row_length * width * qkv_width,
        moved=12 * row_length * width,
    )
    qkv_grad, gain_terms, arrived, gate_up_arrived, down_arrived = lax.optimization_barrier(
        (qkv_grad, gain_terms, arrived, gate_up_scatter.arrived(), down_scatter.arrived())
    )
    down_scatter.take(down_arrived)
    gate_up_scatter.take(gate_up_arrived)
    layer_out = (after_here + half_sum + arrived.astype(F32)).astype(BF)
    gain_rows = jnp.concatenate([gain_terms[0:1], gain_terms[1:2]], axis=1)
    gain_rows = jnp.pad(gain_rows, ((0, 15), (0, qkv_width - 2 * PAIR)))
    packed = jnp.concatenate(
        [
            mm_tn(unit_one, qkv_grad).reshape(dp_count, weight_rows, qkv_width),
            output_terms.reshape(dp_count, -1, qkv_width),
            jnp.broadcast_to(gain_rows, (dp_count, *gain_rows.shape)),
        ],
        axis=1,
    )
    attention_scatter = ScatterRing([packed.reshape(-1, qkv_width)])
    attention_scatter.step()
    gate_up_scatter.take(after(gate_up_scatter.arrived(), attention_scatter.sent))
    gate_up_sums = gate_up_scatter.result().astype(BF)
    keep, send = split_product(
        after(qkv_grad, gate_up_sums),
        (width, qkv_width),
        jnp.zeros((1,), jnp.int32),
        [qkv_weight],
        True,
        order,
    )
    keep, send = attention_scatter.step(keep, send)
    gate_up_sums = after(gate_up_sums, attention_scatter.sent)
    hidden_own = lax.all_to_all(
        gate_up_sums.reshape(seq_count, own_rows, -1), "seq", split_axis=0, concat_axis=0, tiled=True
    )
    half_sum, half_send = halves(keep, swap(send, 1))
    (half_send,) = attention_scatter.step(half_send)
    arrived = swap(half_send, 2)
    for _ in range(attention_scatter.steps - 3):
        (arrived,) = attention_scatter.step(arrived)
        hidden_own = after(hidden_own, attention_scatter.sent)
    unit_tokens, factor_tokens = rms_stats(tokens[0].astype(F32))
    token_grad = (
        grad_after + rms_back(half_sum + arrived.astype(F32), unit_tokens, factor_tokens)
    ).astype(BF)

    down_sums = down_scatter.result()
    attention_sums = attention_scatter.result().astype(BF)
    qkv_sums = attention_sums[:weight_rows]
    output_sums = jnp.concatenate(
        [
            attention_sums[weight_rows + part * chunk_rows : weight_rows + (part + 1) * chunk_rows]
            for part in range(width // qkv_width)
        ],
        axis=1,
    )

    def own(weight):
        return lax.dynamic_slice_in_dim(weight, place * own_rows, own_rows, 0)

    gain_row = attention_sums[-16:]
    qkv_pieces = []
    for bits in range(4):
        part = lax.dynamic_slice_in_dim(qkv_sums, (place ^ bits) * own_rows, own_rows, 0)
        part = after(jnp.concatenate([part, gain_row]), arrived)
        qkv_pieces.append(swap(part, bits) if bits else part)
    gain_sums = sum(piece[own_rows : own_rows + 1].astype(F32) for piece in qkv_pieces)
    gain_sums = jnp.sum(gain_sums[0, : 2 * PAIR].reshape(2, repeats, head_dim), axis=1)
    if kernels_fit:
        gate_grad, up_grad, feed_gain_grad = placed_call(
            functools.partial(hidden_owner_kernel, dp_count),
            [((own_rows, hidden_width), F32)] * 2 + [((1, own_rows), F32)],
            place_array,
            (hidden_own, gate_weight, up_weight, gain_two),
            [
                (hidden_own.shape, lambda i, place: (0, 0, 0)),
                ((own_rows, hidden_width), own_rows_block),
                ((own_rows, hidden_width), own_rows_block),
                ((own_rows, 1), own_rows_block),
            ],
            58,
            moved=20 * own_rows * hidden_width,
        )
        query_grad, key_grad, value_grad, attention_gain_grad = placed_call(
            attention_owner_kernel,
            [((own_rows, query_width), F32)]
            + [((own_rows, key_width), F32)] * 2
            + [((1, own_rows), F32)],
            place_array,
            (*qkv_pieces, query_weight, key_weight, value_weight, gain_one),
            [((own_rows + 16, qkv_width), everything)] * 4
            + [
                ((own_rows, query_width), own_rows_block),
                ((own_rows, key_width), own_rows_block),
                ((own_rows, key_width), own_rows_block),
                ((own_rows, 1), own_rows_block),
            ],
            58,
            moved=20 * own_rows * query_width,
        )
    else:
        spread = jnp.stack(qkv_pieces)[order, :own_rows].astype(F32)

        def joined(first, size):
            return jnp.swapaxes(spread[:, :, first : first + size], 0, 1).reshape(own_rows, -1)

        query_own = joined(0, query_here)
        key_own = joined(query_here, key_here)
        value_own = joined(query_here + key_here, key_here)
        attention_gain_grad = (
            jnp.sum(own(low(query_weight)) * query_own, axis=1)
            + jnp.sum(own(low(key_weight)) * key_own, axis=1)
            + jnp.sum(own(low(value_weight)) * value_own, axis=1)
        )
        gain_own = own(low(gain_one))
        query_grad, key_grad, value_grad = (
            query_own * gain_own,
            key_own * gain_own,
            value_own * gain_own,
        )
        hidden_own = hidden_own.reshape(seq_count, own_rows, 2, dp_count, piece)
        hidden_own = jnp.transpose(hidden_own, (2, 1, 3, 0, 4))
        hidden_own = hidden_own.reshape(2, own_rows, hidden_width).astype(F32)
        feed_gain_grad = jnp.sum(own(low(gate_weight)) * hidden_own[0], axis=1) + jnp.sum(
            own(low(up_weight)) * hidden_own[1], axis=1
        )
        gain_own = own(low(gain_two))
        gate_grad, up_grad = (hidden_own[0] * gain_own, hidden_own[1] * gain_own)

    moves = [
        (dp * seq_count + seq, seq * dp_count + dp)
        for dp in range(dp_count)
        for seq in range(seq_count)
    ]
    output_own = lax.ppermute(output_sums, ("dp", "seq"), moves).astype(F32)

    return (
        layer_out.reshape(1, local_rows, -1),
        token_grad.reshape(1, local_rows, -1),
        attention_gain_grad.reshape(own_rows),
        query_grad,
        key_grad,
        value_grad,
        gain_sums[0],
        gain_sums[1],
        output_own,
        feed_gain_grad.reshape(own_rows),
        gate_grad,
        up_grad,
        down_sums,
    )


def solution(mesh):
    in_specs = (
        P("dp", "seq", None),
        P("dp", None),
        P("dp", None),
        P("dp"),
        P("dp", None),
        P("dp", None),
        P("dp", None),
        P(),
        P(),
        P("dp", None),
        P("dp"),
        P("dp", None),
        P("dp", None),
        P("dp", None),
        P("dp", "seq", None),
    )
    out_specs = (
        P("dp", "seq", None),
        P("dp", "seq", None),
        P(("dp", "seq")),
        P(("dp", "seq"), None),
        P(("dp", "seq"), None),
        P(("dp", "seq"), None),
        P(),
        P(),
        P(("dp", "seq"), None),
        P(("dp", "seq")),
        P(("dp", "seq"), None),
        P(("dp", "seq"), None),
        P(("dp", "seq"), None),
    )
    return jax.shard_map(local, mesh=mesh, in_specs=in_specs, out_specs=out_specs, check_vma=False)
```

```python
import functools
import math

import jax
import jax.numpy as jnp
from jax import lax
from jax.experimental import pallas as pl
from jax.experimental.pallas import tpu as pltpu
from jax.sharding import PartitionSpec as P

EPS = 1e-05
ROPE_BASE = 1000000.0
NEG_FILL = -1e30
BF = jnp.bfloat16
F32 = jnp.float32
BLOCK = 128
PAIR = 128
SEQ = 4
MEGA = 1024 * 1024


def dot(left, right, dims):
    return lax.dot_general(left, right, (dims, ((), ())), preferred_element_type=F32)


def mm(left, right):
    return dot(left, right, ((1,), (0,)))


def mm_nt(left, right):
    return dot(left, right, ((1,), (1,)))


def mm_tn(left, right):
    return dot(left, right, ((0,), (0,)))


def rms_stats(values):
    factor = lax.rsqrt(jnp.mean(values * values, axis=-1, keepdims=True) + EPS)
    return (values * factor, factor)


def rms_back(grad_unit, unit_values, factor):
    return factor * (
        grad_unit - unit_values * jnp.mean(grad_unit * unit_values, axis=-1, keepdims=True)
    )


def doc_positions(segment_row):
    length = segment_row.shape[0]
    places = jnp.arange(length, dtype=jnp.int32)
    change = jnp.concatenate([jnp.ones((1,), dtype=jnp.bool_), segment_row[1:] != segment_row[:-1]])
    starts = lax.cummax(jnp.where(change, places, jnp.zeros_like(places)), axis=0)
    return places - starts


def rope_tables(positions, head_dim):
    half = head_dim // 2
    lane = jnp.arange(PAIR, dtype=jnp.int32)
    frequency = ROPE_BASE ** (-(lane % half).astype(F32) / half)
    angles = positions.astype(F32)[:, None] * frequency[None, :]
    sign = jnp.where(lane % head_dim < half, -1.0, 1.0)
    return (jnp.cos(angles), jnp.sin(angles) * sign[None, :])


def whole_vmem(count):
    return [pl.BlockSpec(memory_space=pltpu.VMEM)] * count


def scalars(count):
    return [pl.BlockSpec(memory_space=pltpu.SMEM)] * count


def lanes(shape):
    return lax.broadcasted_iota(jnp.int32, shape, 1)


def head_means(values, head_dim):
    width = values.shape[1]
    row = lax.broadcasted_iota(jnp.int32, (width, width), 0) // head_dim
    column = lax.broadcasted_iota(jnp.int32, (width, width), 1) // head_dim
    spread = jnp.where(row == column, 1.0 / head_dim, 0.0).astype(BF)
    high = values.astype(BF)
    rest = (values - high.astype(F32)).astype(BF)
    return mm(high, spread) + mm(rest, spread)


def half_partner(values, head_dim):
    half = head_dim // 2
    width = values.shape[1]
    upper = (lanes(values.shape) % head_dim) >= half
    return jnp.where(
        upper, pltpu.roll(values, half, 1), pltpu.roll(values, width - half, 1)
    )


def stacked_heads(pair, head_dim):
    first = lanes(pair.shape) < head_dim
    zero = jnp.zeros_like(pair)
    return jnp.concatenate([jnp.where(first, pair, zero), jnp.where(first, zero, pair)], axis=0)


def side_by_side(stacked, head_dim):
    rows = stacked.shape[0] // 2
    return jnp.where(
        lanes((rows, stacked.shape[1])) < head_dim, stacked[:rows], stacked[rows:]
    )


def mask_bias(start_ref, usable_ref, first_row, first_key, rows, window):
    row = first_row + lax.broadcasted_iota(jnp.int32, (rows, window), 0)
    key = first_key + lax.broadcasted_iota(jnp.int32, (rows, window), 1)
    start = start_ref[pl.ds(first_row, rows), :]
    usable = usable_ref[:, pl.ds(first_key, window)] > 0
    allowed = ((key >= start) & (key <= row) & usable) | (key == row)
    bias = jnp.where(allowed, 0.0, NEG_FILL)
    return jnp.concatenate([bias, bias], axis=0)


def each_block(low_ref, row_length, body):
    long_window = min(5 * BLOCK, row_length)

    def step(index, carry):
        first_row = pl.multiple_of(index * BLOCK, BLOCK)
        short_key = jnp.maximum(first_row - BLOCK, 0)
        is_short = low_ref[index] >= short_key

        @pl.when(is_short)
        def _():
            body(first_row, pl.multiple_of(short_key, BLOCK), 2 * BLOCK)

        @pl.when(jnp.logical_not(is_short))
        def _():
            long_key = jnp.maximum(first_row + BLOCK - long_window, 0)
            body(first_row, pl.multiple_of(long_key, BLOCK), long_window)

        return carry

    lax.fori_loop(0, row_length // BLOCK, step, 0)


def load_pieces(offset_ref, piece_refs, semaphore, *targets):
    copies = []
    for index, piece in enumerate(piece_refs):
        start = pl.multiple_of(offset_ref[index], 16)
        for part, (target, column) in enumerate(targets):
            rows = pl.ds(start, piece.shape[0])
            copies.append(
                pltpu.make_async_copy(
                    piece.at[:, column : column + target.shape[1]],
                    target.at[rows, :],
                    semaphore.at[part, index],
                )
            )
    for copy in copies:
        copy.start()

    def wait():
        for copy in copies:
            copy.wait()

    return wait


def columns_kernel(column, offset_ref, *rest):
    (*piece_refs, out_ref, semaphore) = rest
    load_pieces(offset_ref, piece_refs, semaphore, (out_ref, column))()


def project_kernel(
    head_dim,
    place_ref,
    offset_ref,
    x0_ref,
    x1_ref,
    x2_ref,
    x3_ref,
    cos_ref,
    sin_ref,
    gain_ref,
    *rest,
):
    (*piece_refs, unit_ref, raw_ref, query_ref, key_ref, value_ref, weight_ref) = rest[:-1]
    semaphore = rest[-1]
    wait = load_pieces(offset_ref, piece_refs, semaphore, (weight_ref, 0))
    place = place_ref[0]
    rows_each = x0_ref.shape[0]
    row_length = unit_ref.shape[0]
    query_groups = query_ref.shape[1] // PAIR
    for index, piece in enumerate((x0_ref, x1_ref, x2_ref, x3_ref)):

        def normalize(step, carry, piece=piece, base=(place ^ index) * rows_each):
            start = pl.multiple_of(step * BLOCK, BLOCK)
            values = piece[pl.ds(start, BLOCK), :].astype(F32)
            factor = lax.rsqrt(jnp.mean(values * values, axis=-1, keepdims=True) + EPS)
            rows = pl.ds(pl.multiple_of(base + start, BLOCK), BLOCK)
            unit_ref[rows, :] = (values * factor).astype(BF)
            return carry

        lax.fori_loop(0, rows_each // BLOCK, normalize, 0)
    wait()

    def project(step, carry):
        rows = pl.ds(pl.multiple_of(step * rows_each, rows_each), rows_each)
        raw = mm(unit_ref[rows, :], weight_ref[...])
        raw_ref[rows, :] = raw[:, : raw_ref.shape[1]]
        cos = cos_ref[rows, :]
        sin = sin_ref[rows, :]
        for group in range(query_groups + 1):
            is_key = group == query_groups
            values = raw[:, group * PAIR : (group + 1) * PAIR]
            factor = lax.rsqrt(head_means(values * values, head_dim) + EPS)
            scaled = values * factor * gain_ref[int(is_key) : int(is_key) + 1, :]
            turned = scaled * cos + half_partner(scaled, head_dim) * sin
            if is_key:
                crossed = pltpu.roll(turned, head_dim, 1)
                first = lanes(turned.shape) < head_dim
                key_ref[rows, :PAIR] = jnp.where(first, turned, crossed).astype(BF)
                key_ref[rows, PAIR:] = jnp.where(first, crossed, turned).astype(BF)
                values = raw[:, (group + 1) * PAIR :]
                crossed = pltpu.roll(values, head_dim, 1)
                value_ref[rows, :PAIR] = jnp.where(first, values, crossed).astype(BF)
                value_ref[rows, PAIR:] = jnp.where(first, crossed, values).astype(BF)
            else:
                query_ref[rows, group * PAIR : (group + 1) * PAIR] = (
                    turned * (1.0 / math.sqrt(head_dim))
                ).astype(BF)
        return carry

    lax.fori_loop(0, row_length // rows_each, project, 0)


def attend_kernel(
    head_dim, low_ref, query_ref, key_ref, value_ref, start_ref, usable_ref, mixed_ref
):
    row_length = query_ref.shape[0]
    query_groups = query_ref.shape[1] // PAIR

    def attend(first_row, first_key, window):
        bias = mask_bias(start_ref, usable_ref, first_row, first_key, BLOCK, window)
        rows = pl.ds(first_row, BLOCK)
        keys = pl.ds(first_key, window)
        found = []
        for group in range(query_groups):
            pair = slice(group * PAIR, (group + 1) * PAIR)
            stacked = stacked_heads(query_ref[rows, pair], head_dim)
            grown = jnp.exp(mm_nt(stacked, key_ref[keys, pair]) + bias)
            mixed = mm(grown.astype(BF), value_ref[keys, pair])
            mixed = mixed * (1.0 / jnp.sum(grown, axis=-1, keepdims=True))
            found.append(side_by_side(mixed, head_dim).astype(BF))
        mixed_ref[rows, :] = jnp.concatenate(found, axis=1)

    each_block(low_ref, row_length, attend)


def middle_kernel(
    place_ref,
    x0_ref,
    x1_ref,
    x2_ref,
    x3_ref,
    o0_ref,
    o1_ref,
    o2_ref,
    o3_ref,
    w0_ref,
    w1_ref,
    w2_ref,
    w3_ref,
    unit_ref,
    here_ref,
    sum_ref,
):
    place = place_ref[0]
    rows_each, width = x0_ref.shape
    heads = o0_ref.shape[1]
    columns = w0_ref.shape[1]
    for index, piece in enumerate((x0_ref, x1_ref, x2_ref, x3_ref)):
        base = pl.multiple_of((place ^ index) * rows_each, rows_each)
        rows = pl.ds(base, rows_each)
        for part, weight in enumerate((w0_ref, w1_ref, w2_ref, w3_ref)):
            total = None
            for other, mixed in enumerate((o0_ref, o1_ref, o2_ref, o3_ref)):
                features = pl.ds(pl.multiple_of((place ^ other) * heads, heads), heads)
                term = mm(mixed[rows, :], weight[features, :])
                total = term if total is None else total + term
            spot = pl.multiple_of((place ^ part) * columns, columns)
            sum_ref[:, pl.ds(spot, columns)] = total

        values = sum_ref[...] + piece[...].astype(F32)
        if index == 0:
            here_ref[...] = values
        factor = lax.rsqrt(jnp.mean(values * values, axis=-1, keepdims=True) + EPS)
        unit_ref[index * rows_each : (index + 1) * rows_each, :] = (values * factor).astype(BF)


def hidden_kernel(offset_ref, unit_ref, *rest):
    (*piece_refs, hidden_ref, gate_factor_ref, up_factor_ref, weight_ref, semaphore) = rest
    here = hidden_ref.shape[1]

    @pl.when(pl.program_id(0) == 0)
    def _():
        load_pieces(offset_ref, piece_refs, semaphore, (weight_ref, 0))()

    both = mm(unit_ref[...], weight_ref[...])
    gate = both[:, :here]
    up = both[:, here:]
    sig = 1.0 / (1.0 + jnp.exp(-gate))
    silu = gate * sig
    hidden_ref[...] = (silu * up).astype(BF)
    gate_factor_ref[...] = (up * sig * (1.0 + gate * (1.0 - sig))).astype(BF)
    up_factor_ref[...] = silu.astype(BF)


def hidden_grad_kernel(offset_ref, grad_ref, gate_factor_ref, up_factor_ref, *rest):
    (*piece_refs, both_ref, down_ref, semaphore) = rest
    here = gate_factor_ref.shape[1]

    @pl.when(pl.program_id(0) == 0)
    def _():
        load_pieces(offset_ref, piece_refs, semaphore, (down_ref, 0))()

    grad = mm_nt(grad_ref[...], down_ref[...])
    both_ref[:, :here] = (grad * gate_factor_ref[...].astype(F32)).astype(BF)
    both_ref[:, here:] = (grad * up_factor_ref[...].astype(F32)).astype(BF)


def split_kernel(transposed, order_ref, offset_ref, left_ref, *rest):
    (*piece_refs, keep_ref, send_ref, right_ref, semaphore) = rest

    @pl.when(pl.program_id(0) == 0)
    def _():
        load_pieces(offset_ref, piece_refs, semaphore, (right_ref, 0))()

    product = (mm_nt if transposed else mm)(left_ref[...], right_ref[...])

    @pl.when(pl.program_id(0) % 2 == 0)
    def _():
        keep_ref[...] = product

    @pl.when(pl.program_id(0) % 2 == 1)
    def _():
        send_ref[...] = product.astype(BF)


def output_grad_kernel(
    chunk_rows,
    place_ref,
    g0_ref,
    g1_ref,
    g2_ref,
    g3_ref,
    mixed_ref,
    w0_ref,
    w1_ref,
    w2_ref,
    w3_ref,
    grad_ref,
    terms_ref,
    total_ref,
):
    place = place_ref[0]
    rows_each = g0_ref.shape[0]
    heads = mixed_ref.shape[1]
    columns = w0_ref.shape[1]
    features = pl.ds(pl.multiple_of(place * heads, heads), heads)
    for index, grads in enumerate((g0_ref, g1_ref, g2_ref, g3_ref)):
        rows = pl.ds(pl.multiple_of((place ^ index) * rows_each, rows_each), rows_each)
        total = None
        for part, weight in enumerate((w0_ref, w1_ref, w2_ref, w3_ref)):
            spot = pl.ds(pl.multiple_of((place ^ part) * columns, columns), columns)
            term = mm_nt(grads[:, spot], weight[features, :])
            total = term if total is None else total + term
        grad_ref[rows, :] = total.astype(BF)
        term = mm_tn(mixed_ref[rows, :], grads[...])
        total_ref[...] = term if index == 0 else total_ref[...] + term
    sides = total_ref.shape[1] // terms_ref.shape[1]
    width = terms_ref.shape[1]
    chunks = terms_ref.shape[0] // sides // chunk_rows
    for step in range(chunks):
        for side in range(sides):
            start = (step * sides + side) * chunk_rows
            terms_ref[start : start + chunk_rows, :] = total_ref[
                step * chunk_rows : (step + 1) * chunk_rows, side * width : (side + 1) * width
            ]


def back_kernel(
    head_dim,
    low_ref,
    grad_ref,
    query_ref,
    key_ref,
    value_ref,
    raw_ref,
    cos_ref,
    sin_ref,
    gain_ref,
    start_ref,
    usable_ref,
    out_ref,
    terms_ref,
    key_sum_ref,
    value_sum_ref,
):
    row_length = grad_ref.shape[0]
    query_groups = query_ref.shape[1] // PAIR
    scale = 1.0 / math.sqrt(head_dim)
    key_sum_ref[...] = jnp.zeros_like(key_sum_ref)
    value_sum_ref[...] = jnp.zeros_like(value_sum_ref)
    terms_ref[...] = jnp.zeros_like(terms_ref)

    def through_norm(rows, group, grad, kind):
        grad = grad.astype(BF).astype(F32)
        turned = grad * cos_ref[rows, :] - half_partner(grad, head_dim) * sin_ref[rows, :]
        values = raw_ref[rows, group * PAIR : (group + 1) * PAIR]
        factor = lax.rsqrt(head_means(values * values, head_dim) + EPS)
        unit = values * factor
        terms_ref[kind : kind + 1, :] += jnp.sum(turned * unit, axis=0, keepdims=True)
        scaled = turned * gain_ref[kind : kind + 1, :]
        back = factor * (scaled - unit * head_means(scaled * unit, head_dim))
        out_ref[rows, group * PAIR : (group + 1) * PAIR] = back.astype(BF)

    def attend(first_row, first_key, window):
        bias = mask_bias(start_ref, usable_ref, first_row, first_key, BLOCK, window)
        rows = pl.ds(first_row, BLOCK)
        keys = pl.ds(first_key, window)
        found = []
        for group in range(query_groups):
            pair = slice(group * PAIR, (group + 1) * PAIR)
            stacked = stacked_heads(query_ref[rows, pair], head_dim)
            grads = stacked_heads(grad_ref[rows, pair], head_dim)
            grown = jnp.exp(mm_nt(stacked, key_ref[keys, pair]) + bias)
            share = grown * (1.0 / jnp.sum(grown, axis=-1, keepdims=True))
            grad_share = mm_nt(grads, value_ref[keys, pair])
            centre = jnp.sum(share * grad_share, axis=-1, keepdims=True)
            grad_score = (share * (grad_share - centre)).astype(BF)
            grad_query = side_by_side(mm(grad_score, key_ref[keys, pair]), head_dim) * scale
            key_term = mm_tn(grad_score, stacked)
            found.append((grad_query, key_term, mm_tn(share.astype(BF), grads)))
        for group, (grad_query, key_term, value_term) in enumerate(found):
            pair = slice(group * PAIR, (group + 1) * PAIR)
            key_sum_ref[keys, pair] += key_term
            value_sum_ref[keys, pair] += value_term
            through_norm(rows, group, grad_query, 0)

    each_block(low_ref, row_length, attend)

    def folded(sum_ref, rows):
        first = sum_ref[rows, :PAIR]
        second = sum_ref[rows, PAIR:]
        return jnp.where(
            lanes(first.shape) < head_dim,
            first + pltpu.roll(first, head_dim, 1),
            second + pltpu.roll(second, head_dim, 1),
        )

    def finish(step, carry):
        rows = pl.ds(pl.multiple_of(step * BLOCK, BLOCK), BLOCK)
        through_norm(rows, query_groups, folded(key_sum_ref, rows), 1)
        out_ref[rows, (query_groups + 1) * PAIR :] = folded(value_sum_ref, rows).astype(BF)
        return carry

    lax.fori_loop(0, row_length // BLOCK, finish, 0)


def as_column(values):
    if values.shape[1] == 1:
        return values
    count = values.shape[1]
    return jnp.transpose(jnp.broadcast_to(values, (count, count)))[:, :1]


def attention_pack_kernel(
    place_ref,
    gain_ref,
    query_ref,
    key_ref,
    value_ref,
    output_ref,
    pack_ref,
    wide_ref,
    semaphore,
):
    gain = as_column(gain_ref[...]).astype(BF).astype(F32)
    weights = (query_ref, key_ref, value_ref, output_ref)
    start = 0
    copies = []
    for index, weight_ref in enumerate(weights):
        size = weight_ref.shape[1] // SEQ
        column = pl.multiple_of(place_ref[0] * size, size)
        copies.append(
            pltpu.make_async_copy(
                weight_ref.at[:, pl.ds(column, size)],
                wide_ref.at[:, start : start + size],
                semaphore.at[index],
            )
        )
        copies[-1].start()
        start += size
    start = 0
    for index, weight_ref in enumerate(weights):
        size = weight_ref.shape[1] // SEQ
        copies[index].wait()
        values = wide_ref[:, start : start + size].astype(BF)
        if index < len(weights) - 1:
            values = (values.astype(F32) * gain).astype(BF)
        pack_ref[:, start : start + size] = values
        start += size


def hidden_pack_kernel(
    pieces, place_ref, gain_ref, gate_ref, up_ref, pack_ref, wide_ref, semaphore
):
    piece = gate_ref.shape[1] // (pieces * SEQ)
    here = pieces * piece
    chunk = 32
    steps = gate_ref.shape[0] // chunk
    weights = (gate_ref, up_ref)

    def copy(index, part):
        rows = pl.ds(pl.multiple_of(index * chunk, chunk), chunk)
        return pltpu.make_async_copy(
            weights[part].at[rows, :], wide_ref.at[part, rows, :], semaphore.at[part, index]
        )

    for index in range(steps):
        for part in range(2):
            copy(index, part).start()
    for place in range(SEQ):

        @pl.when(place_ref[0] == place)
        def _(place=place):
            def step(index, carry):
                rows = pl.ds(pl.multiple_of(index * chunk, chunk), chunk)
                gain = gain_ref[rows, :].astype(BF).astype(F32)
                for part in range(2):
                    copy(index, part).wait()
                    joined = jnp.concatenate(
                        [
                            wide_ref[part, rows, start : start + piece]
                            for start in range(place * piece, gate_ref.shape[1], SEQ * piece)
                        ],
                        axis=1,
                    )
                    pack_ref[rows, part * here : (part + 1) * here] = (
                        joined.astype(BF).astype(F32) * gain
                    ).astype(BF)
                return carry

            lax.fori_loop(0, steps, step, 0)


def hidden_owner_kernel(
    pieces, place_ref, sums_ref, gate_ref, up_ref, gain_ref, gate_grad_ref, up_grad_ref, terms_ref
):
    seq_count = sums_ref.shape[0]
    here = sums_ref.shape[2] // 2
    piece = here // pieces
    gain = gain_ref[...].astype(BF).astype(F32)
    total = None
    for part, (weight_ref, grad_ref) in enumerate(
        ((gate_ref, gate_grad_ref), (up_ref, up_grad_ref))
    ):
        sums = [sums_ref[seq].astype(F32) for seq in range(seq_count)]
        joined = jnp.concatenate(
            [
                sums[seq][:, part * here + step * piece : part * here + (step + 1) * piece]
                for step in range(pieces)
                for seq in range(seq_count)
            ],
            axis=1,
        )
        term = row_sums(weight_ref[...].astype(BF).astype(F32) * joined)
        total = term if total is None else total + term
        grad_ref[...] = joined * gain
    terms_ref[...] = total


def attention_owner_kernel(
    place_ref,
    s0_ref,
    s1_ref,
    s2_ref,
    s3_ref,
    query_ref,
    key_ref,
    value_ref,
    gain_ref,
    query_grad_ref,
    key_grad_ref,
    value_grad_ref,
    terms_ref,
):
    place = place_ref[0]
    gain = gain_ref[...].astype(BF).astype(F32)
    pieces = (s0_ref, s1_ref, s2_ref, s3_ref)
    rows = query_ref.shape[0]
    start = 0
    total = None
    for weight_ref, grad_ref in (
        (query_ref, query_grad_ref),
        (key_ref, key_grad_ref),
        (value_ref, value_grad_ref),
    ):
        size = weight_ref.shape[1] // len(pieces)
        for index, sums in enumerate(pieces):
            columns = pl.ds(pl.multiple_of((place ^ index) * size, size), size)
            values = sums[:rows, start : start + size].astype(F32)
            weight = weight_ref[:, columns].astype(BF).astype(F32)
            term = row_sums(weight * values)
            total = term if total is None else total + term
            grad_ref[:, columns] = values * gain
        start += size
    terms_ref[...] = total


def row_sums(values):
    ones = jnp.ones((8, values.shape[1]), BF)
    high = values.astype(BF)
    rest = (values - high.astype(F32)).astype(BF)
    return (mm_nt(ones, high) + mm_nt(ones, rest))[:1]


def placed_call(kernel, results, place_array, operands, blocks, vmem, flops=0, moved=0):
    return pl.pallas_call(
        kernel,
        out_shape=[jax.ShapeDtypeStruct(shape, kind) for shape, kind in results],
        grid_spec=pltpu.PrefetchScalarGridSpec(
            num_scalar_prefetch=1,
            grid=(1,),
            in_specs=[pl.BlockSpec(shape, index) for shape, index in blocks],
            out_specs=[
                pl.BlockSpec(shape, lambda i, place, rank=len(shape): (0,) * rank)
                for shape, _ in results
            ],
        ),
        compiler_params=pltpu.CompilerParams(vmem_limit_bytes=vmem * MEGA),
        cost_estimate=cost(kernel, flops),
    )(place_array, *operands)


def own_rows_block(i, place):
    return (place[0], 0)


def everything(i, place):
    return (0, 0)


MICROSECONDS = {
    "attention_pack_kernel": 2.6,
    "hidden_pack_kernel": 4.2,
    "columns_kernel": 2.6,
    "project_kernel": 9.5,
    "attend_kernel": 7.0,
    "middle_kernel": 5.0,
    "hidden_kernel": 9.0,
    "hidden_grad_kernel": 5.4,
    "output_grad_kernel": 3.0,
    "back_kernel": 15.6,
    "hidden_owner_kernel": 3.1,
    "attention_owner_kernel": 1.9,
}


def cost(kernel, flops):
    name = getattr(kernel, "func", kernel).__name__
    time = MICROSECONDS.get(name, flops * 2.0e-9 + 0.5) * 0.5
    return pl.CostEstimate(flops=int(time * 1.15e9), bytes_accessed=0, transcendentals=0)


def call(
    kernel, results, scalar_count, operands, vmem, pieces=(), scratch=(), flops=0, moved=0
):
    return pl.pallas_call(
        kernel,
        out_shape=[jax.ShapeDtypeStruct(shape, kind) for shape, kind in results],
        in_specs=scalars(scalar_count)
        + whole_vmem(len(operands) - scalar_count)
        + [pl.BlockSpec(memory_space=pltpu.HBM)] * len(pieces),
        out_specs=whole_vmem(len(results)),
        scratch_shapes=list(scratch),
        compiler_params=pltpu.CompilerParams(vmem_limit_bytes=vmem * MEGA),
        cost_estimate=cost(kernel, flops),
    )(*operands, *pieces)


def block_call(kernel, results, scalar_arrays, operands, vmem, pieces, scratch, flops, moved):
    return pl.pallas_call(
        kernel,
        out_shape=[jax.ShapeDtypeStruct(shape, kind) for shape, kind, _, _ in results],
        grid_spec=pltpu.PrefetchScalarGridSpec(
            num_scalar_prefetch=len(scalar_arrays),
            grid=(4,),
            in_specs=[pl.BlockSpec(shape, index) for _, shape, index in operands]
            + [pl.BlockSpec(memory_space=pltpu.HBM)] * len(pieces),
            out_specs=[pl.BlockSpec(shape, index) for _, _, shape, index in results],
            scratch_shapes=list(scratch),
        ),
        compiler_params=pltpu.CompilerParams(vmem_limit_bytes=vmem * MEGA),
        cost_estimate=cost(kernel, flops),
    )(*scalar_arrays, *(array for array, _, _ in operands), *pieces)


def row_block(step, *scalar_refs):
    return (step, 0)


def half_block(step, *scalar_refs):
    return (step // 2, 0)


def first_block(step, *scalar_refs):
    return (0, 0)


def ordered_block(step, order_ref, *scalar_refs):
    return (order_ref[step], 0)


def split_product(left, right_shape, offsets, pieces, transposed, order):
    rows = left.shape[0] // 4
    width = right_shape[0] if transposed else right_shape[1]
    return block_call(
        functools.partial(split_kernel, transposed),
        [
            ((2 * rows, width), F32, (rows, width), half_block),
            ((2 * rows, width), BF, (rows, width), half_block),
        ],
        (order, offsets),
        [(left, (rows, left.shape[1]), ordered_block)],
        20,
        pieces,
        [pltpu.VMEM(right_shape, BF), pltpu.SemaphoreType.DMA((1, len(pieces)))],
        2 * left.shape[0] * left.shape[1] * width,
        2 * (left.size + right_shape[0] * right_shape[1]) + 6 * left.shape[0] * width,
    )


def swap(values, bit):
    count = lax.axis_size("seq")
    return lax.ppermute(values, "seq", [(i, i ^ bit) for i in range(count)])


def seq_pieces(values):
    far = swap(values, 2)
    near = swap(values, 1)
    return (values, near, far, swap(far, 1))


def after(values, *others):
    return lax.optimization_barrier((values, others))[0]


def ring_length():
    count = lax.axis_size("dp")
    return count if count % 2 == 0 and 4 <= count <= 8 else 0


def ring_order(count):
    return list(range(0, count, 2)) + list(range(count - 1, 0, -2))


def ring_sources(offsets):
    count = lax.axis_size("dp")
    place = lax.axis_index("dp")
    spot = jnp.where(place % 2 == 0, place // 2, count - 1 - place // 2)
    spot = (spot + jnp.asarray(offsets, jnp.int32) + count) % count
    return jnp.where(spot < count // 2, 2 * spot, 2 * (count - 1 - spot) + 1)


def ring_source(offset):
    count = lax.axis_size("dp")
    place = lax.axis_index("dp")
    spot = jnp.where(place % 2 == 0, place // 2, count - 1 - place // 2)
    spot = (spot + offset + count) % count
    return jnp.where(spot < count // 2, 2 * spot, 2 * (count - 1 - spot) + 1)


def ring_move(values, step):
    count = lax.axis_size("dp")
    order = ring_order(count)
    return lax.ppermute(
        values, "dp", [(order[i], order[(i + step) % count]) for i in range(count)]
    )


def half_of(rows):
    return rows // 32 * 16 or rows // 2


class GatherRing:
    def __init__(self, shard, long=1, leads=False):
        count = ring_length()
        self.rows = shard.shape[0]
        self.steps = count // 2
        self.pieces = [shard]
        self.spots = [0]
        self.flying = {}
        self.sent = ()
        if not count:
            self.pieces = [lax.all_gather(shard, "dp", axis=0, tiled=True)]
            return
        self.long = long
        self.leads = leads
        self.taken = 0
        self.flying = {1: shard, -1: shard}

    def step(self, *others):
        if not self.steps:
            return others
        self.flying, others = lax.optimization_barrier((self.flying, others))
        self.taken += 1
        ways = [self.long]
        if (self.taken > 1) if self.leads else (self.taken < self.steps):
            ways.append(-self.long)
        self.sent = tuple(self.flying[way] for way in ways)
        for way in ways:
            self.flying[way] = ring_move(self.flying[way], way)
            self.pieces.append(self.flying[way])
            lag = self.leads and way != self.long
            self.spots.append(-way * (self.taken - int(lag)))
        return others

    def arrived(self):
        return self.flying

    @property
    def offsets(self):
        if not self.steps:
            return jnp.zeros((1,), jnp.int32)
        return ring_sources(self.spots) * self.rows


class ScatterRing:
    def __init__(self, terms, halved=False):
        self.count = ring_length()
        self.halved = halved
        self.terms = terms
        self.flying = {}
        if not self.count:
            size = lax.axis_size("dp")
            parts = [term.reshape(size, -1, term.shape[1]) for term in terms]
            whole = self.joined(parts)
            self.sums = lax.psum_scatter(
                whole.reshape(-1, whole.shape[-1]).astype(BF), "dp", scatter_dimension=0, tiled=True
            ).astype(F32)
            self.steps = 0
            self.sent = ()
            return
        self.steps = self.count // 2
        self.taken = 0
        self.sent = ()

    def joined(self, parts):
        return parts[0] if len(parts) == 1 else jnp.concatenate(parts, axis=-2)

    def term(self, offset):
        parts = []
        for term in self.terms:
            rows = term.shape[0] // self.count
            parts.append(lax.dynamic_slice_in_dim(term, ring_source(offset) * rows, rows, 0))
        return self.joined(parts).astype(F32)

    def step(self, *others):
        if not self.steps:
            return others
        self.taken += 1
        left = self.steps + 1 - self.taken
        if self.taken == 1:
            self.terms, others = lax.optimization_barrier((self.terms, others))
            far = self.term(self.steps)
            half = half_of(far.shape[0])
            values = {1: far[:half], -1: far[half:]} if self.halved else {1: far}
        else:
            self.flying, others = lax.optimization_barrier((self.flying, others))
            values = {way: self.term(way * left) for way in (1, -1)}
            if self.taken == 2 and self.halved:
                up, down = (self.flying[1].astype(F32), self.flying[-1].astype(F32))
                half = up.shape[0]
                values = {
                    1: jnp.concatenate([values[1][:half] + up, values[1][half:]]),
                    -1: jnp.concatenate([values[-1][:half], values[-1][half:] + down]),
                }
            else:
                for way, arrived in self.flying.items():
                    values[way] = values[way] + arrived.astype(F32)
        sent = {way: value.astype(BF) for way, value in values.items()}
        self.sent = tuple(sent.values())
        self.flying = {way: ring_move(value, way) for way, value in sent.items()}
        return others

    def arrived(self):
        return self.flying

    def take(self, arrived):
        self.flying = arrived

    def result(self):
        if not self.steps:
            return self.sums
        return self.term(0) + self.flying[1].astype(F32) + self.flying[-1].astype(F32)


def local(
    tokens,
    segments,
    valid_mask,
    attention_gain,
    query_weight,
    key_weight,
    value_weight,
    query_gain,
    key_gain,
    output_weight,
    feedforward_gain,
    gate_weight,
    up_weight,
    down_weight,
    cotangent,
):
    seq_count = lax.axis_size("seq")
    dp_count = lax.axis_size("dp")
    place = lax.axis_index("seq")
    local_rows = tokens.shape[1]
    row_length = segments.shape[1]
    head_dim = query_gain.shape[0]
    width = tokens.shape[2]
    hidden_width = gate_weight.shape[1]
    query_width = query_weight.shape[1]
    key_width = key_weight.shape[1]
    query_here = query_width // seq_count
    key_here = key_width // seq_count
    hidden_here = hidden_width // seq_count
    weight_rows = query_weight.shape[0]
    own_rows = weight_rows // seq_count
    segment_row = segments[0]
    valid_row = valid_mask[0]

    def low(weight):
        return weight.astype(BF).astype(F32)

    place_array = place.astype(jnp.int32).reshape(1)
    gain_one = attention_gain[:, None]
    gain_two = feedforward_gain[:, None]
    qkv_width = query_here + 2 * key_here
    piece = hidden_width // (dp_count * seq_count)
    kernels_fit = weight_rows % 32 == 0 and own_rows % 8 == 0 and dp_count <= 8

    pack_width = qkv_width + width // seq_count
    (attention_pack,) = call(
        attention_pack_kernel,
        [((weight_rows, pack_width), BF)],
        1,
        (place_array, attention_gain[None, :] if weight_rows % PAIR == 0 else gain_one),
        58,
        pieces=(query_weight, key_weight, value_weight, output_weight),
        scratch=[pltpu.VMEM((weight_rows, pack_width), F32), pltpu.SemaphoreType.DMA((4,))],
        moved=8 * weight_rows * width,
    )
    if kernels_fit:
        (gate_up_pack,) = call(
            functools.partial(hidden_pack_kernel, dp_count),
            [((weight_rows, 2 * hidden_here), BF)],
            1,
            (place_array, after(gain_two, attention_pack)),
            58,
            pieces=(gate_weight, up_weight),
            scratch=[
                pltpu.VMEM((2, weight_rows, hidden_width), F32),
                pltpu.SemaphoreType.DMA((2, weight_rows // 32)),
            ],
            moved=8 * weight_rows * hidden_width,
        )
    else:

        def hidden_columns(weight):
            split = weight.reshape(weight_rows, dp_count, seq_count, piece)
            mine = lax.dynamic_index_in_dim(split, place, 2, keepdims=False)
            return (low(mine.reshape(weight_rows, hidden_here)) * low(gain_two)).astype(BF)

        gate_up_pack = jnp.concatenate(
            [hidden_columns(gate_weight), hidden_columns(up_weight)], axis=1
        )
    down_pack = lax.dynamic_slice_in_dim(down_weight, place * piece, piece, 0).astype(BF)
    down_pack = after(down_pack, attention_pack)

    order = place ^ jnp.arange(4, dtype=jnp.int32)
    plain = jnp.arange(4, dtype=jnp.int32)

    token_far = swap(tokens[0], 2)
    token_near = swap(tokens[0], 1)
    attention_ring = GatherRing(attention_pack)
    attention_ring.step()
    positions = doc_positions(segment_row)
    starts = jnp.arange(row_length, dtype=jnp.int32) - positions
    cos_wide, sin_wide = rope_tables(positions, head_dim)
    repeats = PAIR // head_dim
    head_gains = jnp.tile(jnp.stack([query_gain, key_gain]), (1, repeats))
    row_starts = starts[:, None]
    usable = valid_row[None, :]
    starts, row_starts, head_gains = attention_ring.step(starts, row_starts, head_gains)
    block_lows = starts[::BLOCK]
    token_far, cos_wide, sin_wide = attention_ring.step(token_far, cos_wide, sin_wide)
    token_pieces = (tokens[0], token_near, token_far, swap(token_far, 1))
    grad_far = swap(after(cotangent[0], token_far), 2)
    grad_near = swap(after(cotangent[0], token_far), 1)
    (gate_up_pack,) = attention_ring.step(gate_up_pack)

    gate_up_ring = GatherRing(after(gate_up_pack, attention_ring.arrived()))
    (grad_far,) = gate_up_ring.step(grad_far)
    grad_row_pieces = (cotangent[0], grad_near, grad_far, swap(grad_far, 1))
    (output_columns,) = pl.pallas_call(
        functools.partial(columns_kernel, qkv_width),
        out_shape=[jax.ShapeDtypeStruct((query_width, width // seq_count), BF)],
        in_specs=scalars(1) + [pl.BlockSpec(memory_space=pltpu.HBM)] * len(attention_ring.pieces),
        out_specs=whole_vmem(1),
        scratch_shapes=[pltpu.SemaphoreType.DMA((1, len(attention_ring.pieces)))],
        compiler_params=pltpu.CompilerParams(vmem_limit_bytes=58 * MEGA),
        cost_estimate=cost(columns_kernel, 0),
    )(attention_ring.offsets, *attention_ring.pieces)
    output_far = swap(output_columns, 2)
    output_near = swap(output_columns, 1)
    projected = call(
        functools.partial(project_kernel, head_dim),
        [
            ((row_length, width), BF),
            ((row_length, query_here + key_here), F32),
            ((row_length, query_here), BF),
            ((row_length, 2 * key_here), BF),
            ((row_length, 2 * key_here), BF),
            ((width, qkv_width), BF),
        ],
        2,
        (place_array, attention_ring.offsets, *token_pieces, cos_wide, sin_wide, head_gains),
        58,
        pieces=attention_ring.pieces,
        scratch=[pltpu.SemaphoreType.DMA((1, len(attention_ring.pieces)))],
        flops=2 * row_length * width * qkv_width,
        moved=12 * row_length * width,
    )
    projected, output_far = gate_up_ring.step(projected, output_far)
    output_pieces = (output_columns, output_near, output_far, swap(output_far, 1))
    unit_one, raw, queries, keys_two, values_two, qkv_weight = projected
    (mixed_here,) = call(
        functools.partial(attend_kernel, head_dim),
        [((row_length, query_here), BF)],
        1,
        (block_lows, queries, keys_two, values_two, row_starts, usable),
        58,
        flops=row_length * width * qkv_width,
        moved=4 * row_length * width,
    )
    mixed_far = swap(mixed_here, 2)
    mixed_near = swap(mixed_here, 1)
    gate_up_ring.step(mixed_here)
    (mixed_far,) = gate_up_ring.step(mixed_far)
    down_ring = GatherRing(after(down_pack, mixed_far), -1, True)
    down_ring.step()
    mixed_pieces = (mixed_here, mixed_near, mixed_far, swap(mixed_far, 1))
    unit_two, after_here = call(
        middle_kernel,
        [((row_length, width), BF), ((local_rows, width), F32)],
        1,
        (place_array, *token_pieces, *mixed_pieces, *output_pieces),
        18,
        scratch=[pltpu.VMEM((local_rows, width), F32)],
        flops=2 * row_length * width * width,
        moved=10 * row_length * width,
    )
    (unit_two,) = down_ring.step(unit_two)

    rows_each = row_length // 4
    hidden, gate_factor, up_factor = block_call(
        hidden_kernel,
        [((row_length, hidden_here), BF, (rows_each, hidden_here), row_block)] * 3,
        (gate_up_ring.offsets,),
        [(unit_two, (rows_each, width), row_block)],
        28,
        gate_up_ring.pieces,
        [
            pltpu.VMEM((width, 2 * hidden_here), BF),
            pltpu.SemaphoreType.DMA((1, len(gate_up_ring.pieces))),
        ],
        4 * row_length * width * hidden_here,
        8 * row_length * hidden_here + 4 * width * hidden_here,
    )
    hidden, gate_factor, up_factor = down_ring.step(hidden, gate_factor, up_factor)
    grad_rows = jnp.concatenate(grad_row_pieces)
    down_scatter = ScatterRing([mm_tn(hidden, grad_rows)], True)
    (down_scatter.terms,) = down_ring.step(down_scatter.terms)
    down_scatter.step()
    gate_up_grad, down_all = block_call(
        hidden_grad_kernel,
        [
            ((row_length, 2 * hidden_here), BF, (rows_each, 2 * hidden_here), row_block),
            ((hidden_here, width), BF, (hidden_here, width), first_block),
        ],
        (down_ring.offsets,),
        [
            (grad_rows, (rows_each, width), row_block),
            (gate_factor, (rows_each, hidden_here), row_block),
            (up_factor, (rows_each, hidden_here), row_block),
        ],
        24,
        down_ring.pieces,
        [pltpu.SemaphoreType.DMA((1, len(down_ring.pieces)))],
        2 * row_length * width * hidden_here,
        8 * row_length * hidden_here + 4 * width * hidden_here,
    )

    (gate_up_grad,) = down_scatter.step(gate_up_grad)
    keep, send = split_product(
        gate_up_grad, (width, 2 * hidden_here), gate_up_ring.offsets, gate_up_ring.pieces, True, plain
    )
    keep, send = down_scatter.step(keep, send)

    def halves(keep, near):
        return (
            keep[:local_rows] + near[:local_rows].astype(F32),
            (keep[local_rows:] + near[local_rows:].astype(F32)).astype(BF),
        )

    half_sum, half_send = halves(keep, swap(send, 1))
    half_send, unit_two = lax.optimization_barrier((half_send, unit_two))
    arrived = swap(half_send, 2)
    gate_up_scatter = ScatterRing([mm_tn(unit_two, gate_up_grad).astype(BF)], True)
    gate_up_scatter.step()
    unit_here, factor_here = rms_stats(after_here)
    grad_after = cotangent[0].astype(F32) + rms_back(
        half_sum + arrived.astype(F32), unit_here, factor_here
    )
    branch = grad_after.astype(BF)
    branch_far = swap(branch, 2)
    branch_near = swap(branch, 1)
    gate_up_scatter.step(branch)
    keep, send = split_product(
        after(hidden, branch, gate_up_scatter.sent),
        (hidden_here, width),
        jnp.zeros((1,), jnp.int32),
        [down_all],
        False,
        plain,
    )
    keep, send, branch_far = gate_up_scatter.step(keep, send, branch_far)
    branch_pieces = (branch, branch_near, branch_far, swap(branch_far, 1))
    half_sum, half_send = halves(keep, swap(send, 1))
    chunk_rows = query_width // (dp_count * seq_count)
    grad_mixed, output_terms = call(
        functools.partial(output_grad_kernel, chunk_rows),
        [
            ((row_length, query_here), BF),
            ((query_here * width // qkv_width, qkv_width), F32),
        ],
        1,
        (place_array, *branch_pieces, mixed_here, *output_pieces),
        14,
        scratch=[pltpu.VMEM((query_here, width), F32)],
        flops=4 * row_length * width * query_here,
        moved=8 * row_length * width,
    )

    down_scatter.step(grad_mixed)
    grad_mixed, half_send = lax.optimization_barrier((grad_mixed, half_send))
    arrived = swap(half_send, 2)
    qkv_grad, gain_terms = call(
        functools.partial(back_kernel, head_dim),
        [((row_length, qkv_width), BF), ((8, PAIR), F32)],
        1,
        (block_lows, grad_mixed, queries, keys_two, values_two, raw)
        + (cos_wide, sin_wide, head_gains, row_starts, usable),
        24,
        scratch=[pltpu.VMEM((row_length, 2 * key_here), F32)] * 2,
        flops=4 * row_length * width * qkv_width,
        moved=12 * row_length * width,
    )
    qkv_grad, gain_terms, arrived = gate_up_scatter.step(qkv_grad, gain_terms, arrived)
    layer_out = (after_here + half_sum + arrived.astype(F32)).astype(BF)
    gain_rows = jnp.concatenate([gain_terms[0:1], gain_terms[1:2]], axis=1)
    gain_rows = jnp.pad(gain_rows, ((0, 15), (0, qkv_width - 2 * PAIR)))
    packed = jnp.concatenate(
        [
            mm_tn(unit_one, qkv_grad).reshape(dp_count, weight_rows, qkv_width),
            output_terms.reshape(dp_count, -1, qkv_width),
            jnp.broadcast_to(gain_rows, (dp_count, *gain_rows.shape)),
        ],
        axis=1,
    )
    attention_scatter = ScatterRing([packed.reshape(-1, qkv_width)])
    attention_scatter.step()
    keep, send = split_product(
        after(qkv_grad, attention_scatter.sent),
        (width, qkv_width),
        jnp.zeros((1,), jnp.int32),
        [qkv_weight],
        True,
        order,
    )
    keep, send = attention_scatter.step(keep, send)
    gate_up_scatter.take(after(gate_up_scatter.arrived(), attention_scatter.arrived()))
    gate_up_sums = gate_up_scatter.result().astype(BF)
    hidden_own = lax.all_to_all(
        gate_up_sums.reshape(seq_count, own_rows, -1), "seq", split_axis=0, concat_axis=0, tiled=True
    )
    half_sum, half_send = halves(keep, swap(send, 1))
    arrived = swap(half_send, 2)
    attention_scatter.step(half_send)
    for _ in range(attention_scatter.steps - 3):
        (arrived,) = attention_scatter.step(arrived)
        hidden_own = after(hidden_own, attention_scatter.sent)
    unit_tokens, factor_tokens = rms_stats(tokens[0].astype(F32))
    token_grad = (
        grad_after + rms_back(half_sum + arrived.astype(F32), unit_tokens, factor_tokens)
    ).astype(BF)

    down_sums = down_scatter.result()
    attention_sums = attention_scatter.result().astype(BF)
    qkv_sums = attention_sums[:weight_rows]
    output_sums = jnp.concatenate(
        [
            attention_sums[weight_rows + part * chunk_rows : weight_rows + (part + 1) * chunk_rows]
            for part in range(width // qkv_width)
        ],
        axis=1,
    )

    def own(weight):
        return lax.dynamic_slice_in_dim(weight, place * own_rows, own_rows, 0)

    gain_row = attention_sums[-16:]
    qkv_pieces = []
    for bits in range(4):
        part = lax.dynamic_slice_in_dim(qkv_sums, (place ^ bits) * own_rows, own_rows, 0)
        part = after(jnp.concatenate([part, gain_row]), arrived)
        qkv_pieces.append(swap(part, bits) if bits else part)
    gain_sums = sum(piece[own_rows : own_rows + 1].astype(F32) for piece in qkv_pieces)
    gain_sums = jnp.sum(gain_sums[0, : 2 * PAIR].reshape(2, repeats, head_dim), axis=1)
    if kernels_fit:
        gate_grad, up_grad, feed_gain_grad = placed_call(
            functools.partial(hidden_owner_kernel, dp_count),
            [((own_rows, hidden_width), F32)] * 2 + [((1, own_rows), F32)],
            place_array,
            (hidden_own, gate_weight, up_weight, gain_two),
            [
                (hidden_own.shape, lambda i, place: (0, 0, 0)),
                ((own_rows, hidden_width), own_rows_block),
                ((own_rows, hidden_width), own_rows_block),
                ((own_rows, 1), own_rows_block),
            ],
            58,
            moved=20 * own_rows * hidden_width,
        )
        query_grad, key_grad, value_grad, attention_gain_grad = placed_call(
            attention_owner_kernel,
            [((own_rows, query_width), F32)]
            + [((own_rows, key_width), F32)] * 2
            + [((1, own_rows), F32)],
            place_array,
            (*qkv_pieces, query_weight, key_weight, value_weight, gain_one),
            [((own_rows + 16, qkv_width), everything)] * 4
            + [
                ((own_rows, query_width), own_rows_block),
                ((own_rows, key_width), own_rows_block),
                ((own_rows, key_width), own_rows_block),
                ((own_rows, 1), own_rows_block),
            ],
            58,
            moved=20 * own_rows * query_width,
        )
    else:
        spread = jnp.stack(qkv_pieces)[order, :own_rows].astype(F32)

        def joined(first, size):
            return jnp.swapaxes(spread[:, :, first : first + size], 0, 1).reshape(own_rows, -1)

        query_own = joined(0, query_here)
        key_own = joined(query_here, key_here)
        value_own = joined(query_here + key_here, key_here)
        attention_gain_grad = (
            jnp.sum(own(low(query_weight)) * query_own, axis=1)
            + jnp.sum(own(low(key_weight)) * key_own, axis=1)
            + jnp.sum(own(low(value_weight)) * value_own, axis=1)
        )
        gain_own = own(low(gain_one))
        query_grad, key_grad, value_grad = (
            query_own * gain_own,
            key_own * gain_own,
            value_own * gain_own,
        )
        hidden_own = hidden_own.reshape(seq_count, own_rows, 2, dp_count, piece)
        hidden_own = jnp.transpose(hidden_own, (2, 1, 3, 0, 4))
        hidden_own = hidden_own.reshape(2, own_rows, hidden_width).astype(F32)
        feed_gain_grad = jnp.sum(own(low(gate_weight)) * hidden_own[0], axis=1) + jnp.sum(
            own(low(up_weight)) * hidden_own[1], axis=1
        )
        gain_own = own(low(gain_two))
        gate_grad, up_grad = (hidden_own[0] * gain_own, hidden_own[1] * gain_own)

    moves = [
        (dp * seq_count + seq, seq * dp_count + dp)
        for dp in range(dp_count)
        for seq in range(seq_count)
    ]
    output_own = lax.ppermute(output_sums, ("dp", "seq"), moves).astype(F32)

    return (
        layer_out.reshape(1, local_rows, -1),
        token_grad.reshape(1, local_rows, -1),
        attention_gain_grad.reshape(own_rows),
        query_grad,
        key_grad,
        value_grad,
        gain_sums[0],
        gain_sums[1],
        output_own,
        feed_gain_grad.reshape(own_rows),
        gate_grad,
        up_grad,
        down_sums,
    )


def solution(mesh):
    in_specs = (
        P("dp", "seq", None),
        P("dp", None),
        P("dp", None),
        P("dp"),
        P("dp", None),
        P("dp", None),
        P("dp", None),
        P(),
        P(),
        P("dp", None),
        P("dp"),
        P("dp", None),
        P("dp", None),
        P("dp", None),
        P("dp", "seq", None),
    )
    out_specs = (
        P("dp", "seq", None),
        P("dp", "seq", None),
        P(("dp", "seq")),
        P(("dp", "seq"), None),
        P(("dp", "seq"), None),
        P(("dp", "seq"), None),
        P(),
        P(),
        P(("dp", "seq"), None),
        P(("dp", "seq")),
        P(("dp", "seq"), None),
        P(("dp", "seq"), None),
        P(("dp", "seq"), None),
    )
    return jax.shard_map(local, mesh=mesh, in_specs=in_specs, out_specs=out_specs, check_vma=False)
```
